32 devices in a mesh: gx: 2 (over x), gy: 4 (over z), gz: 4 (over y, core).
Axes of the slice: x: 2, y: 2, z: 4, core: 2. Of those that a mesh axis runs over, the one named last changes fastest.
Arguments:
- source_field: float32 [3, 16, 32, 512], P(None, 'gx', 'gy', 'gz'), may hold values from -6 to 6
- cell_contrast: bfloat16 [4096, 1536], P(('gx', 'gy', 'gz')), may hold values from 0.19921875 to 2
- point_field: bfloat16 [3, 4096], P(None, ('gx', 'gy', 'gz')), may hold values from -3 to 3
- point_class: int32 [4096, 1], P(('gx', 'gy', 'gz')), may hold values from 0 to 1; in each aligned block of 128 rows (0 to 127, 128 to 255, ...) at most 128 rows name the same one
- cell_kind: int32 [4096], P(('gx', 'gy', 'gz')), may hold values from 0 to 3
- inverse_blocks: float32 [2, 4, 3, 3, 512], P('gx'), may hold values from -0.3 to 0.3
Outputs:
- newton_step: float32 [3, 16, 32, 512], P(None, 'gx', 'gy', 'gz')
- krylov_residual: float32 [3, 16, 32, 512], P(None, 'gx', 'gy', 'gz')
The draws below stay inside these ranges and needn't reach their ends.
Inputs may be any that keep to these rules, and one draw needn't show every extreme that they name: `point_class`: among the 128 points of one device's block no class is named more than 128 times, a bound that some block reaches there.
All inputs are finite; a program needn't handle non-finite values.
Results may differ from the reference program's by a relative error of at most 0.0076.
Values may be sent and summed in bfloat16 or wider, within the bound.
No kernel may reach another device: no remote copies, remote signals or barrier semaphores. Data moves between devices by JAX's collectives and lax.ppermute only.
A program may use at most 64 MiB of HBM per device.

```python
import math
import jax
import jax.numpy as jnp
import numpy as np
from jax import lax

CELL = 8
VOX = 512
TYPES = 4
CX = 8
CY = 8
ZP = 8
ITERS = 3
ZB = 16
Q_DEV = 128
Q_TOTAL = 4096
CLASSES = 2
CAP = 128
NX = 16
NY = 32
NZ = 512
N_GX = 2
N_GY = 4
N_GZ = 4


def plant(result, own_key, low, largest):
    extent = result.shape
    index_at = [jax.random.randint(jax.random.fold_in(own_key, axis), (), 0, extent[axis]) for axis in range(len(extent))]
    result = result.at[tuple(index_at)].set(low)
    longest = extent.index(max(extent))
    index_at[longest] = (index_at[longest] + 1) % extent[longest]
    return result.at[tuple(index_at)].set(largest)


def block_scale(stream_key, shape, shards, low, top_value):
    loudness = 1.0
    for axis_at, blocks in shards:
        draws = jax.random.uniform(jax.random.fold_in(jax.random.fold_in(stream_key, 6), axis_at), (blocks,), jnp.float32, low / len(shards), top_value / len(shards))
        loudness = loudness * jnp.repeat(jnp.exp(draws), shape[axis_at] // blocks).reshape((-1,) + (1,) * (len(shape) - 1 - axis_at))
    return loudness


def assign_block(key, own, number, rows, number_of, top, bound, skew):
    sequence = jax.random.permutation(key, number_of)
    crowded, common = portions_of(number_of, rows * top, bound, skew, True), portions_of(number_of, rows * top, bound, skew, False)
    places = jnp.arange(number_of)

    def named(sizes, turn):
        used = int((sizes > 0).sum())
        fixed = max(1, used // 4)
        moved = fixed + (places - fixed + turn * (used - fixed)) % max(1, number_of - fixed)
        return jnp.zeros((number_of,), jnp.int32).at[sequence[jnp.where(places < fixed, places, moved)]].set(jnp.asarray(sizes, jnp.int32))

    sizes = jnp.where(number % 4 == 0, named(crowded, number // 4), named(common, number - number // 4 - 1))
    mixed = jax.random.permutation(jax.random.fold_in(own, 3), number_of)
    giver, receiver = mixed[0:number_of // 2 * 2:2], mixed[1:number_of // 2 * 2:2]
    room = jnp.minimum(sizes[giver] - 1, bound - sizes[receiver]) // 2
    room = jnp.where((giver == sequence[0]) | (receiver == sequence[0]) | (sizes[receiver] == 0), 0, jnp.maximum(room, 0))
    moved = jax.random.randint(jax.random.fold_in(own, 4), (number_of // 2,), 0, 1 << 20) % (room + 1)
    sizes = sizes.at[giver].add(-moved).at[receiver].add(moved)
    labels = jnp.searchsorted(jnp.cumsum(sizes), jnp.arange(rows * top), side="right").astype(jnp.int32)
    grid = labels.reshape(top, rows).T
    grid = grid[jax.random.permutation(jax.random.fold_in(own, 1), rows)]
    turn = jax.random.randint(jax.random.fold_in(own, 2), (rows, 1), 0, top)
    return jnp.take_along_axis(grid, (jnp.arange(top)[None, :] + turn) % top, axis=1)


def portions_of(amount, total, limit, lean, full):
    loads = [(1 << 20) // math.isqrt(rank ** lean) + 1 for rank in range(1, amount + 1)]
    largest = limit if full else min(limit, max(-(-total // amount), total * loads[0] // sum(loads)))
    least = 1 if total - largest >= amount - 1 else 0
    holding, spare = [largest] + [least] * (amount - 1), total - largest - least * (amount - 1)
    while spare > 0:
        movable = [i for i in range(1, amount) if holding[i] < largest] or [i for i in range(1, amount) if holding[i] < limit]
        mass, remaining = sum([loads[i] for i in movable]), spare
        for i in movable:
            extra = min(limit - holding[i], max(1, remaining * loads[i] // mass), spare)
            holding[i] = holding[i] + extra
            spare = spare - extra
    return np.array(holding)


def gaussian(key, dims, width, reach, pieces=(), kind=jnp.bfloat16):
    gain = block_scale(key, dims, pieces, -0.22, 0.18) if pieces else 1.0
    entries = jax.random.normal(key, dims, jnp.float32) * width * gain
    return jnp.minimum(jnp.maximum(entries, -reach), reach).astype(kind)


def setup_inputs(seed: int = 0) -> dict:
    key_of = jax.random.split(jax.random.key(seed), 7)
    source_field = gaussian(key_of[0], (3, NX, NY, NZ), 1.0, 6.0, ((1, 2), (2, 4), (3, 4)), jnp.float32)
    cell_contrast = jnp.clip(jnp.exp(math.log(2.0) - 2.306499 * jax.random.uniform(key_of[1], (Q_TOTAL, 3 * VOX), jnp.float32) ** block_scale(key_of[1], (Q_TOTAL, 3 * VOX), ((0, 32),), -0.2, 0.2)), 0.19921875, 2.0).astype(jnp.bfloat16)
    point_field = gaussian(key_of[2], (3, Q_TOTAL), 1.0, 3.0, ((1, 32),))
    point_class_keys = jax.random.split(jax.random.fold_in(key_of[3], 1), Q_TOTAL // Q_DEV)
    point_class_turns = jax.random.permutation(jax.random.fold_in(key_of[3], 3), Q_TOTAL // Q_DEV)
    point_class = jax.vmap(lambda own, number: assign_block(jax.random.fold_in(key_of[3], 2), own, number, Q_DEV, CLASSES, 1, CAP, 2))(point_class_keys, point_class_turns).reshape((Q_TOTAL, 1))
    cell_kind = plant(jax.random.randint(key_of[4], (Q_TOTAL,), 0, TYPES), jax.random.fold_in(key_of[4], 1), 0, TYPES - 1).astype(jnp.int32)
    inverse_blocks = jnp.clip(jax.random.uniform(key_of[5], (CLASSES, TYPES, 3, 3, VOX), jnp.float32, -0.3, 0.3) * block_scale(key_of[5], (CLASSES, TYPES, 3, 3, VOX), ((0, 2),), -0.4, 0.0), -0.3, 0.3)
    return {"source_field": source_field, "cell_contrast": cell_contrast, "point_field": point_field, "point_class": point_class, "cell_kind": cell_kind, "inverse_blocks": inverse_blocks}


kerr_scale = 0.1

def hartley_table():
    voxel_index = jnp.arange(VOX, dtype=jnp.int32)
    along_one = voxel_index // (CELL * CELL)
    along_two = voxel_index // CELL % CELL
    along_three = voxel_index % CELL
    phase_index = (along_one[:, None] * along_one[None, :] + along_two[:, None] * along_two[None, :] + along_three[:, None] * along_three[None, :]) % CELL
    phase_angle = 2.0 * math.pi / CELL * phase_index.astype(jnp.float32)
    return ((jnp.cos(phase_angle) + jnp.sin(phase_angle)) / math.sqrt(VOX)).astype(jnp.bfloat16)

def cell_solve(contrast, point_values, blocks, hartley):
    row_count = contrast.shape[0]
    weights = contrast.reshape(row_count, 3, VOX).astype(jnp.float32)
    base_field = point_values.astype(jnp.float32)[:, :, None]

    def correction(polarization):
        spectrum = jnp.dot(polarization.reshape(row_count * 3, VOX), hartley, preferred_element_type=jnp.float32).reshape(row_count, 3, VOX)
        mixed_spectrum = lax.optimization_barrier(jnp.sum(blocks * spectrum[:, None, :, :], axis=2)).astype(jnp.bfloat16)
        return jnp.dot(mixed_spectrum.reshape(row_count * 3, VOX), hartley, preferred_element_type=jnp.float32).reshape(row_count, 3, VOX)
    local_field = base_field - correction((weights * base_field).astype(jnp.bfloat16))
    kerr_polar = (weights * local_field * (1.0 + kerr_scale * local_field * local_field)).astype(jnp.bfloat16)
    final_field = base_field - correction(kerr_polar)
    flux_mean = lax.optimization_barrier(jnp.mean((1.0 + weights) * final_field, axis=2))
    stiffness = 0.5 + lax.optimization_barrier(jnp.mean(weights * final_field * final_field, axis=(1, 2)))
    return jnp.concatenate([flux_mean, stiffness[:, None]], axis=1)

def to_grid(point_rows):
    comps = point_rows.shape[0]
    shaped = point_rows.reshape(comps, N_GX, N_GY, N_GZ, CY, ZB).transpose(0, 1, 2, 4, 3, 5)
    shaped = shaped.reshape(comps, N_GX, 1, N_GY, CY, N_GZ, ZB, 1)
    return jnp.broadcast_to(shaped, (comps, N_GX, CX, N_GY, CY, N_GZ, ZB, ZP)).reshape(comps, NX, NY, NZ)

def operate(field, diagonal):
    padded = jnp.pad(field, ((0, 0), (1, 1), (1, 1), (1, 1)))
    beside = padded[:, 2:, 1:-1, 1:-1] + padded[:, :-2, 1:-1, 1:-1]
    beside = beside + padded[:, 1:-1, 2:, 1:-1] + padded[:, 1:-1, :-2, 1:-1]
    beside = beside + padded[:, 1:-1, 1:-1, 2:] + padded[:, 1:-1, 1:-1, :-2]
    return (6.0 + diagonal)[None] * field - beside

def reference(source_field, cell_contrast, point_field, point_class, cell_kind, inverse_blocks):
    hartley = hartley_table()
    point_total = cell_contrast.shape[0]
    block_size = math.gcd(point_total, 256)
    block_count = point_total // block_size

    def one_block(packed):
        contrast, point_values, classes, kinds = packed
        blocks = inverse_blocks[classes, kinds]
        return cell_solve(contrast, point_values, blocks, hartley)
    results = lax.map(one_block, (cell_contrast.reshape(block_count, block_size, 3 * VOX), point_field.T.reshape(block_count, block_size, 3), point_class[:, 0].reshape(block_count, block_size), cell_kind.reshape(block_count, block_size)))
    summary = results.reshape(point_total, 4)
    stiffness_grid = to_grid(summary[:, 3][None, :])[0]
    flux_grid = to_grid(summary[:, :3].T)
    right = source_field - flux_grid
    newton_step = jnp.zeros_like(right)
    residual, direction = (right, right)
    norm_now = jnp.sum(residual * residual)
    for iteration in range(ITERS):
        image = operate(direction, stiffness_grid)
        alpha = norm_now / jnp.sum(direction * image)
        newton_step = newton_step + alpha * direction
        residual = residual - alpha * image
        norm_next = jnp.sum(residual * residual)
        direction = residual + norm_next / norm_now * direction
        norm_now = norm_next
    return (newton_step, residual)
```

```python
import functools
import math

import jax
import jax.numpy as jnp
from jax import lax
from jax.experimental import pallas as pl
from jax.experimental.pallas import tpu as pltpu
from jax.sharding import PartitionSpec as P

CELL = 8
VOX = 512
TYPES = 4
ZP = 8
ITERS = 3
AXES = ("gx", "gy", "gz")
DENSE = 64
SHIFT = 8.0

kerr_scale = 0.1


def where_am_i():
    return tuple(lax.axis_index(a) for a in AXES)


def spectrum_kernel(contrast, point_field, hartley, spectrum, columns, polar):
    rows = contrast.shape[0]
    step = CELL * CELL
    inner = lax.broadcasted_iota(jnp.int32, (step, VOX), 0)
    voxel = lax.broadcasted_iota(jnp.int32, (step, VOX), 1)
    phase = (inner // CELL) * (voxel // CELL % CELL) + (inner % CELL) * (voxel % CELL)
    outer = voxel // step
    plain = 1.0 / math.sqrt(VOX)
    peak = math.sqrt(2.0) / math.sqrt(VOX)
    for block in range(VOX // step):
        turn = (phase + block * outer) & (CELL - 1)
        quarter = turn & 3
        size = jnp.where(quarter == 1, peak, jnp.where(quarter == 3, 0.0, plain))
        value = jnp.where(turn >= 4, -size, size)
        hartley[block * step : (block + 1) * step, :] = value.astype(jnp.bfloat16)
    fields = point_field[...].astype(jnp.float32)
    fields = jnp.concatenate([fields, jnp.zeros((5, rows), jnp.float32)], axis=0)
    columns[...] = fields.T
    for j in range(3):
        e = columns[:, j : j + 1]
        m = contrast[:, j * VOX : (j + 1) * VOX].astype(jnp.float32)
        polar[j * rows : (j + 1) * rows, :] = (m * e).astype(jnp.bfloat16)
    spectrum[...] = jnp.dot(polar[...], hartley[...], preferred_element_type=jnp.float32)


def solve_kernel(keep_class, contrast, columns, spectrum, hartley, point_class, cell_kind, library, other,
                 source, tiles, bundle, mixing, stacked, product):
    rows = contrast.shape[0]
    zb = rows // 8
    gx, _, gz = where_am_i()
    keys = point_class[...] if keep_class else jnp.where(point_class[...] == gx, 0, 1)
    keys = keys * TYPES + cell_kind[...]
    count = library.shape[0] * TYPES * (1 if keep_class else 2)
    pick = (lax.broadcasted_iota(jnp.int32, (count, rows), 0) == keys).astype(jnp.float32)
    pick = jnp.concatenate([pick, pick], axis=0)
    pick = pick.T.astype(jnp.bfloat16)
    for ij in range(9):
        i, j = ij // 3, ij % 3
        parts = [library[c, i, j] for c in range(library.shape[0])]
        if not keep_class:
            parts = parts + [other[c, i, j] for c in range(library.shape[0])]
        table = jnp.concatenate(parts, axis=0)
        high = table.astype(jnp.bfloat16).astype(jnp.float32)
        both = jnp.concatenate([high, table - high], axis=0).astype(jnp.bfloat16)
        mixing[ij] = jnp.dot(pick, both, preferred_element_type=jnp.float32)

    def mix(from_ref):
        for c in range(rows // 16):
            at = slice(c * 16, (c + 1) * 16)
            held = [from_ref[j * rows + c * 16 : j * rows + (c + 1) * 16, :] for j in range(3)]
            for i in range(3):
                total = mixing[3 * i, at, :] * held[0]
                total = total + mixing[3 * i + 1, at, :] * held[1]
                total = total + mixing[3 * i + 2, at, :] * held[2]
                stacked[i * rows + c * 16 : i * rows + (c + 1) * 16, :] = total.astype(jnp.bfloat16)

    mix(spectrum)
    product[...] = jnp.dot(stacked[...], hartley[...], preferred_element_type=jnp.float32)
    for c in range(rows // 16):
        for j in range(3):
            at = slice(j * rows + c * 16, j * rows + (c + 1) * 16)
            m = contrast[c * 16 : (c + 1) * 16, j * VOX : (j + 1) * VOX].astype(jnp.float32)
            local = columns[c * 16 : (c + 1) * 16, j : j + 1] - product[at, :]
            stacked[at, :] = (m * local * (1.0 + kerr_scale * local * local)).astype(jnp.bfloat16)
    product[...] = jnp.dot(stacked[...], hartley[...], preferred_element_type=jnp.float32)
    mix(product)
    product[...] = jnp.dot(stacked[...], hartley[...], preferred_element_type=jnp.float32)

    depth = lax.broadcasted_iota(jnp.int32, (zb, 128), 0)
    lane = lax.broadcasted_iota(jnp.int32, (zb, 128), 1)
    spread = lane // ZP == depth
    packed = lane % zb == depth
    group = lane // zb
    for c in range(rows // 16):
        means = []
        stiff = jnp.zeros((16, VOX), jnp.float32)
        for j in range(3):
            at = slice(j * rows + c * 16, j * rows + (c + 1) * 16)
            m = contrast[c * 16 : (c + 1) * 16, j * VOX : (j + 1) * VOX].astype(jnp.float32)
            final = columns[c * 16 : (c + 1) * 16, j : j + 1] - product[at, :]
            means.append(jnp.sum((1.0 + m) * final, axis=1, keepdims=True) * (1.0 / VOX))
            stiff = stiff + m * final * final
        means.append(0.5 + jnp.sum(stiff, axis=1, keepdims=True) * (1.0 / (3 * VOX)))
        compact = jnp.zeros((zb, 128), jnp.float32)
        for t in range(4):
            wide = jnp.broadcast_to(means[t], (zb, 128))
            tiles[t, c : c + 1, :] = jnp.sum(jnp.where(spread, wide, 0.0), axis=0, keepdims=True)
            compact = compact + jnp.where(packed & (group == t), wide, 0.0)
        product[c : c + 1, 0:128] = jnp.sum(compact, axis=0, keepdims=True)
    compact = product[0:8, 0:128]

    place = lax.broadcasted_iota(jnp.int32, (8, 128), 1)
    low = jnp.zeros((8, 128), jnp.float32)
    high = jnp.zeros((8, 128), jnp.float32)
    slabs = source.shape[1]
    for s in range(3 * slabs + 1):
        if s < 3 * slabs:
            value = source[s // slabs, s % slabs] - tiles[s // slabs]
        else:
            value = tiles[3]
        here = (place >= 3 * s) & (place < 3 * s + 3)
        low = jnp.where(here, pltpu.roll(value, (3 * s) % 128, 1) if s else value, low)
        high = jnp.where(here, pltpu.roll(value, (3 * s + 3) % 128, 1), high)
    for d in range(bundle.shape[1]):
        zero = jnp.zeros((8, 128), jnp.float32)
        tile = jnp.where(gz == d, compact, jnp.where(gz + 1 == d, high, jnp.where(gz - 1 == d, low, zero)))
        for x in range(bundle.shape[0]):
            bundle[x, d] = tile


def moment_kernel(dense, counts, tiles, got, source, xlow, xhigh, ylow, yhigh, v0, v1, v2, v3, moments, w0, w1, w2):
    slabs = source.shape[1]
    gx, gy, gz = where_am_i()
    nx, ny, nz = counts
    row = lax.broadcasted_iota(jnp.int32, (8, 128), 0)
    lane = lax.broadcasted_iota(jnp.int32, (8, 128), 1)
    has_xl, has_xh = gx > 0, gx < nx - 1
    has_yl, has_yh = gy > 0, gy < ny - 1
    has_zl, has_zh = gz > 0, gz < nz - 1
    one = lambda flag: jnp.where(flag, 1.0, 0.0)
    mask_y = jnp.where(row < 4, one(has_yh), one(has_yl))
    mask_z = jnp.where(lane < 64, one(has_zh), one(has_zl))
    masks = (None, mask_y, mask_z, mask_y * mask_z)
    yl, yh = jnp.maximum(gy - 1, 0), jnp.minimum(gy + 1, ny - 1)
    zl, zh = jnp.maximum(gz - 1, 0), jnp.minimum(gz + 1, nz - 1)
    if dense:
        regions = (jnp.maximum(gx - 1, 0), gx, jnp.minimum(gx + 1, nx - 1))
    else:
        regions = (0, 1, 2)
    upper = row < 4
    spread = lane // ZP
    zb = 128 // ZP

    def unfold(tile, t):
        return jnp.take_along_axis(tile, spread + t * zb, axis=1)

    def pull(low_tile, high_tile, s):
        a = pltpu.roll(high_tile, (-3 * s) % 128, 1) if s else high_tile
        b = pltpu.roll(low_tile, (125 - 3 * s) % 128, 1)
        return jnp.where(lane < 64, a, b)

    diag = {}
    flux = {}
    for r in range(3):
        x = regions[r]
        rowtile = jnp.where(upper, got[x, yh, gz], got[x, yl, gz])
        flux[r, 1] = [unfold(rowtile, t) for t in range(3)]
        diag[r, 1] = unfold(rowtile, 3)
        if r == 1:
            flux[r, 0] = [tiles[t] for t in range(3)]
            diag[r, 0] = tiles[3]
        else:
            flux[r, 0] = [unfold(got[x, gy, gz], t) for t in range(3)]
            diag[r, 0] = unfold(got[x, gy, gz], 3)
        side_low, side_high = got[x, gy, zl], got[x, gy, zh]
        corner_low = jnp.where(upper, got[x, yh, zl], got[x, yl, zl])
        corner_high = jnp.where(upper, got[x, yh, zh], got[x, yl, zh])
        diag[r, 2] = pull(side_low, side_high, 3 * slabs)
        diag[r, 3] = pull(corner_low, corner_high, 3 * slabs)
        edge_x = None if r == 1 else one(has_xl if r == 0 else has_xh)
        for c in range(3):
            for k in range(3 if r != 1 else slabs):
                at = k if r == 0 else (3 + k if r == 1 else 3 + slabs + k)
                out = (3 - k) if r == 0 else (0 if r == 1 else k + 1)
                s = c * slabs + (slabs - 3 + k if r == 0 else k)
                value = (source if r == 1 else (xlow if r == 0 else xhigh))[c, k] - flux[r, 0][c]
                w0[c, at, 0] = value if edge_x is None else value * edge_x
                if r == 1:
                    v0[c, k] = value
                if out <= 2:
                    halo = jnp.concatenate([yhigh[c, at], ylow[c, at]], axis=0) - flux[r, 1][c]
                    w0[c, at, 1] = halo * (mask_y if edge_x is None else mask_y * edge_x)
                    value = pull(side_low, side_high, s)
                    w0[c, at, 2] = value * (mask_z if edge_x is None else mask_z * edge_x)
                if out <= 1:
                    value = pull(corner_low, corner_high, s)
                    w0[c, at, 3] = value * (masks[3] if edge_x is None else masks[3] * edge_x)
    for key in diag:
        diag[key] = diag[key] + (6.0 - SHIFT)

    first_row, last_row = row == 0, row == 7
    first_lane, last_lane = lane == 0, lane == 127
    acc = [jnp.zeros((8, 128), jnp.float32) for _ in range(6)]
    levels = (w0, w1, w2, None)
    results = (v0, v1, v2, v3)
    for level in (1, 2, 3):
        src, dst = levels[level - 1], levels[level]
        reach = 3 - level
        for c in range(3):
            for at in range(3 - reach, 3 + slabs + reach):
                out = max(3 - at, at - slabs - 2, 0)
                r = 0 if at < 3 else (1 if at < 3 + slabs else 2)
                depth = reach - out
                want = (0,) if depth == 0 else ((0, 1, 2) if depth == 1 else (0, 1, 2, 3))
                have = (0, 1, 2) if depth == 0 else (0, 1, 2, 3)
                v = {t: src[c, at, t] for t in have}
                left = {t: pltpu.roll(v[t], 127, 1) for t in have if t in (0, 2) or depth > 0}
                right = {t: pltpu.roll(v[t], 1, 1) for t in have if t in (0, 2) or depth > 0}
                down = {t: pltpu.roll(v[t], 7, 0) for t in have if t in (0, 1) or depth > 0}
                over = {t: pltpu.roll(v[t], 1, 0) for t in have if t in (0, 1) or depth > 0}
                edge_x = None if r == 1 else one(has_xl if r == 0 else has_xh)
                for t in want:
                    zp = jnp.where(last_lane, left[t ^ 2], left[t])
                    zm = jnp.where(first_lane, right[t ^ 2], right[t])
                    yp = jnp.where(last_row, down[t ^ 1], down[t])
                    ym = jnp.where(first_row, over[t ^ 1], over[t])
                    beside = (src[c, at - 1, t] + src[c, at + 1, t]) + (zp + zm) + (yp + ym)
                    value = diag[r, t] * v[t] - beside
                    if masks[t] is not None:
                        value = value * masks[t]
                    if edge_x is not None:
                        value = value * edge_x
                    if dst is not None:
                        dst[c, at, t] = value
                    if t == 0 and r == 1:
                        results[level][c, at - 3] = value
                        acc[2 * level - 1] = acc[2 * level - 1] + v[0] * value
                        if level < 3:
                            acc[2 * level] = acc[2 * level] + value * value
                        if level == 1:
                            acc[0] = acc[0] + v[0] * v[0]
    for k in range(6):
        moments[k : k + 1, :] = jnp.sum(acc[k], axis=0, keepdims=True)
    moments[6:8, :] = jnp.zeros((2, 128), jnp.float32)


def combine_kernel(parts, v0, v1, v2, v3, step_out, residual_out):
    total = parts[0]
    for k in range(1, parts.shape[0]):
        total = total + parts[k]
    sums = jnp.sum(total, axis=1, keepdims=True)
    nu = [sums[k : k + 1, :] for k in range(6)]

    def gram(a, b):
        result = None
        for i, ai in enumerate(a):
            for j, bj in enumerate(b):
                term = ai * bj * nu[i + j]
                result = term if result is None else result + term
        return result

    def added(a, b):
        size = max(len(a), len(b))
        return [a[k] if k >= len(b) else (b[k] if k >= len(a) else a[k] + b[k]) for k in range(size)]

    unit = jnp.ones((1, 1), jnp.float32)
    direction, residual, newton = [unit], [unit], []
    norm = nu[0]
    for iteration in range(ITERS):
        image = added([SHIFT * d for d in direction], [0.0 * unit] + direction)
        alpha = norm / gram(direction, image)
        newton = added(newton, [alpha * d for d in direction])
        residual = added(residual, [-alpha * g for g in image])
        if iteration + 1 < ITERS:
            following = gram(residual, residual)
            ratio = following / norm
            direction = added(residual, [ratio * d for d in direction])
            norm = following
    wide = lambda a: jnp.broadcast_to(a, (8, 128))
    newton = [wide(a) for a in newton]
    residual = [wide(a) for a in residual]
    for c in range(v0.shape[0]):
        for x in range(v0.shape[1]):
            a, b, d = v0[c, x], v1[c, x], v2[c, x]
            step_out[c, x] = newton[0] * a + newton[1] * b + newton[2] * d
            residual_out[c, x] = residual[0] * a + residual[1] * b + residual[2] * d + residual[3] * v3[c, x]


def call(body, outs, ins, scratch=(), name=None):
    vmem = pl.BlockSpec(memory_space=pltpu.VMEM)
    return pl.pallas_call(
        body,
        name=name,
        out_shape=tuple(jax.ShapeDtypeStruct(s, d) for s, d in outs),
        in_specs=[vmem] * len(ins),
        out_specs=tuple(vmem for _ in outs),
        scratch_shapes=list(scratch),
    )(*ins)


def ladder(axis):
    count = lax.axis_size(axis)
    forward = [(i, i + 1) for i in range(count - 1)]
    return forward, [(b, a) for a, b in forward]


def from_both(low_face, high_face, axis):
    forward, backward = ladder(axis)
    return lax.ppermute(high_face, axis, forward), lax.ppermute(low_face, axis, backward)


def per_device(source, contrast, point_field, point_class, cell_kind, inverse_blocks):
    f32, bf16 = jnp.float32, jnp.bfloat16
    rows = contrast.shape[0]
    counts = tuple(lax.axis_size(a) for a in AXES)
    nx, ny, nz = counts
    slabs = source.shape[1]
    gx = lax.axis_index("gx")
    dense = nx * ny * nz <= DENSE
    pair = nx == 2
    library = inverse_blocks.transpose(0, 2, 3, 1, 4)
    if pair:
        swap = [(0, 1), (1, 0)]
        other = lax.ppermute(library, "gx", swap)
        face = jnp.where(gx == 0, source[:, slabs - 3 :], source[:, :3])
        face = lax.ppermute(face, "gx", swap)
        xlow = jnp.where(gx == 1, face, 0.0)
        xhigh = jnp.where(gx == 0, face, 0.0)
    else:
        library = lax.all_gather(library, "gx", axis=0, tiled=True)
        other = library
        xlow, xhigh = from_both(source[:, :3], source[:, slabs - 3 :], "gx")
    hartley, spectrum, columns = call(
        spectrum_kernel,
        [((VOX, VOX), bf16), ((3 * rows, VOX), f32), ((rows, 8), f32)],
        (contrast, point_field),
        [pltpu.VMEM((3 * rows, VOX), bf16)],
        name="spectrum",
    )
    longer = jnp.concatenate([xlow, source, xhigh], axis=1)
    ylow, yhigh = from_both(longer[:, :, :4], longer[:, :, 4:], "gy")
    tiles, bundle = call(
        functools.partial(solve_kernel, not pair),
        [((4, 8, 128), f32), ((nx * ny if dense else 1, nz, 8, 128), f32)],
        (contrast, columns, spectrum, hartley, point_class.reshape(1, rows), cell_kind.reshape(1, rows),
         library, other, source),
        [pltpu.VMEM((9, rows, VOX), f32), pltpu.VMEM((3 * rows, VOX), bf16), pltpu.VMEM((3 * rows, VOX), f32)],
        name="solve",
    )
    if dense:
        got = lax.all_to_all(bundle.reshape(nx * ny * nz, 8, 128), AXES, 0, 0).reshape(nx, ny, nz, 8, 128)
    else:
        below, above = from_both(bundle[0], bundle[0], "gx")
        trio = jnp.stack([below, bundle[0], above], axis=1)
        trio = jnp.broadcast_to(trio[None], (ny,) + trio.shape).reshape(ny * nz, 3, 8, 128)
        got = lax.all_to_all(trio, ("gy", "gz"), 0, 0).reshape(ny, nz, 3, 8, 128).transpose(2, 0, 1, 3, 4)
    field = (source.shape, f32)
    v0, v1, v2, v3, moments = call(
        functools.partial(moment_kernel, dense, counts),
        [field, field, field, field, ((8, 128), f32)],
        (tiles, got, source, xlow, xhigh, ylow, yhigh),
        [pltpu.VMEM((3, slabs + 6, 4, 8, 128), f32) for _ in range(3)],
        name="moments",
    )
    if dense:
        parts = jnp.broadcast_to(moments[None], (nx * ny * nz, 8, 128))
        parts = lax.all_to_all(parts, AXES, 0, 0)
    else:
        parts = lax.psum(moments, AXES)[None]
    return call(combine_kernel, [field, field], (parts, v0, v1, v2, v3), name="combine")


def solution(mesh):
    placed = (
        P(None, "gx", "gy", "gz"),
        P(("gx", "gy", "gz"), None),
        P(None, ("gx", "gy", "gz")),
        P(("gx", "gy", "gz"), None),
        P(("gx", "gy", "gz")),
        P("gx", None, None, None, None),
    )
    return jax.shard_map(
        per_device,
        mesh=mesh,
        in_specs=placed,
        out_specs=(P(None, "gx", "gy", "gz"), P(None, "gx", "gy", "gz")),
        check_vma=False,
    )
```

```python
import functools
import math

import jax
import jax.numpy as jnp
from jax import lax
from jax.experimental import pallas as pl
from jax.experimental.pallas import tpu as pltpu
from jax.sharding import PartitionSpec as P


CELL = 8
VOX = 512
TYPES = 4
ZP = 8
ITERS = 3
AXES = ("gx", "gy", "gz")
DENSE = 64
SHIFT = 8.0
GRANT = 16 * 1024 * 1024

kerr_scale = 0.1


def where_am_i():
    return tuple(lax.axis_index(a) for a in AXES)


def spectrum_kernel(pair, count, contrast_in, field_in, class_in, kind_in, source_in, library_in,
                    hartley, spectrum, columns, pick, contrast, source, library, polar, field, classes, kinds, sems):
    rows = contrast.shape[0]
    moves = [(field_in, field), (class_in, classes), (kind_in, kinds), (contrast_in, contrast), (source_in, source)]
    if pair:
        moves.append((library_in, library))
    moves = [pltpu.make_async_copy(a, b, sems.at[k]) for k, (a, b) in enumerate(moves)]
    for move in moves:
        move.start()
    step = CELL * CELL
    inner = lax.broadcasted_iota(jnp.int32, (step, VOX), 0)
    voxel = lax.broadcasted_iota(jnp.int32, (step, VOX), 1)
    phase = (inner // CELL) * (voxel // CELL % CELL) + (inner % CELL) * (voxel % CELL)
    outer = voxel // step
    plain = 1.0 / math.sqrt(VOX)
    peak = math.sqrt(2.0) / math.sqrt(VOX)
    for block in range(VOX // step):
        turn = (phase + block * outer) & (CELL - 1)
        quarter = turn & 3
        size = jnp.where(quarter == 1, peak, jnp.where(quarter == 3, 0.0, plain))
        value = jnp.where(turn >= 4, -size, size)
        hartley[block * step : (block + 1) * step, :] = value.astype(jnp.bfloat16)
    for move in moves[:3]:
        move.wait()
    fields = field[...].astype(jnp.float32)
    fields = jnp.concatenate([fields, jnp.zeros((5, rows), jnp.float32)], axis=0)
    columns[...] = fields.T
    keys = jnp.where(classes[...] == lax.axis_index("gx"), 0, 1) if pair else classes[...]
    keys = keys * TYPES + kinds[...]
    named = (lax.broadcasted_iota(jnp.int32, (count, rows), 0) == keys).astype(jnp.float32)
    named = jnp.concatenate([named, named], axis=0)
    pick[...] = named.T.astype(jnp.bfloat16)
    moves[3].wait()
    for j in range(3):
        e = columns[:, j : j + 1]
        m = contrast[:, j * VOX : (j + 1) * VOX].astype(jnp.float32)
        polar[j * rows : (j + 1) * rows, :] = (m * e).astype(jnp.bfloat16)
    spectrum[...] = jnp.dot(polar[...], hartley[...], preferred_element_type=jnp.float32)
    for move in moves[4:]:
        move.wait()


def solve_kernel(contrast, columns, spectrum, hartley, pick, library, other, source, tiles, bundle,
                 mixing, stacked, product):
    rows = contrast.shape[0]
    zb = rows // 8
    _, _, gz = where_am_i()
    for ij in range(9):
        i, j = ij // 3, ij % 3
        parts = [library[c, i, j] for c in range(library.shape[0])]
        if pick.shape[1] > 2 * TYPES * library.shape[0]:
            parts = parts + [other[c, i, j] for c in range(other.shape[0])]
        table = jnp.concatenate(parts, axis=0)
        high = table.astype(jnp.bfloat16).astype(jnp.float32)
        both = jnp.concatenate([high, table - high], axis=0).astype(jnp.bfloat16)
        mixing[ij] = jnp.dot(pick[...], both, preferred_element_type=jnp.float32)

    def mix(from_ref):
        for c in range(rows // 16):
            at = slice(c * 16, (c + 1) * 16)
            held = [from_ref[j * rows + c * 16 : j * rows + (c + 1) * 16, :] for j in range(3)]
            for i in range(3):
                total = mixing[3 * i, at, :] * held[0]
                total = total + mixing[3 * i + 1, at, :] * held[1]
                total = total + mixing[3 * i + 2, at, :] * held[2]
                stacked[i * rows + c * 16 : i * rows + (c + 1) * 16, :] = total.astype(jnp.bfloat16)

    mix(spectrum)
    product[...] = jnp.dot(stacked[...], hartley[...], preferred_element_type=jnp.float32)
    for c in range(rows // 16):
        for j in range(3):
            at = slice(j * rows + c * 16, j * rows + (c + 1) * 16)
            m = contrast[c * 16 : (c + 1) * 16, j * VOX : (j + 1) * VOX].astype(jnp.float32)
            local = columns[c * 16 : (c + 1) * 16, j : j + 1] - product[at, :]
            stacked[at, :] = (m * local * (1.0 + kerr_scale * local * local)).astype(jnp.bfloat16)
    product[...] = jnp.dot(stacked[...], hartley[...], preferred_element_type=jnp.float32)
    mix(product)
    product[...] = jnp.dot(stacked[...], hartley[...], preferred_element_type=jnp.float32)

    depth = lax.broadcasted_iota(jnp.int32, (zb, 128), 0)
    lane = lax.broadcasted_iota(jnp.int32, (zb, 128), 1)
    spread = lane // ZP == depth
    packed = lane % zb == depth
    group = lane // zb
    for c in range(rows // 16):
        means = []
        stiff = jnp.zeros((16, VOX), jnp.float32)
        for j in range(3):
            at = slice(j * rows + c * 16, j * rows + (c + 1) * 16)
            m = contrast[c * 16 : (c + 1) * 16, j * VOX : (j + 1) * VOX].astype(jnp.float32)
            final = columns[c * 16 : (c + 1) * 16, j : j + 1] - product[at, :]
            means.append(jnp.sum((1.0 + m) * final, axis=1, keepdims=True) * (1.0 / VOX))
            stiff = stiff + m * final * final
        means.append(0.5 + jnp.sum(stiff, axis=1, keepdims=True) * (1.0 / (3 * VOX)))
        compact = jnp.zeros((zb, 128), jnp.float32)
        for t in range(4):
            wide = jnp.broadcast_to(means[t], (zb, 128))
            tiles[t, c : c + 1, :] = jnp.sum(jnp.where(spread, wide, 0.0), axis=0, keepdims=True)
            compact = compact + jnp.where(packed & (group == t), wide, 0.0)
        product[c : c + 1, 0:128] = jnp.sum(compact, axis=0, keepdims=True)
    compact = product[0:8, 0:128]

    place = lax.broadcasted_iota(jnp.int32, (8, 128), 1)
    low = jnp.zeros((8, 128), jnp.float32)
    high = jnp.zeros((8, 128), jnp.float32)
    slabs = source.shape[1]
    for s in range(3 * slabs + 1):
        if s < 3 * slabs:
            value = source[s // slabs, s % slabs] - tiles[s // slabs]
        else:
            value = tiles[3]
        here = (place >= 3 * s) & (place < 3 * s + 3)
        low = jnp.where(here, pltpu.roll(value, (3 * s) % 128, 1) if s else value, low)
        high = jnp.where(here, pltpu.roll(value, (3 * s + 3) % 128, 1), high)
    for d in range(bundle.shape[1]):
        zero = jnp.zeros((8, 128), jnp.float32)
        tile = jnp.where(gz == d, compact, jnp.where(gz + 1 == d, high, jnp.where(gz - 1 == d, low, zero)))
        for x in range(bundle.shape[0]):
            bundle[x, d] = tile


def moment_kernel(dense, counts, tiles, got, source, xlow, xhigh, ylow, yhigh, v0, v1, v2, v3, moments, w0, w1, w2):
    slabs = source.shape[1]
    gx, gy, gz = where_am_i()
    nx, ny, nz = counts
    row = lax.broadcasted_iota(jnp.int32, (8, 128), 0)
    lane = lax.broadcasted_iota(jnp.int32, (8, 128), 1)
    has_xl, has_xh = gx > 0, gx < nx - 1
    has_yl, has_yh = gy > 0, gy < ny - 1
    has_zl, has_zh = gz > 0, gz < nz - 1
    one = lambda flag: jnp.where(flag, 1.0, 0.0)
    mask_y = jnp.where(row < 4, one(has_yh), one(has_yl))
    mask_z = jnp.where(lane < 64, one(has_zh), one(has_zl))
    masks = (None, mask_y, mask_z, mask_y * mask_z)
    yl, yh = jnp.maximum(gy - 1, 0), jnp.minimum(gy + 1, ny - 1)
    zl, zh = jnp.maximum(gz - 1, 0), jnp.minimum(gz + 1, nz - 1)
    if dense:
        regions = (jnp.maximum(gx - 1, 0), gx, jnp.minimum(gx + 1, nx - 1))
    else:
        regions = (0, 1, 2)
    upper = row < 4
    spread = lane // ZP
    zb = 128 // ZP

    def unfold(tile, t):
        return jnp.take_along_axis(tile, spread + t * zb, axis=1)

    def pull(low_tile, high_tile, s):
        a = pltpu.roll(high_tile, (-3 * s) % 128, 1) if s else high_tile
        b = pltpu.roll(low_tile, (125 - 3 * s) % 128, 1)
        return jnp.where(lane < 64, a, b)

    diag = {}
    flux = {}
    for r in range(3):
        x = regions[r]
        rowtile = jnp.where(upper, got[x, yh, gz], got[x, yl, gz])
        flux[r, 1] = [unfold(rowtile, t) for t in range(3)]
        diag[r, 1] = unfold(rowtile, 3)
        if r == 1:
            flux[r, 0] = [tiles[t] for t in range(3)]
            diag[r, 0] = tiles[3]
        else:
            flux[r, 0] = [unfold(got[x, gy, gz], t) for t in range(3)]
            diag[r, 0] = unfold(got[x, gy, gz], 3)
        side_low, side_high = got[x, gy, zl], got[x, gy, zh]
        corner_low = jnp.where(upper, got[x, yh, zl], got[x, yl, zl])
        corner_high = jnp.where(upper, got[x, yh, zh], got[x, yl, zh])
        diag[r, 2] = pull(side_low, side_high, 3 * slabs)
        diag[r, 3] = pull(corner_low, corner_high, 3 * slabs)
        edge_x = None if r == 1 else one(has_xl if r == 0 else has_xh)
        for c in range(3):
            for k in range(3 if r != 1 else slabs):
                at = k if r == 0 else (3 + k if r == 1 else 3 + slabs + k)
                out = (3 - k) if r == 0 else (0 if r == 1 else k + 1)
                s = c * slabs + (slabs - 3 + k if r == 0 else k)
                value = (source if r == 1 else (xlow if r == 0 else xhigh))[c, k] - flux[r, 0][c]
                w0[c, at, 0] = value if edge_x is None else value * edge_x
                if r == 1:
                    v0[c, k] = value
                if out <= 2:
                    halo = jnp.concatenate([yhigh[c, at], ylow[c, at]], axis=0) - flux[r, 1][c]
                    w0[c, at, 1] = halo * (mask_y if edge_x is None else mask_y * edge_x)
                    value = pull(side_low, side_high, s)
                    w0[c, at, 2] = value * (mask_z if edge_x is None else mask_z * edge_x)
                if out <= 1:
                    value = pull(corner_low, corner_high, s)
                    w0[c, at, 3] = value * (masks[3] if edge_x is None else masks[3] * edge_x)
    for key in diag:
        diag[key] = diag[key] + (6.0 - SHIFT)

    first_row, last_row = row == 0, row == 7
    first_lane, last_lane = lane == 0, lane == 127
    acc = [jnp.zeros((8, 128), jnp.float32) for _ in range(6)]
    levels = (w0, w1, w2, None)
    results = (v0, v1, v2, v3)
    for level in (1, 2, 3):
        src, dst = levels[level - 1], levels[level]
        reach = 3 - level
        for c in range(3):
            for at in range(3 - reach, 3 + slabs + reach):
                out = max(3 - at, at - slabs - 2, 0)
                r = 0 if at < 3 else (1 if at < 3 + slabs else 2)
                depth = reach - out
                want = (0,) if depth == 0 else ((0, 1, 2) if depth == 1 else (0, 1, 2, 3))
                have = (0, 1, 2) if depth == 0 else (0, 1, 2, 3)
                v = {t: src[c, at, t] for t in have}
                left = {t: pltpu.roll(v[t], 127, 1) for t in have if t in (0, 2) or depth > 0}
                right = {t: pltpu.roll(v[t], 1, 1) for t in have if t in (0, 2) or depth > 0}
                down = {t: pltpu.roll(v[t], 7, 0) for t in have if t in (0, 1) or depth > 0}
                over = {t: pltpu.roll(v[t], 1, 0) for t in have if t in (0, 1) or depth > 0}
                edge_x = None if r == 1 else one(has_xl if r == 0 else has_xh)
                for t in want:
                    zp = jnp.where(last_lane, left[t ^ 2], left[t])
                    zm = jnp.where(first_lane, right[t ^ 2], right[t])
                    yp = jnp.where(last_row, down[t ^ 1], down[t])
                    ym = jnp.where(first_row, over[t ^ 1], over[t])
                    beside = (src[c, at - 1, t] + src[c, at + 1, t]) + (zp + zm) + (yp + ym)
                    value = diag[r, t] * v[t] - beside
                    if masks[t] is not None:
                        value = value * masks[t]
                    if edge_x is not None:
                        value = value * edge_x
                    if dst is not None:
                        dst[c, at, t] = value
                    if t == 0 and r == 1:
                        results[level][c, at - 3] = value
                        acc[2 * level - 1] = acc[2 * level - 1] + v[0] * value
                        if level < 3:
                            acc[2 * level] = acc[2 * level] + value * value
                        if level == 1:
                            acc[0] = acc[0] + v[0] * v[0]
    line = jnp.zeros((1, 128), jnp.float32)
    slot = lax.broadcasted_iota(jnp.int32, (1, 128), 1)
    for k in range(6):
        sums = jnp.sum(jnp.sum(acc[k], axis=0, keepdims=True), axis=1, keepdims=True)
        line = jnp.where(slot == k, sums, line)
    moments[...] = jnp.broadcast_to(line[None], moments.shape)


def combine_kernel(parts, v0, v1, v2, v3, step_out, residual_out):
    total = jnp.sum(parts[...], axis=0)
    nu = [total[:, k : k + 1] for k in range(6)]

    def gram(a, b):
        result = None
        for i, ai in enumerate(a):
            for j, bj in enumerate(b):
                term = ai * bj * nu[i + j]
                result = term if result is None else result + term
        return result

    def added(a, b):
        size = max(len(a), len(b))
        return [a[k] if k >= len(b) else (b[k] if k >= len(a) else a[k] + b[k]) for k in range(size)]

    unit = jnp.ones((1, 1), jnp.float32)
    direction, residual, newton = [unit], [unit], []
    norm = nu[0]
    for iteration in range(ITERS):
        image = added([SHIFT * d for d in direction], [0.0 * unit] + direction)
        alpha = norm / gram(direction, image)
        newton = added(newton, [alpha * d for d in direction])
        residual = added(residual, [-alpha * g for g in image])
        if iteration + 1 < ITERS:
            following = gram(residual, residual)
            ratio = following / norm
            direction = added(residual, [ratio * d for d in direction])
            norm = following
    wide = lambda a: jnp.broadcast_to(a, (8, 128))
    newton = [wide(a) for a in newton]
    residual = [wide(a) for a in residual]
    for c in range(v0.shape[0]):
        for x in range(v0.shape[1]):
            a, b, d = v0[c, x], v1[c, x], v2[c, x]
            step_out[c, x] = newton[0] * a + newton[1] * b + newton[2] * d
            residual_out[c, x] = residual[0] * a + residual[1] * b + residual[2] * d + residual[3] * v3[c, x]


def call(body, outs, ins, scratch=(), last=False, raw=False):
    vmem = pl.BlockSpec(memory_space=pltpu.VMEM)
    shape = jax.ShapeDtypeStruct if last else pltpu.VMEM
    return pl.pallas_call(
        body,
        out_shape=tuple(shape(s, d) for s, d in outs),
        in_specs=[pl.BlockSpec(memory_space=pltpu.HBM) if raw else vmem] * len(ins),
        out_specs=tuple(vmem for _ in outs),
        scratch_shapes=list(scratch),
        compiler_params=pltpu.CompilerParams(vmem_limit_bytes=GRANT),
    )(*(pltpu.with_memory_space_constraint(x, pltpu.HBM if raw else pltpu.VMEM) for x in ins))


def ladder(axis):
    count = lax.axis_size(axis)
    forward = [(i, i + 1) for i in range(count - 1)]
    return forward, [(b, a) for a, b in forward]


def from_both(low_face, high_face, axis):
    forward, backward = ladder(axis)
    up = lax.ppermute(high_face, axis, forward)
    down = lax.ppermute(low_face, axis, backward)
    return up, down


def whole_step(source, contrast, point_field, point_class, cell_kind, inverse_blocks):
    f32, bf16 = jnp.float32, jnp.bfloat16
    rows = contrast.shape[0]
    counts = tuple(lax.axis_size(a) for a in AXES)
    nx, ny, nz = counts
    devices = nx * ny * nz
    slabs = source.shape[1]
    gx = lax.axis_index("gx")
    dense = devices <= DENSE
    pair = nx == 2
    library = inverse_blocks.transpose(0, 2, 3, 1, 4)
    field = (source.shape, f32)
    if pair:
        swap = [(0, 1), (1, 0)]
        other = lax.ppermute(library, "gx", swap)
        face = jnp.where(gx == 0, source[:, slabs - 3 :], source[:, :3])
        face = lax.ppermute(face, "gx", swap)
        xlow = jnp.where(gx == 1, face, 0.0)
        xhigh = jnp.where(gx == 0, face, 0.0)
    else:
        other = lax.all_gather(library, "gx", axis=0, tiled=True)
        xlow, xhigh = from_both(source[:, :3], source[:, slabs - 3 :], "gx")
    count = TYPES * nx
    hartley, spectrum, columns, pick, contrast, source, library = call(
        functools.partial(spectrum_kernel, pair, count),
        [((VOX, VOX), bf16), ((3 * rows, VOX), f32), ((rows, 8), f32), ((rows, 2 * count), bf16),
         (contrast.shape, bf16), field, (library.shape, f32)],
        (contrast, point_field, point_class.reshape(1, rows), cell_kind.reshape(1, rows), source, library),
        [pltpu.VMEM((3 * rows, VOX), bf16), pltpu.VMEM((3, rows), bf16), pltpu.VMEM((1, rows), jnp.int32),
         pltpu.VMEM((1, rows), jnp.int32), pltpu.SemaphoreType.DMA((6,))],
        raw=True,
    )
    longer = jnp.concatenate([xlow, source, xhigh], axis=1)
    ylow, yhigh = from_both(longer[:, :, :4], longer[:, :, 4:], "gy")
    tiles, bundle = call(
        solve_kernel,
        [((4, 8, 128), f32), ((nx * ny if dense else 1, nz, 8, 128), f32)],
        (contrast, columns, spectrum, hartley, pick, library if pair else other, other, source),
        [pltpu.VMEM((9, rows, VOX), f32), pltpu.VMEM((3 * rows, VOX), bf16), pltpu.VMEM((3 * rows, VOX), f32)],
    )
    if dense:
        got = lax.all_to_all(bundle.reshape(devices, 8, 128), AXES, 0, 0).reshape(nx, ny, nz, 8, 128)
    else:
        below, above = from_both(bundle[0], bundle[0], "gx")
        trio = jnp.stack([below, bundle[0], above], axis=1)
        trio = jnp.broadcast_to(trio[None], (ny,) + trio.shape).reshape(ny * nz, 3, 8, 128)
        got = lax.all_to_all(trio, ("gy", "gz"), 0, 0).reshape(ny, nz, 3, 8, 128).transpose(2, 0, 1, 3, 4)
    v0, v1, v2, v3, moments = call(
        functools.partial(moment_kernel, dense, counts),
        [field, field, field, field, ((devices if dense else 1, 1, 128), f32)],
        (tiles, got, source, xlow, xhigh, ylow, yhigh),
        [pltpu.VMEM((3, slabs + 6, 4, 8, 128), f32) for _ in range(3)],
    )
    if dense:
        parts = lax.all_to_all(moments, AXES, 0, 0)
    else:
        parts = lax.psum(moments, AXES)
    return call(combine_kernel, [field, field], (parts, v0, v1, v2, v3), last=True)


def solution(mesh):
    placed = (
        P(None, "gx", "gy", "gz"),
        P(("gx", "gy", "gz"), None),
        P(None, ("gx", "gy", "gz")),
        P(("gx", "gy", "gz"), None),
        P(("gx", "gy", "gz")),
        P("gx", None, None, None, None),
    )
    return jax.shard_map(
        whole_step,
        mesh=mesh,
        in_specs=placed,
        out_specs=(P(None, "gx", "gy", "gz"), P(None, "gx", "gy", "gz")),
        check_vma=False,
    )
```

```python
import functools
import math

import jax
import jax.numpy as jnp
from jax import lax
from jax.experimental import pallas as pl
from jax.experimental.pallas import tpu as pltpu
from jax.sharding import PartitionSpec as P


CELL = 8
VOX = 512
TYPES = 4
ZP = 8
ITERS = 3
AXES = ("gx", "gy", "gz")
DENSE = 64
SHIFT = 8.0
GRANT = 16 * 1024 * 1024

kerr_scale = 0.1


def where_am_i():
    return tuple(lax.axis_index(a) for a in AXES)


def spectrum_kernel(pair, count, contrast_in, field_in, class_in, kind_in, source_in, library_in,
                    hartley, spectrum, columns, pick, contrast, source, library, face,
                    polar, field, classes, kinds, plain_source, sems):
    rows = contrast.shape[0]
    slabs = source.shape[1]
    gx = lax.axis_index("gx")
    moves = [(field_in, field), (class_in, classes), (kind_in, kinds), (contrast_in, contrast),
             (source_in, plain_source)]
    if pair:
        moves.append((library_in, library))
    moves = [pltpu.make_async_copy(a, b, sems.at[k]) for k, (a, b) in enumerate(moves)]
    for move in moves:
        move.start()
    step = CELL * CELL
    inner = lax.broadcasted_iota(jnp.int32, (step, VOX), 0)
    voxel = lax.broadcasted_iota(jnp.int32, (step, VOX), 1)
    phase = (inner // CELL) * (voxel // CELL % CELL) + (inner % CELL) * (voxel % CELL)
    outer = voxel // step
    plain = 1.0 / math.sqrt(VOX)
    peak = math.sqrt(2.0) / math.sqrt(VOX)
    for block in range(VOX // step):
        turn = (phase + block * outer) & (CELL - 1)
        quarter = turn & 3
        size = jnp.where(quarter == 1, peak, jnp.where(quarter == 3, 0.0, plain))
        value = jnp.where(turn >= 4, -size, size)
        hartley[block * step : (block + 1) * step, :] = value.astype(jnp.bfloat16)
    for move in moves[:3]:
        move.wait()
    fields = field[...].astype(jnp.float32)
    fields = jnp.concatenate([fields, jnp.zeros((5, rows), jnp.float32)], axis=0)
    columns[...] = fields.T
    keys = jnp.where(classes[...] == gx, 0, 1) if pair else classes[...]
    keys = keys * TYPES + kinds[...]
    named = (lax.broadcasted_iota(jnp.int32, (count, rows), 0) == keys).astype(jnp.float32)
    named = jnp.concatenate([named, named], axis=0)
    pick[...] = named.T.astype(jnp.bfloat16)
    moves[3].wait()
    for j in range(3):
        e = columns[:, j : j + 1]
        m = contrast[:, j * VOX : (j + 1) * VOX].astype(jnp.float32)
        polar[j * rows : (j + 1) * rows, :] = (m * e).astype(jnp.bfloat16)
    spectrum[...] = jnp.dot(polar[...], hartley[...], preferred_element_type=jnp.float32)
    for move in moves[4:]:
        move.wait()
    for p in range(slabs):
        x = jnp.where(gx == 0, p, slabs - 1 - p) if pair else p
        for c in range(3):
            value = plain_source[c, x]
            source[c, p] = value
            if p >= slabs - 3:
                face[c, slabs - 1 - p] = value


def solve_kernel(contrast, columns, spectrum, hartley, pick, library, other, source, tiles, bundle,
                 mixing, stacked, product):
    rows = contrast.shape[0]
    zb = rows // 8
    _, _, gz = where_am_i()
    for ij in range(9):
        i, j = ij // 3, ij % 3
        parts = [library[c, i, j] for c in range(library.shape[0])]
        if pick.shape[1] > 2 * TYPES * library.shape[0]:
            parts = parts + [other[c, i, j] for c in range(other.shape[0])]
        table = jnp.concatenate(parts, axis=0)
        high = table.astype(jnp.bfloat16).astype(jnp.float32)
        both = jnp.concatenate([high, table - high], axis=0).astype(jnp.bfloat16)
        mixing[ij] = jnp.dot(pick[...], both, preferred_element_type=jnp.float32)

    def mix(from_ref):
        for c in range(rows // 16):
            at = slice(c * 16, (c + 1) * 16)
            held = [from_ref[j * rows + c * 16 : j * rows + (c + 1) * 16, :] for j in range(3)]
            for i in range(3):
                total = mixing[3 * i, at, :] * held[0]
                total = total + mixing[3 * i + 1, at, :] * held[1]
                total = total + mixing[3 * i + 2, at, :] * held[2]
                stacked[i * rows + c * 16 : i * rows + (c + 1) * 16, :] = total.astype(jnp.bfloat16)

    mix(spectrum)
    product[...] = jnp.dot(stacked[...], hartley[...], preferred_element_type=jnp.float32)
    for c in range(rows // 16):
        for j in range(3):
            at = slice(j * rows + c * 16, j * rows + (c + 1) * 16)
            m = contrast[c * 16 : (c + 1) * 16, j * VOX : (j + 1) * VOX].astype(jnp.float32)
            local = columns[c * 16 : (c + 1) * 16, j : j + 1] - product[at, :]
            stacked[at, :] = (m * local * (1.0 + kerr_scale * local * local)).astype(jnp.bfloat16)
    product[...] = jnp.dot(stacked[...], hartley[...], preferred_element_type=jnp.float32)
    mix(product)
    product[...] = jnp.dot(stacked[...], hartley[...], preferred_element_type=jnp.float32)

    depth = lax.broadcasted_iota(jnp.int32, (zb, 128), 0)
    lane = lax.broadcasted_iota(jnp.int32, (zb, 128), 1)
    spread = lane // ZP == depth
    packed = lane % zb == depth
    group = lane // zb
    for c in range(rows // 16):
        means = []
        stiff = jnp.zeros((16, VOX), jnp.float32)
        for j in range(3):
            at = slice(j * rows + c * 16, j * rows + (c + 1) * 16)
            m = contrast[c * 16 : (c + 1) * 16, j * VOX : (j + 1) * VOX].astype(jnp.float32)
            final = columns[c * 16 : (c + 1) * 16, j : j + 1] - product[at, :]
            means.append(jnp.sum((1.0 + m) * final, axis=1, keepdims=True) * (1.0 / VOX))
            stiff = stiff + m * final * final
        means.append(0.5 + jnp.sum(stiff, axis=1, keepdims=True) * (1.0 / (3 * VOX)))
        compact = jnp.zeros((zb, 128), jnp.float32)
        for t in range(4):
            wide = jnp.broadcast_to(means[t], (zb, 128))
            tiles[t, c : c + 1, :] = jnp.sum(jnp.where(spread, wide, 0.0), axis=0, keepdims=True)
            compact = compact + jnp.where(packed & (group == t), wide, 0.0)
        product[c : c + 1, 0:128] = jnp.sum(compact, axis=0, keepdims=True)
    compact = product[0:8, 0:128]

    place = lax.broadcasted_iota(jnp.int32, (8, 128), 1)
    low = jnp.zeros((8, 128), jnp.float32)
    high = jnp.zeros((8, 128), jnp.float32)
    slabs = source.shape[1]
    for s in range(3 * slabs + 1):
        if s < 3 * slabs:
            value = source[s // slabs, s % slabs] - tiles[s // slabs]
        else:
            value = tiles[3]
        here = (place >= 3 * s) & (place < 3 * s + 3)
        low = jnp.where(here, pltpu.roll(value, (3 * s) % 128, 1) if s else value, low)
        high = jnp.where(here, pltpu.roll(value, (3 * s + 3) % 128, 1), high)
    for d in range(bundle.shape[1]):
        zero = jnp.zeros((8, 128), jnp.float32)
        tile = jnp.where(gz == d, compact, jnp.where(gz + 1 == d, high, jnp.where(gz - 1 == d, low, zero)))
        for x in range(bundle.shape[0]):
            bundle[x, d] = tile


def moment_kernel(dense, counts, tiles, got, source, xlow, xhigh, ya, yb, v0, v1, v2, v3, moments, w0, w1, w2):
    slabs = source.shape[1]
    gx, gy, gz = where_am_i()
    nx, ny, nz = counts
    pair = nx == 2
    base = 0 if pair else 3
    row = lax.broadcasted_iota(jnp.int32, (8, 128), 0)
    lane = lax.broadcasted_iota(jnp.int32, (8, 128), 1)
    even = gy % 2 == 0
    has_xl, has_xh = gx > 0, gx < nx - 1
    has_yl, has_yh = gy > 0, gy < ny - 1
    has_zl, has_zh = gz > 0, gz < nz - 1
    one = lambda flag: jnp.where(flag, 1.0, 0.0)
    mask_y = jnp.where(row < 4, one(has_yh), one(has_yl))
    mask_z = jnp.where(lane < 64, one(has_zh), one(has_zl))
    masks = (None, mask_y, mask_z, mask_y * mask_z)
    yl, yh = jnp.maximum(gy - 1, 0), jnp.minimum(gy + 1, ny - 1)
    zl, zh = jnp.maximum(gz - 1, 0), jnp.minimum(gz + 1, nz - 1)
    if pair:
        regions = (None, gx, 1 - gx)
    elif dense:
        regions = (jnp.maximum(gx - 1, 0), gx, jnp.minimum(gx + 1, nx - 1))
    else:
        regions = (0, 1, 2)
    upper = row < 4
    spread = lane // ZP
    zb = 128 // ZP

    def unfold(tile, t):
        return jnp.take_along_axis(tile, spread + t * zb, axis=1)

    def pull(low_tile, high_tile, s):
        a = pltpu.roll(high_tile, (-3 * s) % 128, 1) if s else high_tile
        b = pltpu.roll(low_tile, (125 - 3 * s) % 128, 1)
        return jnp.where(lane < 64, a, b)

    diag = {}
    flux = {}
    edges = {1: None, 2: None} if pair else {0: one(has_xl), 1: None, 2: one(has_xh)}
    for r in edges:
        x = regions[r]
        rowtile = jnp.where(upper, got[x, yh, gz], got[x, yl, gz])
        flux[r, 1] = [unfold(rowtile, t) for t in range(3)]
        diag[r, 1] = unfold(rowtile, 3)
        if r == 1:
            flux[r, 0] = [tiles[t] for t in range(3)]
            diag[r, 0] = tiles[3]
        else:
            flux[r, 0] = [unfold(got[x, gy, gz], t) for t in range(3)]
            diag[r, 0] = unfold(got[x, gy, gz], 3)
        side_low, side_high = got[x, gy, zl], got[x, gy, zh]
        corner_low = jnp.where(upper, got[x, yh, zl], got[x, yl, zl])
        corner_high = jnp.where(upper, got[x, yh, zh], got[x, yl, zh])
        diag[r, 2] = pull(side_low, side_high, 3 * slabs)
        diag[r, 3] = pull(corner_low, corner_high, 3 * slabs)
        edge_x = edges[r]
        for c in range(3):
            for k in range(slabs if r == 1 else 3):
                at = k if r == 0 else (base + k if r == 1 else base + slabs + k)
                out = (3 - k) if r == 0 else (0 if r == 1 else k + 1)
                s = slabs - 3 + k if r == 0 else (slabs - 1 - k if pair and r == 2 else k)
                s = c * slabs + s
                value = (source if r == 1 else (xlow if r == 0 else xhigh))[c, k] - flux[r, 0][c]
                w0[c, at, 0] = value if edge_x is None else value * edge_x
                if r == 1:
                    v0[c, k] = value
                if out <= 2:
                    a, b = ya[c, at], yb[c, at]
                    halo = jnp.concatenate([jnp.where(even, a, b), jnp.where(even, b, a)], axis=0)
                    halo = halo - flux[r, 1][c]
                    w0[c, at, 1] = halo * (mask_y if edge_x is None else mask_y * edge_x)
                    value = pull(side_low, side_high, s)
                    w0[c, at, 2] = value * (mask_z if edge_x is None else mask_z * edge_x)
                if out <= 1:
                    value = pull(corner_low, corner_high, s)
                    w0[c, at, 3] = value * (masks[3] if edge_x is None else masks[3] * edge_x)
    for key in diag:
        diag[key] = diag[key] + (6.0 - SHIFT)

    first_row, last_row = row == 0, row == 7
    first_lane, last_lane = lane == 0, lane == 127
    acc = [jnp.zeros((8, 128), jnp.float32) for _ in range(6)]
    levels = (w0, w1, w2, None)
    results = (v0, v1, v2, v3)
    for level in (1, 2, 3):
        src, dst = levels[level - 1], levels[level]
        reach = 3 - level
        for c in range(3):
            for at in range(max(base - reach, 0), base + slabs + reach):
                out = max(base - at, at - base - slabs + 1, 0)
                r = 0 if at < base else (1 if at < base + slabs else 2)
                depth = reach - out
                want = (0,) if depth == 0 else ((0, 1, 2) if depth == 1 else (0, 1, 2, 3))
                have = (0, 1, 2) if depth == 0 else (0, 1, 2, 3)
                v = {t: src[c, at, t] for t in have}
                left = {t: pltpu.roll(v[t], 127, 1) for t in have if t in (0, 2) or depth > 0}
                right = {t: pltpu.roll(v[t], 1, 1) for t in have if t in (0, 2) or depth > 0}
                down = {t: pltpu.roll(v[t], 7, 0) for t in have if t in (0, 1) or depth > 0}
                over = {t: pltpu.roll(v[t], 1, 0) for t in have if t in (0, 1) or depth > 0}
                edge_x = edges[r]
                for t in want:
                    zp = jnp.where(last_lane, left[t ^ 2], left[t])
                    zm = jnp.where(first_lane, right[t ^ 2], right[t])
                    yp = jnp.where(last_row, down[t ^ 1], down[t])
                    ym = jnp.where(first_row, over[t ^ 1], over[t])
                    beside = src[c, at + 1, t] + (zp + zm) + (yp + ym)
                    if at > 0:
                        beside = beside + src[c, at - 1, t]
                    value = diag[r, t] * v[t] - beside
                    if masks[t] is not None:
                        value = value * masks[t]
                    if edge_x is not None:
                        value = value * edge_x
                    if dst is not None:
                        dst[c, at, t] = value
                    if t == 0 and r == 1:
                        results[level][c, at - base] = value
                        acc[2 * level - 1] = acc[2 * level - 1] + v[0] * value
                        if level < 3:
                            acc[2 * level] = acc[2 * level] + value * value
                        if level == 1:
                            acc[0] = acc[0] + v[0] * v[0]
    line = jnp.zeros((1, 128), jnp.float32)
    slot = lax.broadcasted_iota(jnp.int32, (1, 128), 1)
    for k in range(6):
        sums = jnp.sum(jnp.sum(acc[k], axis=0, keepdims=True), axis=1, keepdims=True)
        line = jnp.where(slot == k, sums, line)
    moments[...] = jnp.broadcast_to(line[None], moments.shape)


def combine_kernel(pair, parts, v0, v1, v2, v3, step_out, residual_out):
    total = jnp.sum(parts[...], axis=0)
    nu = [total[:, k : k + 1] for k in range(6)]

    def gram(a, b):
        result = None
        for i, ai in enumerate(a):
            for j, bj in enumerate(b):
                term = ai * bj * nu[i + j]
                result = term if result is None else result + term
        return result

    def added(a, b):
        size = max(len(a), len(b))
        return [a[k] if k >= len(b) else (b[k] if k >= len(a) else a[k] + b[k]) for k in range(size)]

    unit = jnp.ones((1, 1), jnp.float32)
    direction, residual, newton = [unit], [unit], []
    norm = nu[0]
    for iteration in range(ITERS):
        image = added([SHIFT * d for d in direction], [0.0 * unit] + direction)
        alpha = norm / gram(direction, image)
        newton = added(newton, [alpha * d for d in direction])
        residual = added(residual, [-alpha * g for g in image])
        if iteration + 1 < ITERS:
            following = gram(residual, residual)
            ratio = following / norm
            direction = added(residual, [ratio * d for d in direction])
            norm = following
    wide = lambda a: jnp.broadcast_to(a, (8, 128))
    newton = [wide(a) for a in newton]
    residual = [wide(a) for a in residual]
    for c in range(v0.shape[0]):
        for x in range(v0.shape[1]):
            a, b, d = v0[c, x], v1[c, x], v2[c, x]
            to = jnp.where(lax.axis_index("gx") == 0, x, v0.shape[1] - 1 - x) if pair else x
            step_out[c, to] = newton[0] * a + newton[1] * b + newton[2] * d
            residual_out[c, to] = residual[0] * a + residual[1] * b + residual[2] * d + residual[3] * v3[c, x]


def call(body, outs, ins, scratch=(), last=False, raw=False):
    vmem = pl.BlockSpec(memory_space=pltpu.VMEM)
    shape = jax.ShapeDtypeStruct if last else pltpu.VMEM
    return pl.pallas_call(
        body,
        out_shape=tuple(shape(s, d) for s, d in outs),
        in_specs=[pl.BlockSpec(memory_space=pltpu.HBM) if raw else vmem] * len(ins),
        out_specs=tuple(vmem for _ in outs),
        scratch_shapes=list(scratch),
        compiler_params=pltpu.CompilerParams(vmem_limit_bytes=GRANT),
    )(*(pltpu.with_memory_space_constraint(x, pltpu.HBM if raw else pltpu.VMEM) for x in ins))


def ladder(axis):
    count = lax.axis_size(axis)
    forward = [(i, i + 1) for i in range(count - 1)]
    return forward, [(b, a) for a, b in forward]


def pairs_from(first, count):
    couples = [(i, i + 1) for i in range(first, count - 1, 2)]
    return couples + [(b, a) for a, b in couples]


def from_both(low_face, high_face, axis):
    forward, backward = ladder(axis)
    up = lax.ppermute(high_face, axis, forward)
    down = lax.ppermute(low_face, axis, backward)
    return up, down


def whole_step(source, contrast, point_field, point_class, cell_kind, inverse_blocks):
    f32, bf16 = jnp.float32, jnp.bfloat16
    rows = contrast.shape[0]
    counts = tuple(lax.axis_size(a) for a in AXES)
    nx, ny, nz = counts
    devices = nx * ny * nz
    slabs = source.shape[1]
    dense = devices <= DENSE
    pair = nx == 2
    library = inverse_blocks.transpose(0, 2, 3, 1, 4)
    field = (source.shape, f32)
    if pair:
        swap = [(0, 1), (1, 0)]
        other = lax.ppermute(library, "gx", swap)
    else:
        other = lax.all_gather(library, "gx", axis=0, tiled=True)
    count = TYPES * nx
    hartley, spectrum, columns, pick, contrast, source, library, face = call(
        functools.partial(spectrum_kernel, pair, count),
        [((VOX, VOX), bf16), ((3 * rows, VOX), f32), ((rows, 8), f32), ((rows, 2 * count), bf16),
         (contrast.shape, bf16), field, (library.shape, f32), ((3, 3, 8, 128), f32)],
        (contrast, point_field, point_class.reshape(1, rows), cell_kind.reshape(1, rows), source, library),
        [pltpu.VMEM((3 * rows, VOX), bf16), pltpu.VMEM((3, rows), bf16), pltpu.VMEM((1, rows), jnp.int32),
         pltpu.VMEM((1, rows), jnp.int32), pltpu.VMEM(*field), pltpu.SemaphoreType.DMA((6,))],
        raw=True,
    )
    if pair:
        face = lax.ppermute(face, "gx", swap)
        xlow = xhigh = face
        longer = jnp.concatenate([source, face[:, :2]], axis=1)
    else:
        xlow, xhigh = from_both(source[:, :3], source[:, slabs - 3 :], "gx")
        longer = jnp.concatenate([xlow, source, xhigh], axis=1)
    even = lax.axis_index("gy") % 2 == 0
    low_rows, high_rows = longer[:, :, :4], longer[:, :, 4:]
    ya = lax.ppermute(jnp.where(even, high_rows, low_rows), "gy", pairs_from(0, ny))
    yb = lax.ppermute(jnp.where(even, low_rows, high_rows), "gy", pairs_from(1, ny))
    tiles, bundle = call(
        solve_kernel,
        [((4, 8, 128), f32), ((nx * ny if dense else 1, nz, 8, 128), f32)],
        (contrast, columns, spectrum, hartley, pick, library if pair else other, other, source),
        [pltpu.VMEM((9, rows, VOX), f32), pltpu.VMEM((3 * rows, VOX), bf16), pltpu.VMEM((3 * rows, VOX), f32)],
    )
    if dense:
        got = lax.all_to_all(bundle.reshape(devices, 8, 128), AXES, 0, 0).reshape(nx, ny, nz, 8, 128)
    else:
        below, above = from_both(bundle[0], bundle[0], "gx")
        trio = jnp.stack([below, bundle[0], above], axis=1)
        trio = jnp.broadcast_to(trio[None], (ny,) + trio.shape).reshape(ny * nz, 3, 8, 128)
        got = lax.all_to_all(trio, ("gy", "gz"), 0, 0).reshape(ny, nz, 3, 8, 128).transpose(2, 0, 1, 3, 4)
    v0, v1, v2, v3, moments = call(
        functools.partial(moment_kernel, dense, counts),
        [field, field, field, field, ((devices if dense else 1, 1, 128), f32)],
        (tiles, got, source, xlow, xhigh, ya, yb),
        [pltpu.VMEM((3, slabs + (3 if pair else 6), 4, 8, 128), f32) for _ in range(3)],
    )
    if dense:
        parts = lax.all_to_all(moments, AXES, 0, 0)
    else:
        parts = lax.psum(moments, AXES)
    return call(functools.partial(combine_kernel, pair), [field, field], (parts, v0, v1, v2, v3), last=True)


def solution(mesh):
    placed = (
        P(None, "gx", "gy", "gz"),
        P(("gx", "gy", "gz"), None),
        P(None, ("gx", "gy", "gz")),
        P(("gx", "gy", "gz"), None),
        P(("gx", "gy", "gz")),
        P("gx", None, None, None, None),
    )
    return jax.shard_map(
        whole_step,
        mesh=mesh,
        in_specs=placed,
        out_specs=(P(None, "gx", "gy", "gz"), P(None, "gx", "gy", "gz")),
        check_vma=False,
    )
```

```python
import functools
import math

import jax
import jax.numpy as jnp
from jax import lax
from jax.experimental import pallas as pl
from jax.experimental.pallas import tpu as pltpu
from jax.sharding import PartitionSpec as P


CELL = 8
VOX = 512
TYPES = 4
ZP = 8
ITERS = 3
AXES = ("gx", "gy", "gz")
DENSE = 64
SHIFT = 8.0
GRANT = 16 * 1024 * 1024

kerr_scale = 0.1


def where_am_i():
    return tuple(lax.axis_index(a) for a in AXES)


def spectrum_kernel(pair, count, contrast_in, field_in, class_in, kind_in, source_in, library_in,
                    hartley, spectrum, columns, pick, contrast, source, library,
                    polar, field, classes, kinds, plain_source, sems):
    rows = contrast.shape[0]
    slabs = source.shape[1]
    gx = lax.axis_index("gx")
    moves = [(field_in, field), (class_in, classes), (kind_in, kinds), (contrast_in, contrast),
             (source_in, plain_source)]
    if pair:
        moves.append((library_in, library))
    moves = [pltpu.make_async_copy(a, b, sems.at[k]) for k, (a, b) in enumerate(moves)]
    for move in moves:
        move.start()
    step = CELL * CELL
    inner = lax.broadcasted_iota(jnp.int32, (step, VOX), 0)
    voxel = lax.broadcasted_iota(jnp.int32, (step, VOX), 1)
    phase = (inner // CELL) * (voxel // CELL % CELL) + (inner % CELL) * (voxel % CELL)
    outer = voxel // step
    plain = 1.0 / math.sqrt(VOX)
    peak = math.sqrt(2.0) / math.sqrt(VOX)
    for block in range(VOX // step):
        turn = (phase + block * outer) & (CELL - 1)
        quarter = turn & 3
        size = jnp.where(quarter == 1, peak, jnp.where(quarter == 3, 0.0, plain))
        value = jnp.where(turn >= 4, -size, size)
        hartley[block * step : (block + 1) * step, :] = value.astype(jnp.bfloat16)
    for move in moves[:3]:
        move.wait()
    fields = field[...].astype(jnp.float32)
    fields = jnp.concatenate([fields, jnp.zeros((5, rows), jnp.float32)], axis=0)
    columns[...] = fields.T
    keys = jnp.where(classes[...] == gx, 0, 1) if pair else classes[...]
    keys = keys * TYPES + kinds[...]
    named = (lax.broadcasted_iota(jnp.int32, (count, rows), 0) == keys).astype(jnp.float32)
    named = jnp.concatenate([named, named], axis=0)
    pick[...] = named.T.astype(jnp.bfloat16)
    moves[3].wait()
    for j in range(3):
        e = columns[:, j : j + 1]
        m = contrast[:, j * VOX : (j + 1) * VOX].astype(jnp.float32)
        polar[j * rows : (j + 1) * rows, :] = (m * e).astype(jnp.bfloat16)
    spectrum[...] = jnp.dot(polar[...], hartley[...], preferred_element_type=jnp.float32)
    for move in moves[4:]:
        move.wait()
    for p in range(slabs):
        x = jnp.where(gx == 0, p, slabs - 1 - p) if pair else p
        for c in range(3):
            value = plain_source[c, x]
            source[c, p] = value


def solve_kernel(contrast, columns, spectrum, hartley, pick, library, other, source, tiles, bundle,
                 mixing, stacked, product):
    rows = contrast.shape[0]
    zb = rows // 8
    _, _, gz = where_am_i()
    for ij in range(9):
        i, j = ij // 3, ij % 3
        parts = [library[c, i, j] for c in range(library.shape[0])]
        if pick.shape[1] > 2 * TYPES * library.shape[0]:
            parts = parts + [other[c, i, j] for c in range(other.shape[0])]
        table = jnp.concatenate(parts, axis=0)
        high = table.astype(jnp.bfloat16).astype(jnp.float32)
        both = jnp.concatenate([high, table - high], axis=0).astype(jnp.bfloat16)
        mixing[ij] = jnp.dot(pick[...], both, preferred_element_type=jnp.float32)

    def mix(from_ref):
        for c in range(rows // 16):
            at = slice(c * 16, (c + 1) * 16)
            held = [from_ref[j * rows + c * 16 : j * rows + (c + 1) * 16, :] for j in range(3)]
            for i in range(3):
                total = mixing[3 * i, at, :] * held[0]
                total = total + mixing[3 * i + 1, at, :] * held[1]
                total = total + mixing[3 * i + 2, at, :] * held[2]
                stacked[i * rows + c * 16 : i * rows + (c + 1) * 16, :] = total.astype(jnp.bfloat16)

    mix(spectrum)
    product[...] = jnp.dot(stacked[...], hartley[...], preferred_element_type=jnp.float32)
    for c in range(rows // 16):
        for j in range(3):
            at = slice(j * rows + c * 16, j * rows + (c + 1) * 16)
            m = contrast[c * 16 : (c + 1) * 16, j * VOX : (j + 1) * VOX].astype(jnp.float32)
            local = columns[c * 16 : (c + 1) * 16, j : j + 1] - product[at, :]
            stacked[at, :] = (m * local * (1.0 + kerr_scale * local * local)).astype(jnp.bfloat16)
    product[...] = jnp.dot(stacked[...], hartley[...], preferred_element_type=jnp.float32)
    mix(product)
    product[...] = jnp.dot(stacked[...], hartley[...], preferred_element_type=jnp.float32)

    depth = lax.broadcasted_iota(jnp.int32, (zb, 128), 0)
    lane = lax.broadcasted_iota(jnp.int32, (zb, 128), 1)
    spread = lane // ZP == depth
    packed = lane % zb == depth
    group = lane // zb
    for c in range(rows // 16):
        means = []
        stiff = jnp.zeros((16, VOX), jnp.float32)
        for j in range(3):
            at = slice(j * rows + c * 16, j * rows + (c + 1) * 16)
            m = contrast[c * 16 : (c + 1) * 16, j * VOX : (j + 1) * VOX].astype(jnp.float32)
            final = columns[c * 16 : (c + 1) * 16, j : j + 1] - product[at, :]
            means.append(jnp.sum((1.0 + m) * final, axis=1, keepdims=True) * (1.0 / VOX))
            stiff = stiff + m * final * final
        means.append(0.5 + jnp.sum(stiff, axis=1, keepdims=True) * (1.0 / (3 * VOX)))
        compact = jnp.zeros((zb, 128), jnp.float32)
        for t in range(4):
            wide = jnp.broadcast_to(means[t], (zb, 128))
            tiles[t, c : c + 1, :] = jnp.sum(jnp.where(spread, wide, 0.0), axis=0, keepdims=True)
            compact = compact + jnp.where(packed & (group == t), wide, 0.0)
        product[c : c + 1, 0:128] = jnp.sum(compact, axis=0, keepdims=True)
    compact = product[0:8, 0:128]

    place = lax.broadcasted_iota(jnp.int32, (8, 128), 1)
    low = jnp.zeros((8, 128), jnp.float32)
    high = jnp.zeros((8, 128), jnp.float32)
    slabs = source.shape[1]
    for s in range(3 * slabs + 1):
        if s < 3 * slabs:
            value = source[s // slabs, s % slabs] - tiles[s // slabs]
        else:
            value = tiles[3]
        here = (place >= 3 * s) & (place < 3 * s + 3)
        low = jnp.where(here, pltpu.roll(value, (3 * s) % 128, 1) if s else value, low)
        high = jnp.where(here, pltpu.roll(value, (3 * s + 3) % 128, 1), high)
    for d in range(bundle.shape[1]):
        zero = jnp.zeros((8, 128), jnp.float32)
        tile = jnp.where(gz == d, compact, jnp.where(gz + 1 == d, high, jnp.where(gz - 1 == d, low, zero)))
        for x in range(bundle.shape[0]):
            bundle[x, d] = tile


def moment_kernel(dense, counts, tiles, got, source, xlow, xhigh, ya, yb, v0, v1, v2, v3, moments, w0, w1, w2):
    slabs = source.shape[1]
    gx, gy, gz = where_am_i()
    nx, ny, nz = counts
    pair = nx == 2
    base = 0 if pair else 3
    row = lax.broadcasted_iota(jnp.int32, (8, 128), 0)
    lane = lax.broadcasted_iota(jnp.int32, (8, 128), 1)
    even = gy % 2 == 0
    has_xl, has_xh = gx > 0, gx < nx - 1
    has_yl, has_yh = gy > 0, gy < ny - 1
    has_zl, has_zh = gz > 0, gz < nz - 1
    one = lambda flag: jnp.where(flag, 1.0, 0.0)
    mask_y = jnp.where(row < 4, one(has_yh), one(has_yl))
    mask_z = jnp.where(lane < 64, one(has_zh), one(has_zl))
    masks = (None, mask_y, mask_z, mask_y * mask_z)
    yl, yh = jnp.maximum(gy - 1, 0), jnp.minimum(gy + 1, ny - 1)
    zl, zh = jnp.maximum(gz - 1, 0), jnp.minimum(gz + 1, nz - 1)
    if pair:
        regions = (None, gx, 1 - gx)
    elif dense:
        regions = (jnp.maximum(gx - 1, 0), gx, jnp.minimum(gx + 1, nx - 1))
    else:
        regions = (0, 1, 2)
    upper = row < 4
    spread = lane // ZP
    zb = 128 // ZP

    def unfold(tile, t):
        return jnp.take_along_axis(tile, spread + t * zb, axis=1)

    def pull(low_tile, high_tile, s):
        a = pltpu.roll(high_tile, (-3 * s) % 128, 1) if s else high_tile
        b = pltpu.roll(low_tile, (125 - 3 * s) % 128, 1)
        return jnp.where(lane < 64, a, b)

    diag = {}
    flux = {}
    edges = {1: None, 2: None} if pair else {0: one(has_xl), 1: None, 2: one(has_xh)}
    for r in edges:
        x = regions[r]
        rowtile = jnp.where(upper, got[x, yh, gz], got[x, yl, gz])
        flux[r, 1] = [unfold(rowtile, t) for t in range(3)]
        diag[r, 1] = unfold(rowtile, 3)
        if r == 1:
            flux[r, 0] = [tiles[t] for t in range(3)]
            diag[r, 0] = tiles[3]
        else:
            flux[r, 0] = [unfold(got[x, gy, gz], t) for t in range(3)]
            diag[r, 0] = unfold(got[x, gy, gz], 3)
        side_low, side_high = got[x, gy, zl], got[x, gy, zh]
        corner_low = jnp.where(upper, got[x, yh, zl], got[x, yl, zl])
        corner_high = jnp.where(upper, got[x, yh, zh], got[x, yl, zh])
        diag[r, 2] = pull(side_low, side_high, 3 * slabs)
        diag[r, 3] = pull(corner_low, corner_high, 3 * slabs)
        edge_x = edges[r]
        for c in range(3):
            for k in range(slabs if r == 1 else 3):
                at = k if r == 0 else (base + k if r == 1 else base + slabs + k)
                out = (3 - k) if r == 0 else (0 if r == 1 else k + 1)
                s = slabs - 3 + k if r == 0 else (slabs - 1 - k if pair and r == 2 else k)
                s = c * slabs + s
                value = (source if r == 1 else (xlow if r == 0 else xhigh))[c, k] - flux[r, 0][c]
                w0[c, at, 0] = value if edge_x is None else value * edge_x
                if r == 1:
                    v0[c, k] = value
                if out <= 2:
                    a, b = ya[c, at], yb[c, at]
                    halo = jnp.concatenate([jnp.where(even, a, b), jnp.where(even, b, a)], axis=0)
                    halo = halo - flux[r, 1][c]
                    w0[c, at, 1] = halo * (mask_y if edge_x is None else mask_y * edge_x)
                    value = pull(side_low, side_high, s)
                    w0[c, at, 2] = value * (mask_z if edge_x is None else mask_z * edge_x)
                if out <= 1:
                    value = pull(corner_low, corner_high, s)
                    w0[c, at, 3] = value * (masks[3] if edge_x is None else masks[3] * edge_x)
    for key in diag:
        diag[key] = diag[key] + (6.0 - SHIFT)

    first_row, last_row = row == 0, row == 7
    first_lane, last_lane = lane == 0, lane == 127
    acc = [jnp.zeros((8, 128), jnp.float32) for _ in range(6)]
    levels = (w0, w1, w2, None)
    results = (v0, v1, v2, v3)
    for level in (1, 2, 3):
        src, dst = levels[level - 1], levels[level]
        reach = 3 - level
        for c in range(3):
            for at in range(max(base - reach, 0), base + slabs + reach):
                out = max(base - at, at - base - slabs + 1, 0)
                r = 0 if at < base else (1 if at < base + slabs else 2)
                depth = reach - out
                want = (0,) if depth == 0 else ((0, 1, 2) if depth == 1 else (0, 1, 2, 3))
                have = (0, 1, 2) if depth == 0 else (0, 1, 2, 3)
                v = {t: src[c, at, t] for t in have}
                left = {t: pltpu.roll(v[t], 127, 1) for t in have if t in (0, 2) or depth > 0}
                right = {t: pltpu.roll(v[t], 1, 1) for t in have if t in (0, 2) or depth > 0}
                down = {t: pltpu.roll(v[t], 7, 0) for t in have if t in (0, 1) or depth > 0}
                over = {t: pltpu.roll(v[t], 1, 0) for t in have if t in (0, 1) or depth > 0}
                edge_x = edges[r]
                for t in want:
                    zp = jnp.where(last_lane, left[t ^ 2], left[t])
                    zm = jnp.where(first_lane, right[t ^ 2], right[t])
                    yp = jnp.where(last_row, down[t ^ 1], down[t])
                    ym = jnp.where(first_row, over[t ^ 1], over[t])
                    beside = src[c, at + 1, t] + (zp + zm) + (yp + ym)
                    if at > 0:
                        beside = beside + src[c, at - 1, t]
                    value = diag[r, t] * v[t] - beside
                    if masks[t] is not None:
                        value = value * masks[t]
                    if edge_x is not None:
                        value = value * edge_x
                    if dst is not None:
                        dst[c, at, t] = value
                    if t == 0 and r == 1:
                        results[level][c, at - base] = value
                        acc[2 * level - 1] = acc[2 * level - 1] + v[0] * value
                        if level < 3:
                            acc[2 * level] = acc[2 * level] + value * value
                        if level == 1:
                            acc[0] = acc[0] + v[0] * v[0]
    line = jnp.zeros((1, 128), jnp.float32)
    slot = lax.broadcasted_iota(jnp.int32, (1, 128), 1)
    for k in range(6):
        sums = jnp.sum(jnp.sum(acc[k], axis=0, keepdims=True), axis=1, keepdims=True)
        line = jnp.where(slot == k, sums, line)
    moments[...] = jnp.broadcast_to(line[None], moments.shape)


def combine_kernel(pair, parts, v0, v1, v2, v3, step_out, residual_out):
    total = jnp.sum(parts[...], axis=0)
    nu = [total[:, k : k + 1] for k in range(6)]

    def gram(a, b):
        result = None
        for i, ai in enumerate(a):
            for j, bj in enumerate(b):
                term = ai * bj * nu[i + j]
                result = term if result is None else result + term
        return result

    def added(a, b):
        size = max(len(a), len(b))
        return [a[k] if k >= len(b) else (b[k] if k >= len(a) else a[k] + b[k]) for k in range(size)]

    unit = jnp.ones((1, 1), jnp.float32)
    direction, residual, newton = [unit], [unit], []
    norm = nu[0]
    for iteration in range(ITERS):
        image = added([SHIFT * d for d in direction], [0.0 * unit] + direction)
        alpha = norm / gram(direction, image)
        newton = added(newton, [alpha * d for d in direction])
        residual = added(residual, [-alpha * g for g in image])
        if iteration + 1 < ITERS:
            following = gram(residual, residual)
            ratio = following / norm
            direction = added(residual, [ratio * d for d in direction])
            norm = following
    wide = lambda a: jnp.broadcast_to(a, (8, 128))
    newton = [wide(a) for a in newton]
    residual = [wide(a) for a in residual]
    for c in range(v0.shape[0]):
        for x in range(v0.shape[1]):
            a, b, d = v0[c, x], v1[c, x], v2[c, x]
            to = jnp.where(lax.axis_index("gx") == 0, x, v0.shape[1] - 1 - x) if pair else x
            step_out[c, to] = newton[0] * a + newton[1] * b + newton[2] * d
            residual_out[c, to] = residual[0] * a + residual[1] * b + residual[2] * d + residual[3] * v3[c, x]


def call(body, outs, ins, scratch=(), last=False, raw=False):
    vmem = pl.BlockSpec(memory_space=pltpu.VMEM)
    shape = jax.ShapeDtypeStruct if last else pltpu.VMEM
    return pl.pallas_call(
        body,
        out_shape=tuple(shape(s, d) for s, d in outs),
        in_specs=[pl.BlockSpec(memory_space=pltpu.HBM) if raw else vmem] * len(ins),
        out_specs=tuple(vmem for _ in outs),
        scratch_shapes=list(scratch),
        compiler_params=pltpu.CompilerParams(vmem_limit_bytes=GRANT),
    )(*(pltpu.with_memory_space_constraint(x, pltpu.HBM if raw else pltpu.VMEM) for x in ins))


def ladder(axis):
    count = lax.axis_size(axis)
    forward = [(i, i + 1) for i in range(count - 1)]
    return forward, [(b, a) for a, b in forward]


def pairs_from(first, count):
    couples = [(i, i + 1) for i in range(first, count - 1, 2)]
    return couples + [(b, a) for a, b in couples]


def from_both(low_face, high_face, axis):
    forward, backward = ladder(axis)
    up = lax.ppermute(high_face, axis, forward)
    down = lax.ppermute(low_face, axis, backward)
    return up, down


def whole_step(source, contrast, point_field, point_class, cell_kind, inverse_blocks):
    f32, bf16 = jnp.float32, jnp.bfloat16
    rows = contrast.shape[0]
    counts = tuple(lax.axis_size(a) for a in AXES)
    nx, ny, nz = counts
    devices = nx * ny * nz
    slabs = source.shape[1]
    gx = lax.axis_index("gx")
    dense = devices <= DENSE
    pair = nx == 2
    library = inverse_blocks.transpose(0, 2, 3, 1, 4)
    field = (source.shape, f32)
    if pair:
        swap = [(0, 1), (1, 0)]
        other = lax.ppermute(library, "gx", swap)
        face = jnp.where(gx == 0, source[:, slabs - 3 :][:, ::-1], source[:, :3])
        face = lax.ppermute(face, "gx", swap)
    else:
        other = lax.all_gather(library, "gx", axis=0, tiled=True)
    count = TYPES * nx
    hartley, spectrum, columns, pick, contrast, source, library = call(
        functools.partial(spectrum_kernel, pair, count),
        [((VOX, VOX), bf16), ((3 * rows, VOX), f32), ((rows, 8), f32), ((rows, 2 * count), bf16),
         (contrast.shape, bf16), field, (library.shape, f32)],
        (contrast, point_field, point_class.reshape(1, rows), cell_kind.reshape(1, rows), source, library),
        [pltpu.VMEM((3 * rows, VOX), bf16), pltpu.VMEM((3, rows), bf16), pltpu.VMEM((1, rows), jnp.int32),
         pltpu.VMEM((1, rows), jnp.int32), pltpu.VMEM(*field), pltpu.SemaphoreType.DMA((6,))],
        raw=True,
    )
    if pair:
        xlow = xhigh = face
        longer = jnp.concatenate([source, face[:, :2]], axis=1)
    else:
        xlow, xhigh = from_both(source[:, :3], source[:, slabs - 3 :], "gx")
        longer = jnp.concatenate([xlow, source, xhigh], axis=1)
    even = lax.axis_index("gy") % 2 == 0
    low_rows, high_rows = longer[:, :, :4], longer[:, :, 4:]
    yb = lax.ppermute(jnp.where(even, low_rows, high_rows), "gy", pairs_from(1, ny))
    ya = lax.ppermute(jnp.where(even, high_rows, low_rows), "gy", pairs_from(0, ny))
    tiles, bundle = call(
        solve_kernel,
        [((4, 8, 128), f32), ((nx * ny if dense else 1, nz, 8, 128), f32)],
        (contrast, columns, spectrum, hartley, pick, library if pair else other, other, source),
        [pltpu.VMEM((9, rows, VOX), f32), pltpu.VMEM((3 * rows, VOX), bf16), pltpu.VMEM((3 * rows, VOX), f32)],
    )
    if dense:
        got = lax.all_to_all(bundle.reshape(devices, 8, 128), AXES, 0, 0).reshape(nx, ny, nz, 8, 128)
    else:
        below, above = from_both(bundle[0], bundle[0], "gx")
        trio = jnp.stack([below, bundle[0], above], axis=1)
        trio = jnp.broadcast_to(trio[None], (ny,) + trio.shape).reshape(ny * nz, 3, 8, 128)
        got = lax.all_to_all(trio, ("gy", "gz"), 0, 0).reshape(ny, nz, 3, 8, 128).transpose(2, 0, 1, 3, 4)
    v0, v1, v2, v3, moments = call(
        functools.partial(moment_kernel, dense, counts),
        [field, field, field, field, ((devices if dense else 1, 1, 128), f32)],
        (tiles, got, source, xlow, xhigh, ya, yb),
        [pltpu.VMEM((3, slabs + (3 if pair else 6), 4, 8, 128), f32) for _ in range(3)],
    )
    if dense:
        parts = lax.all_to_all(moments, AXES, 0, 0)
    else:
        parts = lax.psum(moments, AXES)
    return call(functools.partial(combine_kernel, pair), [field, field], (parts, v0, v1, v2, v3), last=True)


def solution(mesh):
    placed = (
        P(None, "gx", "gy", "gz"),
        P(("gx", "gy", "gz"), None),
        P(None, ("gx", "gy", "gz")),
        P(("gx", "gy", "gz"), None),
        P(("gx", "gy", "gz")),
        P("gx", None, None, None, None),
    )
    return jax.shard_map(
        whole_step,
        mesh=mesh,
        in_specs=placed,
        out_specs=(P(None, "gx", "gy", "gz"), P(None, "gx", "gy", "gz")),
        check_vma=False,
    )
```

```python
import functools
import math

import jax
import jax.numpy as jnp
from jax import lax
from jax.experimental import pallas as pl
from jax.experimental.pallas import tpu as pltpu
from jax.sharding import PartitionSpec as P


CELL = 8
VOX = 512
TYPES = 4
ZP = 8
ITERS = 3
AXES = ("gx", "gy", "gz")
DENSE = 64
SHIFT = 8.0
GRANT = 16 * 1024 * 1024

kerr_scale = 0.1


def where_am_i():
    return tuple(lax.axis_index(a) for a in AXES)


def spectrum_kernel(pair, count, contrast_in, field_in, class_in, kind_in, source_in, library_in,
                    hartley, spectrum, columns, pick, contrast, source, library, send_a, send_b,
                    polar, field, classes, kinds, plain_source, sems):
    rows = contrast.shape[0]
    slabs = source.shape[1]
    gx = lax.axis_index("gx")
    moves = [(field_in, field), (class_in, classes), (kind_in, kinds), (contrast_in, contrast),
             (source_in, plain_source)]
    if pair:
        moves.append((library_in, library))
    moves = [pltpu.make_async_copy(a, b, sems.at[k]) for k, (a, b) in enumerate(moves)]
    for move in moves:
        move.start()
    step = CELL * CELL
    inner = lax.broadcasted_iota(jnp.int32, (step, VOX), 0)
    voxel = lax.broadcasted_iota(jnp.int32, (step, VOX), 1)
    phase = (inner // CELL) * (voxel // CELL % CELL) + (inner % CELL) * (voxel % CELL)
    outer = voxel // step
    plain = 1.0 / math.sqrt(VOX)
    peak = math.sqrt(2.0) / math.sqrt(VOX)
    for block in range(VOX // step):
        turn = (phase + block * outer) & (CELL - 1)
        quarter = turn & 3
        size = jnp.where(quarter == 1, peak, jnp.where(quarter == 3, 0.0, plain))
        value = jnp.where(turn >= 4, -size, size)
        hartley[block * step : (block + 1) * step, :] = value.astype(jnp.bfloat16)
    for move in moves[:3]:
        move.wait()
    fields = field[...].astype(jnp.float32)
    fields = jnp.concatenate([fields, jnp.zeros((5, rows), jnp.float32)], axis=0)
    columns[...] = fields.T
    keys = jnp.where(classes[...] == gx, 0, 1) if pair else classes[...]
    keys = keys * TYPES + kinds[...]
    named = (lax.broadcasted_iota(jnp.int32, (count, rows), 0) == keys).astype(jnp.float32)
    named = jnp.concatenate([named, named], axis=0)
    pick[...] = named.T.astype(jnp.bfloat16)
    moves[3].wait()
    for j in range(3):
        e = columns[:, j : j + 1]
        m = contrast[:, j * VOX : (j + 1) * VOX].astype(jnp.float32)
        polar[j * rows : (j + 1) * rows, :] = (m * e).astype(jnp.bfloat16)
    spectrum[...] = jnp.dot(polar[...], hartley[...], preferred_element_type=jnp.float32)
    for move in moves[4:]:
        move.wait()
    even = lax.axis_index("gy") % 2 == 0
    for p in range(slabs):
        x = jnp.where(gx == 0, p, slabs - 1 - p) if pair else p
        for c in range(3):
            value = plain_source[c, x]
            source[c, p] = value
            send_a[c, p] = jnp.where(even, value[4:], value[:4])
            send_b[c, p] = jnp.where(even, value[:4], value[4:])


def solve_kernel(contrast, columns, spectrum, hartley, pick, library, other, source, tiles, bundle,
                 mixing, stacked, product):
    rows = contrast.shape[0]
    zb = rows // 8
    _, _, gz = where_am_i()
    for ij in range(9):
        i, j = ij // 3, ij % 3
        parts = [library[c, i, j] for c in range(library.shape[0])]
        if pick.shape[1] > 2 * TYPES * library.shape[0]:
            parts = parts + [other[c, i, j] for c in range(other.shape[0])]
        table = jnp.concatenate(parts, axis=0)
        high = table.astype(jnp.bfloat16).astype(jnp.float32)
        both = jnp.concatenate([high, table - high], axis=0).astype(jnp.bfloat16)
        mixing[ij] = jnp.dot(pick[...], both, preferred_element_type=jnp.float32)

    def mix(from_ref):
        for c in range(rows // 16):
            at = slice(c * 16, (c + 1) * 16)
            held = [from_ref[j * rows + c * 16 : j * rows + (c + 1) * 16, :] for j in range(3)]
            for i in range(3):
                total = mixing[3 * i, at, :] * held[0]
                total = total + mixing[3 * i + 1, at, :] * held[1]
                total = total + mixing[3 * i + 2, at, :] * held[2]
                stacked[i * rows + c * 16 : i * rows + (c + 1) * 16, :] = total.astype(jnp.bfloat16)

    mix(spectrum)
    product[...] = jnp.dot(stacked[...], hartley[...], preferred_element_type=jnp.float32)
    for c in range(rows // 16):
        for j in range(3):
            at = slice(j * rows + c * 16, j * rows + (c + 1) * 16)
            m = contrast[c * 16 : (c + 1) * 16, j * VOX : (j + 1) * VOX].astype(jnp.float32)
            local = columns[c * 16 : (c + 1) * 16, j : j + 1] - product[at, :]
            stacked[at, :] = (m * local * (1.0 + kerr_scale * local * local)).astype(jnp.bfloat16)
    product[...] = jnp.dot(stacked[...], hartley[...], preferred_element_type=jnp.float32)
    mix(product)
    product[...] = jnp.dot(stacked[...], hartley[...], preferred_element_type=jnp.float32)

    depth = lax.broadcasted_iota(jnp.int32, (zb, 128), 0)
    lane = lax.broadcasted_iota(jnp.int32, (zb, 128), 1)
    spread = lane // ZP == depth
    packed = lane % zb == depth
    group = lane // zb
    for c in range(rows // 16):
        means = []
        stiff = jnp.zeros((16, VOX), jnp.float32)
        for j in range(3):
            at = slice(j * rows + c * 16, j * rows + (c + 1) * 16)
            m = contrast[c * 16 : (c + 1) * 16, j * VOX : (j + 1) * VOX].astype(jnp.float32)
            final = columns[c * 16 : (c + 1) * 16, j : j + 1] - product[at, :]
            means.append(jnp.sum((1.0 + m) * final, axis=1, keepdims=True) * (1.0 / VOX))
            stiff = stiff + m * final * final
        means.append(0.5 + jnp.sum(stiff, axis=1, keepdims=True) * (1.0 / (3 * VOX)))
        compact = jnp.zeros((zb, 128), jnp.float32)
        for t in range(4):
            wide = jnp.broadcast_to(means[t], (zb, 128))
            tiles[t, c : c + 1, :] = jnp.sum(jnp.where(spread, wide, 0.0), axis=0, keepdims=True)
            compact = compact + jnp.where(packed & (group == t), wide, 0.0)
        product[c : c + 1, 0:128] = jnp.sum(compact, axis=0, keepdims=True)
    compact = product[0:8, 0:128]

    place = lax.broadcasted_iota(jnp.int32, (8, 128), 1)
    low = jnp.zeros((8, 128), jnp.float32)
    high = jnp.zeros((8, 128), jnp.float32)
    slabs = source.shape[1]
    for s in range(3 * slabs + 1):
        if s < 3 * slabs:
            value = source[s // slabs, s % slabs] - tiles[s // slabs]
        else:
            value = tiles[3]
        here = (place >= 3 * s) & (place < 3 * s + 3)
        low = jnp.where(here, pltpu.roll(value, (3 * s) % 128, 1) if s else value, low)
        high = jnp.where(here, pltpu.roll(value, (3 * s + 3) % 128, 1), high)
    for d in range(bundle.shape[1]):
        zero = jnp.zeros((8, 128), jnp.float32)
        tile = jnp.where(gz == d, compact, jnp.where(gz + 1 == d, high, jnp.where(gz - 1 == d, low, zero)))
        for x in range(bundle.shape[0]):
            bundle[x, d] = tile


def moment_kernel(dense, counts, tiles, got, source, ytile, xlow, xhigh, v0, v1, v2, v3, moments, w0, w1, w2):
    slabs = source.shape[1]
    gx, gy, gz = where_am_i()
    nx, ny, nz = counts
    pair = nx == 2
    base = 0 if pair else 3
    row = lax.broadcasted_iota(jnp.int32, (8, 128), 0)
    lane = lax.broadcasted_iota(jnp.int32, (8, 128), 1)
    has_xl, has_xh = gx > 0, gx < nx - 1
    has_yl, has_yh = gy > 0, gy < ny - 1
    has_zl, has_zh = gz > 0, gz < nz - 1
    one = lambda flag: jnp.where(flag, 1.0, 0.0)
    mask_y = jnp.where(row < 4, one(has_yh), one(has_yl))
    mask_z = jnp.where(lane < 64, one(has_zh), one(has_zl))
    masks = (None, mask_y, mask_z, mask_y * mask_z)
    yl, yh = jnp.maximum(gy - 1, 0), jnp.minimum(gy + 1, ny - 1)
    zl, zh = jnp.maximum(gz - 1, 0), jnp.minimum(gz + 1, nz - 1)
    if pair:
        regions = (None, gx, 1 - gx)
    elif dense:
        regions = (jnp.maximum(gx - 1, 0), gx, jnp.minimum(gx + 1, nx - 1))
    else:
        regions = (0, 1, 2)
    upper = row < 4
    spread = lane // ZP
    zb = 128 // ZP

    def unfold(tile, t):
        return jnp.take_along_axis(tile, spread + t * zb, axis=1)

    def pull(low_tile, high_tile, s):
        a = pltpu.roll(high_tile, (-3 * s) % 128, 1) if s else high_tile
        b = pltpu.roll(low_tile, (125 - 3 * s) % 128, 1)
        return jnp.where(lane < 64, a, b)

    diag = {}
    flux = {}
    edges = {1: None, 2: None} if pair else {0: one(has_xl), 1: None, 2: one(has_xh)}
    for r in edges:
        x = regions[r]
        rowtile = jnp.where(upper, got[x, yh, gz], got[x, yl, gz])
        flux[r, 1] = [unfold(rowtile, t) for t in range(3)]
        diag[r, 1] = unfold(rowtile, 3)
        if r == 1:
            flux[r, 0] = [tiles[t] for t in range(3)]
            diag[r, 0] = tiles[3]
        else:
            flux[r, 0] = [unfold(got[x, gy, gz], t) for t in range(3)]
            diag[r, 0] = unfold(got[x, gy, gz], 3)
        side_low, side_high = got[x, gy, zl], got[x, gy, zh]
        corner_low = jnp.where(upper, got[x, yh, zl], got[x, yl, zl])
        corner_high = jnp.where(upper, got[x, yh, zh], got[x, yl, zh])
        diag[r, 2] = pull(side_low, side_high, 3 * slabs)
        diag[r, 3] = pull(corner_low, corner_high, 3 * slabs)
        edge_x = edges[r]
        for c in range(3):
            for k in range(slabs if r == 1 else 3):
                at = base - 1 - k if r == 0 else (base + k if r == 1 else base + slabs + k)
                out = 0 if r == 1 else k + 1
                s = k if r == 1 or (r == 2 and not pair) else slabs - 1 - k
                s = c * slabs + s
                beyond = xlow if r == 0 else xhigh
                value = (source if r == 1 else beyond)[c, k] - flux[r, 0][c]
                w0[c, at, 0] = value if edge_x is None else value * edge_x
                if r == 1:
                    v0[c, k] = value
                if out <= 2:
                    halo = (ytile[c, k] if r == 1 else beyond[c, 3 + k]) - flux[r, 1][c]
                    w0[c, at, 1] = halo * (mask_y if edge_x is None else mask_y * edge_x)
                    value = pull(side_low, side_high, s)
                    w0[c, at, 2] = value * (mask_z if edge_x is None else mask_z * edge_x)
                if out <= 1:
                    value = pull(corner_low, corner_high, s)
                    w0[c, at, 3] = value * (masks[3] if edge_x is None else masks[3] * edge_x)
    for key in diag:
        diag[key] = diag[key] + (6.0 - SHIFT)

    first_row, last_row = row == 0, row == 7
    first_lane, last_lane = lane == 0, lane == 127
    acc = [jnp.zeros((8, 128), jnp.float32) for _ in range(6)]
    levels = (w0, w1, w2, None)
    results = (v0, v1, v2, v3)
    for level in (1, 2, 3):
        src, dst = levels[level - 1], levels[level]
        reach = 3 - level
        for c in range(3):
            for at in range(max(base - reach, 0), base + slabs + reach):
                out = max(base - at, at - base - slabs + 1, 0)
                r = 0 if at < base else (1 if at < base + slabs else 2)
                depth = reach - out
                want = (0,) if depth == 0 else ((0, 1, 2) if depth == 1 else (0, 1, 2, 3))
                have = (0, 1, 2) if depth == 0 else (0, 1, 2, 3)
                v = {t: src[c, at, t] for t in have}
                left = {t: pltpu.roll(v[t], 127, 1) for t in have if t in (0, 2) or depth > 0}
                right = {t: pltpu.roll(v[t], 1, 1) for t in have if t in (0, 2) or depth > 0}
                down = {t: pltpu.roll(v[t], 7, 0) for t in have if t in (0, 1) or depth > 0}
                over = {t: pltpu.roll(v[t], 1, 0) for t in have if t in (0, 1) or depth > 0}
                edge_x = edges[r]
                for t in want:
                    zp = jnp.where(last_lane, left[t ^ 2], left[t])
                    zm = jnp.where(first_lane, right[t ^ 2], right[t])
                    yp = jnp.where(last_row, down[t ^ 1], down[t])
                    ym = jnp.where(first_row, over[t ^ 1], over[t])
                    beside = src[c, at + 1, t] + (zp + zm) + (yp + ym)
                    if at > 0:
                        beside = beside + src[c, at - 1, t]
                    value = diag[r, t] * v[t] - beside
                    if masks[t] is not None:
                        value = value * masks[t]
                    if edge_x is not None:
                        value = value * edge_x
                    if dst is not None:
                        dst[c, at, t] = value
                    if t == 0 and r == 1:
                        results[level][c, at - base] = value
                        acc[2 * level - 1] = acc[2 * level - 1] + v[0] * value
                        if level < 3:
                            acc[2 * level] = acc[2 * level] + value * value
                        if level == 1:
                            acc[0] = acc[0] + v[0] * v[0]
    line = jnp.zeros((1, 128), jnp.float32)
    slot = lax.broadcasted_iota(jnp.int32, (1, 128), 1)
    for k in range(6):
        sums = jnp.sum(jnp.sum(acc[k], axis=0, keepdims=True), axis=1, keepdims=True)
        line = jnp.where(slot == k, sums, line)
    moments[...] = jnp.broadcast_to(line[None], moments.shape)


def combine_kernel(pair, parts, v0, v1, v2, v3, step_out, residual_out):
    total = jnp.sum(parts[...], axis=0)
    nu = [total[:, k : k + 1] for k in range(6)]

    def gram(a, b):
        result = None
        for i, ai in enumerate(a):
            for j, bj in enumerate(b):
                term = ai * bj * nu[i + j]
                result = term if result is None else result + term
        return result

    def added(a, b):
        size = max(len(a), len(b))
        return [a[k] if k >= len(b) else (b[k] if k >= len(a) else a[k] + b[k]) for k in range(size)]

    unit = jnp.ones((1, 1), jnp.float32)
    direction, residual, newton = [unit], [unit], []
    norm = nu[0]
    for iteration in range(ITERS):
        image = added([SHIFT * d for d in direction], [0.0 * unit] + direction)
        alpha = norm / gram(direction, image)
        newton = added(newton, [alpha * d for d in direction])
        residual = added(residual, [-alpha * g for g in image])
        if iteration + 1 < ITERS:
            following = gram(residual, residual)
            ratio = following / norm
            direction = added(residual, [ratio * d for d in direction])
            norm = following
    wide = lambda a: jnp.broadcast_to(a, (8, 128))
    newton = [wide(a) for a in newton]
    residual = [wide(a) for a in residual]
    for c in range(v0.shape[0]):
        for x in range(v0.shape[1]):
            a, b, d = v0[c, x], v1[c, x], v2[c, x]
            to = jnp.where(lax.axis_index("gx") == 0, x, v0.shape[1] - 1 - x) if pair else x
            step_out[c, to] = newton[0] * a + newton[1] * b + newton[2] * d
            residual_out[c, to] = residual[0] * a + residual[1] * b + residual[2] * d + residual[3] * v3[c, x]


def call(body, outs, ins, scratch=(), last=False, raw=False):
    vmem = pl.BlockSpec(memory_space=pltpu.VMEM)
    shape = jax.ShapeDtypeStruct if last else pltpu.VMEM
    return pl.pallas_call(
        body,
        out_shape=tuple(shape(s, d) for s, d in outs),
        in_specs=[pl.BlockSpec(memory_space=pltpu.HBM) if raw else vmem] * len(ins),
        out_specs=tuple(vmem for _ in outs),
        scratch_shapes=list(scratch),
        compiler_params=pltpu.CompilerParams(vmem_limit_bytes=GRANT),
    )(*(pltpu.with_memory_space_constraint(x, pltpu.HBM if raw else pltpu.VMEM) for x in ins))


def ladder(axis):
    count = lax.axis_size(axis)
    forward = [(i, i + 1) for i in range(count - 1)]
    return forward, [(b, a) for a, b in forward]


def pairs_from(first, count):
    couples = [(i, i + 1) for i in range(first, count - 1, 2)]
    return couples + [(b, a) for a, b in couples]


def from_both(low_face, high_face, axis):
    forward, backward = ladder(axis)
    up = lax.ppermute(high_face, axis, forward)
    down = lax.ppermute(low_face, axis, backward)
    return up, down


def whole_step(source, contrast, point_field, point_class, cell_kind, inverse_blocks):
    f32, bf16 = jnp.float32, jnp.bfloat16
    rows = contrast.shape[0]
    counts = tuple(lax.axis_size(a) for a in AXES)
    nx, ny, nz = counts
    devices = nx * ny * nz
    slabs = source.shape[1]
    dense = devices <= DENSE
    pair = nx == 2
    library = inverse_blocks.transpose(0, 2, 3, 1, 4)
    field = (source.shape, f32)
    if pair:
        swap = [(0, 1), (1, 0)]
        other = lax.ppermute(library, "gx", swap)
    else:
        other = lax.all_gather(library, "gx", axis=0, tiled=True)
    count = TYPES * nx
    hartley, spectrum, columns, pick, contrast, source, library, send_a, send_b = call(
        functools.partial(spectrum_kernel, pair, count),
        [((VOX, VOX), bf16), ((3 * rows, VOX), f32), ((rows, 8), f32), ((rows, 2 * count), bf16),
         (contrast.shape, bf16), field, (library.shape, f32), ((3, slabs, 4, 128), f32), ((3, slabs, 4, 128), f32)],
        (contrast, point_field, point_class.reshape(1, rows), cell_kind.reshape(1, rows), source, library),
        [pltpu.VMEM((3 * rows, VOX), bf16), pltpu.VMEM((3, rows), bf16), pltpu.VMEM((1, rows), jnp.int32),
         pltpu.VMEM((1, rows), jnp.int32), pltpu.VMEM(*field), pltpu.SemaphoreType.DMA((6,))],
        raw=True,
    )
    yb = lax.ppermute(send_b, "gy", pairs_from(1, ny))
    ya = lax.ppermute(send_a, "gy", pairs_from(0, ny))
    tiles, bundle = call(
        solve_kernel,
        [((4, 8, 128), f32), ((nx * ny if dense else 1, nz, 8, 128), f32)],
        (contrast, columns, spectrum, hartley, pick, library if pair else other, other, source),
        [pltpu.VMEM((9, rows, VOX), f32), pltpu.VMEM((3 * rows, VOX), bf16), pltpu.VMEM((3 * rows, VOX), f32)],
    )
    if dense:
        got = lax.all_to_all(bundle.reshape(devices, 8, 128), AXES, 0, 0).reshape(nx, ny, nz, 8, 128)
    else:
        below, above = from_both(bundle[0], bundle[0], "gx")
        trio = jnp.stack([below, bundle[0], above], axis=1)
        trio = jnp.broadcast_to(trio[None], (ny,) + trio.shape).reshape(ny * nz, 3, 8, 128)
        got = lax.all_to_all(trio, ("gy", "gz"), 0, 0).reshape(ny, nz, 3, 8, 128).transpose(2, 0, 1, 3, 4)
    even = lax.axis_index("gy") % 2 == 0
    ytile = jnp.concatenate([jnp.where(even, ya, yb), jnp.where(even, yb, ya)], axis=2)
    high = jnp.concatenate([source[:, : slabs - 4 : -1], ytile[:, : slabs - 3 : -1]], axis=1)
    if pair:
        xlow = xhigh = lax.ppermute(high, "gx", swap)
    else:
        xlow, xhigh = from_both(jnp.concatenate([source[:, :3], ytile[:, :2]], axis=1), high, "gx")
    v0, v1, v2, v3, moments = call(
        functools.partial(moment_kernel, dense, counts),
        [field, field, field, field, ((devices if dense else 1, 1, 128), f32)],
        (tiles, got, source, ytile, xlow, xhigh),
        [pltpu.VMEM((3, slabs + (3 if pair else 6), 4, 8, 128), f32) for _ in range(3)],
    )
    if dense:
        parts = lax.all_to_all(moments, AXES, 0, 0)
    else:
        parts = lax.psum(moments, AXES)
    return call(functools.partial(combine_kernel, pair), [field, field], (parts, v0, v1, v2, v3), last=True)


def solution(mesh):
    placed = (
        P(None, "gx", "gy", "gz"),
        P(("gx", "gy", "gz"), None),
        P(None, ("gx", "gy", "gz")),
        P(("gx", "gy", "gz"), None),
        P(("gx", "gy", "gz")),
        P("gx", None, None, None, None),
    )
    return jax.shard_map(
        whole_step,
        mesh=mesh,
        in_specs=placed,
        out_specs=(P(None, "gx", "gy", "gz"), P(None, "gx", "gy", "gz")),
        check_vma=False,
    )
```

```python
import functools
import math

import jax
import jax.numpy as jnp
from jax import lax
from jax.experimental import pallas as pl
from jax.experimental.pallas import tpu as pltpu
from jax.sharding import PartitionSpec as P


CELL = 8
VOX = 512
TYPES = 4
ZP = 8
ITERS = 3
AXES = ("gx", "gy", "gz")
DENSE = 64
SHIFT = 8.0
GRANT = 16 * 1024 * 1024

kerr_scale = 0.1


def where_am_i():
    return tuple(lax.axis_index(a) for a in AXES)


def spectrum_kernel(pair, count, contrast_in, field_in, class_in, kind_in, source_in, library_in,
                    hartley, spectrum, columns, pick, weights, source, library, send_a, send_b,
                    polar, field, classes, kinds, plain_source, contrast, sems):
    rows = contrast.shape[0]
    slabs = source.shape[1]
    gx = lax.axis_index("gx")
    moves = [(field_in, field), (class_in, classes), (kind_in, kinds), (contrast_in, contrast),
             (source_in, plain_source)]
    if pair:
        moves.append((library_in, library))
    moves = [pltpu.make_async_copy(a, b, sems.at[k]) for k, (a, b) in enumerate(moves)]
    for move in moves:
        move.start()
    step = CELL * CELL
    inner = lax.broadcasted_iota(jnp.int32, (step, VOX), 0)
    voxel = lax.broadcasted_iota(jnp.int32, (step, VOX), 1)
    phase = (inner // CELL) * (voxel // CELL % CELL) + (inner % CELL) * (voxel % CELL)
    outer = voxel // step
    plain = 1.0 / math.sqrt(VOX)
    peak = math.sqrt(2.0) / math.sqrt(VOX)
    for block in range(VOX // step):
        turn = (phase + block * outer) & (CELL - 1)
        quarter = turn & 3
        size = jnp.where(quarter == 1, peak, jnp.where(quarter == 3, 0.0, plain))
        value = jnp.where(turn >= 4, -size, size)
        hartley[block * step : (block + 1) * step, :] = value.astype(jnp.bfloat16)
    for move in moves[:3]:
        move.wait()
    fields = field[...].astype(jnp.float32)
    fields = jnp.concatenate([fields, jnp.zeros((5, rows), jnp.float32)], axis=0)
    columns[...] = fields.T
    keys = jnp.where(classes[...] == gx, 0, 1) if pair else classes[...]
    keys = keys * TYPES + kinds[...]
    named = (lax.broadcasted_iota(jnp.int32, (count, rows), 0) == keys).astype(jnp.float32)
    named = jnp.concatenate([named, named], axis=0)
    pick[...] = named.T.astype(jnp.bfloat16)
    moves[3].wait()
    for j in range(3):
        e = columns[:, j : j + 1]
        m = contrast[:, j * VOX : (j + 1) * VOX].astype(jnp.float32)
        weights[:, j * VOX : (j + 1) * VOX] = m
        polar[j * rows : (j + 1) * rows, :] = (m * e).astype(jnp.bfloat16)
    spectrum[...] = jnp.dot(polar[...], hartley[...], preferred_element_type=jnp.float32)
    for move in moves[4:]:
        move.wait()
    even = lax.axis_index("gy") % 2 == 0
    for p in range(slabs):
        x = jnp.where(gx == 0, p, slabs - 1 - p) if pair else p
        for c in range(3):
            value = plain_source[c, x]
            source[c, p] = value
            send_a[c, p] = jnp.where(even, value[4:], value[:4])
            send_b[c, p] = jnp.where(even, value[:4], value[4:])


def solve_kernel(weights, columns, spectrum, hartley, pick, library, other, source, tiles, bundle,
                 mixing, stacked, product):
    rows = weights.shape[0]
    zb = rows // 8
    _, _, gz = where_am_i()
    for ij in range(9):
        i, j = ij // 3, ij % 3
        parts = [library[c, i, j] for c in range(library.shape[0])]
        if pick.shape[1] > 2 * TYPES * library.shape[0]:
            parts = parts + [other[c, i, j] for c in range(other.shape[0])]
        table = jnp.concatenate(parts, axis=0)
        high = table.astype(jnp.bfloat16).astype(jnp.float32)
        both = jnp.concatenate([high, table - high], axis=0).astype(jnp.bfloat16)
        mixing[ij] = jnp.dot(pick[...], both, preferred_element_type=jnp.float32)

    def mix(from_ref):
        for c in range(rows // 16):
            at = slice(c * 16, (c + 1) * 16)
            held = [from_ref[j * rows + c * 16 : j * rows + (c + 1) * 16, :] for j in range(3)]
            for i in range(3):
                total = mixing[3 * i, at, :] * held[0]
                total = total + mixing[3 * i + 1, at, :] * held[1]
                total = total + mixing[3 * i + 2, at, :] * held[2]
                stacked[i * rows + c * 16 : i * rows + (c + 1) * 16, :] = total.astype(jnp.bfloat16)

    mix(spectrum)
    product[...] = jnp.dot(stacked[...], hartley[...], preferred_element_type=jnp.float32)
    for c in range(rows // 16):
        for j in range(3):
            at = slice(j * rows + c * 16, j * rows + (c + 1) * 16)
            m = weights[c * 16 : (c + 1) * 16, j * VOX : (j + 1) * VOX]
            local = columns[c * 16 : (c + 1) * 16, j : j + 1] - product[at, :]
            stacked[at, :] = (m * local * (1.0 + kerr_scale * local * local)).astype(jnp.bfloat16)
    product[...] = jnp.dot(stacked[...], hartley[...], preferred_element_type=jnp.float32)
    mix(product)
    product[...] = jnp.dot(stacked[...], hartley[...], preferred_element_type=jnp.float32)

    depth = lax.broadcasted_iota(jnp.int32, (zb, 128), 0)
    lane = lax.broadcasted_iota(jnp.int32, (zb, 128), 1)
    spread = lane // ZP == depth
    packed = lane % zb == depth
    group = lane // zb
    for c in range(rows // 16):
        means = []
        stiff = jnp.zeros((16, VOX), jnp.float32)
        for j in range(3):
            at = slice(j * rows + c * 16, j * rows + (c + 1) * 16)
            m = weights[c * 16 : (c + 1) * 16, j * VOX : (j + 1) * VOX]
            final = columns[c * 16 : (c + 1) * 16, j : j + 1] - product[at, :]
            weighted = m * final
            means.append(jnp.sum(final + weighted, axis=1, keepdims=True) * (1.0 / VOX))
            stiff = stiff + weighted * final
        means.append(0.5 + jnp.sum(stiff, axis=1, keepdims=True) * (1.0 / (3 * VOX)))
        compact = jnp.zeros((zb, 128), jnp.float32)
        for t in range(4):
            wide = jnp.broadcast_to(means[t], (zb, 128))
            tiles[t, c : c + 1, :] = jnp.sum(jnp.where(spread, wide, 0.0), axis=0, keepdims=True)
            compact = compact + jnp.where(packed & (group == t), wide, 0.0)
        product[c : c + 1, 0:128] = jnp.sum(compact, axis=0, keepdims=True)
    compact = product[0:8, 0:128]

    place = lax.broadcasted_iota(jnp.int32, (8, 128), 1)
    low = jnp.zeros((8, 128), jnp.float32)
    high = jnp.zeros((8, 128), jnp.float32)
    slabs = source.shape[1]
    for s in range(3 * slabs + 1):
        if s < 3 * slabs:
            value = source[s // slabs, s % slabs] - tiles[s // slabs]
        else:
            value = tiles[3]
        here = (place >= 3 * s) & (place < 3 * s + 3)
        low = jnp.where(here, pltpu.roll(value, (3 * s) % 128, 1) if s else value, low)
        high = jnp.where(here, pltpu.roll(value, (3 * s + 3) % 128, 1), high)
    mirrored = jnp.minimum(place + 2 - 2 * (place % 3), 127)
    low = jnp.take_along_axis(low, mirrored, axis=1)
    high = jnp.take_along_axis(high, mirrored, axis=1)
    for d in range(bundle.shape[1]):
        zero = jnp.zeros((8, 128), jnp.float32)
        tile = jnp.where(gz == d, compact, jnp.where(gz + 1 == d, high, jnp.where(gz - 1 == d, low, zero)))
        for x in range(bundle.shape[0]):
            bundle[x, d] = tile


def moment_kernel(dense, counts, tiles, got, source, ytile, xlow, xhigh, v0, v1, v2, v3, moments, w0, w1, w2):
    slabs = source.shape[1]
    gx, gy, gz = where_am_i()
    nx, ny, nz = counts
    pair = nx == 2
    base = 0 if pair else 3
    row = lax.broadcasted_iota(jnp.int32, (8, 128), 0)
    lane = lax.broadcasted_iota(jnp.int32, (8, 128), 1)
    has_xl, has_xh = gx > 0, gx < nx - 1
    has_yl, has_yh = gy > 0, gy < ny - 1
    has_zl, has_zh = gz > 0, gz < nz - 1
    one = lambda flag: jnp.where(flag, 1.0, 0.0)
    mask_y = jnp.where(row < 4, one(has_yh), one(has_yl))
    mask_z = jnp.where(lane < 64, one(has_zl), one(has_zh))
    masks = (None, mask_y, mask_z, mask_y * mask_z)
    yl, yh = jnp.maximum(gy - 1, 0), jnp.minimum(gy + 1, ny - 1)
    zl, zh = jnp.maximum(gz - 1, 0), jnp.minimum(gz + 1, nz - 1)
    if pair:
        regions = (None, gx, 1 - gx)
    elif dense:
        regions = (jnp.maximum(gx - 1, 0), gx, jnp.minimum(gx + 1, nx - 1))
    else:
        regions = (0, 1, 2)
    upper = row < 4
    spread = lane // ZP
    zb = 128 // ZP

    def unfold(tile, t):
        return jnp.take_along_axis(tile, spread + t * zb, axis=1)

    def pull(low_tile, high_tile, s):
        a = pltpu.roll(low_tile, (-3 * s) % 128, 1) if s else low_tile
        b = pltpu.roll(high_tile, (125 - 3 * s) % 128, 1)
        return jnp.where(lane < 64, a, b)

    def put(ref, c, at, t, value):
        if t & 1:
            ref[c, at, t >> 1, 0:8, :] = value
            ref[c, at, t >> 1, 16:24, :] = value
        else:
            ref[c, at, t >> 1, 8:16, :] = value

    def take(ref, c, at, t, shift=0):
        start = (8, 9, 7)[shift] if not t & 1 else (0, 1, 15)[shift]
        return ref[c, at, t >> 1, start : start + 8, :]

    diag = {}
    flux = {}
    edges = {1: None, 2: None} if pair else {0: one(has_xl), 1: None, 2: one(has_xh)}
    for r in edges:
        x = regions[r]
        rowtile = jnp.where(upper, got[x, yh, gz], got[x, yl, gz])
        flux[r, 1] = [unfold(rowtile, t) for t in range(3)]
        diag[r, 1] = unfold(rowtile, 3)
        if r == 1:
            flux[r, 0] = [tiles[t] for t in range(3)]
            diag[r, 0] = tiles[3]
        else:
            flux[r, 0] = [unfold(got[x, gy, gz], t) for t in range(3)]
            diag[r, 0] = unfold(got[x, gy, gz], 3)
        side_low, side_high = got[x, gy, zl], got[x, gy, zh]
        corner_low = jnp.where(upper, got[x, yh, zl], got[x, yl, zl])
        corner_high = jnp.where(upper, got[x, yh, zh], got[x, yl, zh])
        diag[r, 2] = pull(side_low, side_high, 3 * slabs)
        diag[r, 3] = pull(corner_low, corner_high, 3 * slabs)
        edge_x = edges[r]
        for c in range(3):
            for k in range(slabs if r == 1 else 3):
                at = base - 1 - k if r == 0 else (base + k if r == 1 else base + slabs + k)
                out = 0 if r == 1 else k + 1
                s = k if r == 1 or (r == 2 and not pair) else slabs - 1 - k
                s = c * slabs + s
                beyond = xlow if r == 0 else xhigh
                value = (source if r == 1 else beyond)[c, k] - flux[r, 0][c]
                put(w0, c, at, 0, value if edge_x is None else value * edge_x)
                if r == 1:
                    v0[c, k] = value
                if out <= 2:
                    halo = (ytile[c, k] if r == 1 else beyond[c, 3 + k]) - flux[r, 1][c]
                    put(w0, c, at, 1, halo * (mask_y if edge_x is None else mask_y * edge_x))
                    value = pull(side_low, side_high, s)
                    put(w0, c, at, 2, value * (mask_z if edge_x is None else mask_z * edge_x))
                if out <= 1:
                    value = pull(corner_low, corner_high, s)
                    put(w0, c, at, 3, value * (masks[3] if edge_x is None else masks[3] * edge_x))
    for key in diag:
        diag[key] = diag[key] + (6.0 - SHIFT)

    first_lane, last_lane = lane == 0, lane == 127
    acc = [jnp.zeros((8, 128), jnp.float32) for _ in range(6)]
    levels = (w0, w1, w2, None)
    results = (v0, v1, v2, v3)
    for level in (1, 2, 3):
        src, dst = levels[level - 1], levels[level]
        reach = 3 - level
        for c in range(3):
            for at in range(max(base - reach, 0), base + slabs + reach):
                out = max(base - at, at - base - slabs + 1, 0)
                r = 0 if at < base else (1 if at < base + slabs else 2)
                depth = reach - out
                want = (0,) if depth == 0 else ((0, 1, 2) if depth == 1 else (0, 1, 2, 3))
                edge_x = edges[r]
                for t in want:
                    here, across = take(src, c, at, t), take(src, c, at, t ^ 2)
                    zm = jnp.where(first_lane, across, pltpu.roll(here, 1, 1))
                    zp = jnp.where(last_lane, across, pltpu.roll(here, 127, 1))
                    beside = take(src, c, at + 1, t) + (zp + zm) + (take(src, c, at, t, 1) + take(src, c, at, t, 2))
                    if at > 0:
                        beside = beside + take(src, c, at - 1, t)
                    value = diag[r, t] * here - beside
                    if masks[t] is not None:
                        value = value * masks[t]
                    if edge_x is not None:
                        value = value * edge_x
                    if dst is not None:
                        put(dst, c, at, t, value)
                    if t == 0 and r == 1:
                        results[level][c, at - base] = value
                        acc[2 * level - 1] = acc[2 * level - 1] + here * value
                        if level < 3:
                            acc[2 * level] = acc[2 * level] + value * value
                        if level == 1:
                            acc[0] = acc[0] + here * here
    line = jnp.zeros((1, 128), jnp.float32)
    slot = lax.broadcasted_iota(jnp.int32, (1, 128), 1)
    for k in range(6):
        sums = jnp.sum(jnp.sum(acc[k], axis=0, keepdims=True), axis=1, keepdims=True)
        line = jnp.where(slot == k, sums, line)
    moments[...] = jnp.broadcast_to(line[None], moments.shape)


def combine_kernel(pair, parts, v0, v1, v2, v3, step_out, residual_out):
    total = jnp.sum(parts[...], axis=0)
    nu = [total[:, k : k + 1] for k in range(6)]

    def gram(a, b):
        result = None
        for i, ai in enumerate(a):
            for j, bj in enumerate(b):
                term = ai * bj * nu[i + j]
                result = term if result is None else result + term
        return result

    def added(a, b):
        size = max(len(a), len(b))
        return [a[k] if k >= len(b) else (b[k] if k >= len(a) else a[k] + b[k]) for k in range(size)]

    unit = jnp.ones((1, 1), jnp.float32)
    direction, residual, newton = [unit], [unit], []
    norm = nu[0]
    for iteration in range(ITERS):
        image = added([SHIFT * d for d in direction], [0.0 * unit] + direction)
        alpha = norm / gram(direction, image)
        newton = added(newton, [alpha * d for d in direction])
        residual = added(residual, [-alpha * g for g in image])
        if iteration + 1 < ITERS:
            following = gram(residual, residual)
            ratio = following / norm
            direction = added(residual, [ratio * d for d in direction])
            norm = following
    wide = lambda a: jnp.broadcast_to(a, (8, 128))
    newton = [wide(a) for a in newton]
    residual = [wide(a) for a in residual]
    for c in range(v0.shape[0]):
        for x in range(v0.shape[1]):
            a, b, d = v0[c, x], v1[c, x], v2[c, x]
            to = jnp.where(lax.axis_index("gx") == 0, x, v0.shape[1] - 1 - x) if pair else x
            step_out[c, to] = newton[0] * a + newton[1] * b + newton[2] * d
            residual_out[c, to] = residual[0] * a + residual[1] * b + residual[2] * d + residual[3] * v3[c, x]


def call(body, outs, ins, scratch=(), last=False, raw=False):
    vmem = pl.BlockSpec(memory_space=pltpu.VMEM)
    shape = jax.ShapeDtypeStruct if last else pltpu.VMEM
    return pl.pallas_call(
        body,
        out_shape=tuple(shape(s, d) for s, d in outs),
        in_specs=[pl.BlockSpec(memory_space=pltpu.HBM) if raw else vmem] * len(ins),
        out_specs=tuple(vmem for _ in outs),
        scratch_shapes=list(scratch),
        compiler_params=pltpu.CompilerParams(vmem_limit_bytes=GRANT),
    )(*(pltpu.with_memory_space_constraint(x, pltpu.HBM if raw else pltpu.VMEM) for x in ins))


def ladder(axis):
    count = lax.axis_size(axis)
    forward = [(i, i + 1) for i in range(count - 1)]
    return forward, [(b, a) for a, b in forward]


def pairs_from(first, count):
    couples = [(i, i + 1) for i in range(first, count - 1, 2)]
    return couples + [(b, a) for a, b in couples]


def from_both(low_face, high_face, axis):
    forward, backward = ladder(axis)
    up = lax.ppermute(high_face, axis, forward)
    down = lax.ppermute(low_face, axis, backward)
    return up, down


def whole_step(source, contrast, point_field, point_class, cell_kind, inverse_blocks):
    f32, bf16 = jnp.float32, jnp.bfloat16
    rows = contrast.shape[0]
    counts = tuple(lax.axis_size(a) for a in AXES)
    nx, ny, nz = counts
    devices = nx * ny * nz
    slabs = source.shape[1]
    dense = devices <= DENSE
    pair = nx == 2
    library = inverse_blocks.transpose(0, 2, 3, 1, 4)
    field = (source.shape, f32)
    if pair:
        swap = [(0, 1), (1, 0)]
        other = lax.ppermute(library, "gx", swap)
    else:
        other = lax.all_gather(library, "gx", axis=0, tiled=True)
    count = TYPES * nx
    hartley, spectrum, columns, pick, weights, source, library, send_a, send_b = call(
        functools.partial(spectrum_kernel, pair, count),
        [((VOX, VOX), bf16), ((3 * rows, VOX), f32), ((rows, 8), f32), ((rows, 2 * count), bf16),
         (contrast.shape, f32), field, (library.shape, f32), ((3, slabs, 4, 128), f32), ((3, slabs, 4, 128), f32)],
        (contrast, point_field, point_class.reshape(1, rows), cell_kind.reshape(1, rows), source, library),
        [pltpu.VMEM((3 * rows, VOX), bf16), pltpu.VMEM((3, rows), bf16), pltpu.VMEM((1, rows), jnp.int32),
         pltpu.VMEM((1, rows), jnp.int32), pltpu.VMEM(*field), pltpu.VMEM(contrast.shape, bf16), pltpu.SemaphoreType.DMA((6,))],
        raw=True,
    )
    yb = lax.ppermute(send_b, "gy", pairs_from(1, ny))
    ya = lax.ppermute(send_a, "gy", pairs_from(0, ny))
    tiles, bundle = call(
        solve_kernel,
        [((4, 8, 128), f32), ((nx * ny if dense else 1, nz, 8, 128), f32)],
        (weights, columns, spectrum, hartley, pick, library if pair else other, other, source),
        [pltpu.VMEM((9, rows, VOX), f32), pltpu.VMEM((3 * rows, VOX), bf16), pltpu.VMEM((3 * rows, VOX), f32)],
    )
    if dense:
        got = lax.all_to_all(bundle.reshape(devices, 8, 128), AXES, 0, 0).reshape(nx, ny, nz, 8, 128)
    else:
        below, above = from_both(bundle[0], bundle[0], "gx")
        trio = jnp.stack([below, bundle[0], above], axis=1)
        trio = jnp.broadcast_to(trio[None], (ny,) + trio.shape).reshape(ny * nz, 3, 8, 128)
        got = lax.all_to_all(trio, ("gy", "gz"), 0, 0).reshape(ny, nz, 3, 8, 128).transpose(2, 0, 1, 3, 4)
    even = lax.axis_index("gy") % 2 == 0
    ytile = jnp.concatenate([jnp.where(even, ya, yb), jnp.where(even, yb, ya)], axis=2)
    high = jnp.concatenate([source[:, : slabs - 4 : -1], ytile[:, : slabs - 3 : -1]], axis=1)
    if pair:
        xlow = xhigh = lax.ppermute(high, "gx", swap)
    else:
        xlow, xhigh = from_both(jnp.concatenate([source[:, :3], ytile[:, :2]], axis=1), high, "gx")
    v0, v1, v2, v3, moments = call(
        functools.partial(moment_kernel, dense, counts),
        [field, field, field, field, ((devices if dense else 1, 1, 128), f32)],
        (tiles, got, source, ytile, xlow, xhigh),
        [pltpu.VMEM((3, slabs + (3 if pair else 6), 2, 24, 128), f32) for _ in range(3)],
    )
    if dense:
        parts = lax.all_to_all(moments, AXES, 0, 0)
    else:
        parts = lax.psum(moments, AXES)
    return call(functools.partial(combine_kernel, pair), [field, field], (parts, v0, v1, v2, v3), last=True)


def solution(mesh):
    placed = (
        P(None, "gx", "gy", "gz"),
        P(("gx", "gy", "gz"), None),
        P(None, ("gx", "gy", "gz")),
        P(("gx", "gy", "gz"), None),
        P(("gx", "gy", "gz")),
        P("gx", None, None, None, None),
    )
    return jax.shard_map(
        whole_step,
        mesh=mesh,
        in_specs=placed,
        out_specs=(P(None, "gx", "gy", "gz"), P(None, "gx", "gy", "gz")),
        check_vma=False,
    )
```

```python
import functools
import math

import jax
import jax.numpy as jnp
from jax import lax
from jax.experimental import pallas as pl
from jax.experimental.pallas import tpu as pltpu
from jax.sharding import PartitionSpec as P


CELL = 8
VOX = 512
TYPES = 4
ZP = 8
ITERS = 3
AXES = ("gx", "gy", "gz")
DENSE = 64
GRANT = 16 * 1024 * 1024

kerr_scale = 0.1


def where_am_i():
    return tuple(lax.axis_index(a) for a in AXES)


def spectrum_kernel(pair, count, contrast_in, field_in, class_in, kind_in, source_in, library_in,
                    hartley, spectrum, columns, pick, weights, source, library, send_a, send_b,
                    polar, field, classes, kinds, plain_source, contrast, sems):
    rows = contrast.shape[0]
    slabs = source.shape[1]
    gx = lax.axis_index("gx")
    moves = [(field_in, field), (class_in, classes), (kind_in, kinds), (contrast_in, contrast),
             (source_in, plain_source)]
    if pair:
        moves.append((library_in, library))
    moves = [pltpu.make_async_copy(a, b, sems.at[k]) for k, (a, b) in enumerate(moves)]
    for move in moves:
        move.start()
    step = CELL * CELL
    inner = lax.broadcasted_iota(jnp.int32, (step, VOX), 0)
    voxel = lax.broadcasted_iota(jnp.int32, (step, VOX), 1)
    phase = (inner // CELL) * (voxel // CELL % CELL) + (inner % CELL) * (voxel % CELL)
    outer = voxel // step
    plain = 1.0 / math.sqrt(VOX)
    peak = math.sqrt(2.0) / math.sqrt(VOX)
    for block in range(VOX // step):
        turn = (phase + block * outer) & (CELL - 1)
        quarter = turn & 3
        size = jnp.where(quarter == 1, peak, jnp.where(quarter == 3, 0.0, plain))
        value = jnp.where(turn >= 4, -size, size)
        hartley[block * step : (block + 1) * step, :] = value.astype(jnp.bfloat16)
    for move in moves[:3]:
        move.wait()
    fields = field[...].astype(jnp.float32)
    fields = jnp.concatenate([fields, jnp.zeros((5, rows), jnp.float32)], axis=0)
    columns[...] = fields.T
    keys = jnp.where(classes[...] == gx, 0, 1) if pair else classes[...]
    keys = keys * TYPES + kinds[...]
    named = (lax.broadcasted_iota(jnp.int32, (count, rows), 0) == keys).astype(jnp.float32)
    named = jnp.concatenate([named, named], axis=0)
    pick[...] = named.T.astype(jnp.bfloat16)
    moves[3].wait()
    for j in range(3):
        e = columns[:, j : j + 1]
        m = contrast[:, j * VOX : (j + 1) * VOX].astype(jnp.float32)
        weights[:, j * VOX : (j + 1) * VOX] = m
        polar[j * rows : (j + 1) * rows, :] = (m * e).astype(jnp.bfloat16)
    spectrum[...] = jnp.dot(polar[...], hartley[...], preferred_element_type=jnp.float32)
    for move in moves[4:]:
        move.wait()
    even = lax.axis_index("gy") % 2 == 0
    for p in range(slabs):
        x = jnp.where(gx == 0, p, slabs - 1 - p) if pair else p
        for c in range(3):
            value = plain_source[c, x]
            source[c, p] = value
            send_a[c, p] = jnp.where(even, value[4:], value[:4])
            send_b[c, p] = jnp.where(even, value[:4], value[4:])


def solve_kernel(weights, columns, spectrum, hartley, pick, library, other, source, tiles, bundle,
                 mixing, stacked, product):
    rows = weights.shape[0]
    zb = rows // 8
    _, _, gz = where_am_i()
    for ij in range(9):
        i, j = ij // 3, ij % 3
        parts = [library[c, i, j] for c in range(library.shape[0])]
        if pick.shape[1] > 2 * TYPES * library.shape[0]:
            parts = parts + [other[c, i, j] for c in range(other.shape[0])]
        table = jnp.concatenate(parts, axis=0)
        high = table.astype(jnp.bfloat16).astype(jnp.float32)
        both = jnp.concatenate([high, table - high], axis=0).astype(jnp.bfloat16)
        mixing[ij] = jnp.dot(pick[...], both, preferred_element_type=jnp.float32)

    def mix(from_ref):
        for c in range(rows // 16):
            at = slice(c * 16, (c + 1) * 16)
            held = [from_ref[j * rows + c * 16 : j * rows + (c + 1) * 16, :] for j in range(3)]
            for i in range(3):
                total = mixing[3 * i, at, :] * held[0]
                total = total + mixing[3 * i + 1, at, :] * held[1]
                total = total + mixing[3 * i + 2, at, :] * held[2]
                stacked[i * rows + c * 16 : i * rows + (c + 1) * 16, :] = total.astype(jnp.bfloat16)

    mix(spectrum)
    product[...] = jnp.dot(stacked[...], hartley[...], preferred_element_type=jnp.float32)
    for c in range(rows // 16):
        for j in range(3):
            at = slice(j * rows + c * 16, j * rows + (c + 1) * 16)
            m = weights[c * 16 : (c + 1) * 16, j * VOX : (j + 1) * VOX]
            local = columns[c * 16 : (c + 1) * 16, j : j + 1] - product[at, :]
            stacked[at, :] = (m * local * (1.0 + kerr_scale * local * local)).astype(jnp.bfloat16)
    product[...] = jnp.dot(stacked[...], hartley[...], preferred_element_type=jnp.float32)
    mix(product)
    product[...] = jnp.dot(stacked[...], hartley[...], preferred_element_type=jnp.float32)

    depth = lax.broadcasted_iota(jnp.int32, (zb, 128), 0)
    lane = lax.broadcasted_iota(jnp.int32, (zb, 128), 1)
    spread = lane // ZP == depth
    packed = lane % zb == depth
    group = lane // zb
    for c in range(rows // 16):
        means = []
        stiff = jnp.zeros((16, VOX), jnp.float32)
        for j in range(3):
            at = slice(j * rows + c * 16, j * rows + (c + 1) * 16)
            m = weights[c * 16 : (c + 1) * 16, j * VOX : (j + 1) * VOX]
            final = columns[c * 16 : (c + 1) * 16, j : j + 1] - product[at, :]
            weighted = m * final
            means.append(jnp.sum(final + weighted, axis=1, keepdims=True) * (1.0 / VOX))
            stiff = stiff + weighted * final
        means.append(0.5 + jnp.sum(stiff, axis=1, keepdims=True) * (1.0 / (3 * VOX)))
        compact = jnp.zeros((zb, 128), jnp.float32)
        for t in range(4):
            wide = jnp.broadcast_to(means[t], (zb, 128))
            tiles[t, c : c + 1, :] = jnp.sum(jnp.where(spread, wide, 0.0), axis=0, keepdims=True)
            compact = compact + jnp.where(packed & (group == t), wide, 0.0)
        product[c : c + 1, 0:128] = jnp.sum(compact, axis=0, keepdims=True)
        product[c : c + 1, 128:256] = jnp.max(wide, axis=0, keepdims=True)
        product[c : c + 1, 256:384] = jnp.min(wide, axis=0, keepdims=True)
    compact = product[0:8, 0:128]
    tallest, lowest = product[0:8, 128:256], product[0:8, 256:384]

    place = lax.broadcasted_iota(jnp.int32, (8, 128), 1)
    low = jnp.zeros((8, 128), jnp.float32)
    high = jnp.zeros((8, 128), jnp.float32)
    slabs = source.shape[1]
    for s in range(3 * slabs + 1):
        if s < 3 * slabs:
            value = source[s // slabs, s % slabs] - tiles[s // slabs]
        else:
            value = tiles[3]
        here = (place >= 3 * s) & (place < 3 * s + 3)
        low = jnp.where(here, pltpu.roll(value, (3 * s) % 128, 1) if s else value, low)
        high = jnp.where(here, pltpu.roll(value, (3 * s + 3) % 128, 1), high)
    mirrored = jnp.minimum(place + 2 - 2 * (place % 3), 127)
    low = jnp.take_along_axis(low, mirrored, axis=1)
    high = jnp.take_along_axis(high, mirrored, axis=1)
    for d in range(bundle.shape[1]):
        zero = jnp.zeros((8, 128), jnp.float32)
        tile = jnp.where(gz == d, compact, jnp.where(gz + 1 == d, high, jnp.where(gz - 1 == d, low, zero)))
        tile = jnp.where(place == 126, tallest, jnp.where(place == 127, lowest, tile))
        for x in range(bundle.shape[0]):
            bundle[x, d] = tile


def moment_kernel(dense, counts, tiles, got, source, ytile, xlow, xhigh, v0, v1, v2, v3, moments, scale, w0, w1, w2):
    slabs = source.shape[1]
    gx, gy, gz = where_am_i()
    nx, ny, nz = counts
    pair = nx == 2
    base = 0 if pair else 3
    row = lax.broadcasted_iota(jnp.int32, (8, 128), 0)
    lane = lax.broadcasted_iota(jnp.int32, (8, 128), 1)
    has_xl, has_xh = gx > 0, gx < nx - 1
    has_yl, has_yh = gy > 0, gy < ny - 1
    has_zl, has_zh = gz > 0, gz < nz - 1
    one = lambda flag: jnp.where(flag, 1.0, 0.0)
    mask_y = jnp.where(row < 4, one(has_yh), one(has_yl))
    mask_z = jnp.where(lane < 64, one(has_zl), one(has_zh))
    masks = (None, mask_y, mask_z, mask_y * mask_z)
    yl, yh = jnp.maximum(gy - 1, 0), jnp.minimum(gy + 1, ny - 1)
    zl, zh = jnp.maximum(gz - 1, 0), jnp.minimum(gz + 1, nz - 1)
    if pair:
        regions = (None, gx, 1 - gx)
    elif dense:
        regions = (jnp.maximum(gx - 1, 0), gx, jnp.minimum(gx + 1, nx - 1))
    else:
        regions = (0, 1, 2)
    upper = row < 4
    spread = lane // ZP
    zb = 128 // ZP

    def unfold(tile, t):
        return jnp.take_along_axis(tile, spread + t * zb, axis=1)

    def pull(low_tile, high_tile, s):
        a = pltpu.roll(low_tile, (-3 * s) % 128, 1) if s else low_tile
        b = pltpu.roll(high_tile, (125 - 3 * s) % 128, 1)
        return jnp.where(lane < 64, a, b)

    def put(ref, c, at, t, value):
        if t & 1:
            ref[c, at, t >> 1, 0:8, :] = value
            ref[c, at, t >> 1, 16:24, :] = value
        else:
            ref[c, at, t >> 1, 8:16, :] = value

    def take(ref, c, at, t, shift=0):
        start = (8, 9, 7)[shift] if not t & 1 else (0, 1, 15)[shift]
        return ref[c, at, t >> 1, start : start + 8, :]

    diag = {}
    flux = {}
    edges = {1: None, 2: None} if pair else {0: one(has_xl), 1: None, 2: one(has_xh)}
    for r in edges:
        x = regions[r]
        rowtile = jnp.where(upper, got[x, yh, gz], got[x, yl, gz])
        flux[r, 1] = [unfold(rowtile, t) for t in range(3)]
        diag[r, 1] = unfold(rowtile, 3)
        if r == 1:
            flux[r, 0] = [tiles[t] for t in range(3)]
            diag[r, 0] = tiles[3]
        else:
            flux[r, 0] = [unfold(got[x, gy, gz], t) for t in range(3)]
            diag[r, 0] = unfold(got[x, gy, gz], 3)
        side_low, side_high = got[x, gy, zl], got[x, gy, zh]
        corner_low = jnp.where(upper, got[x, yh, zl], got[x, yl, zl])
        corner_high = jnp.where(upper, got[x, yh, zh], got[x, yl, zh])
        diag[r, 2] = pull(side_low, side_high, 3 * slabs)
        diag[r, 3] = pull(corner_low, corner_high, 3 * slabs)
        edge_x = edges[r]
        for c in range(3):
            for k in range(slabs if r == 1 else 3):
                at = base - 1 - k if r == 0 else (base + k if r == 1 else base + slabs + k)
                out = 0 if r == 1 else k + 1
                s = k if r == 1 or (r == 2 and not pair) else slabs - 1 - k
                s = c * slabs + s
                beyond = xlow if r == 0 else xhigh
                value = (source if r == 1 else beyond)[c, k] - flux[r, 0][c]
                put(w0, c, at, 0, value if edge_x is None else value * edge_x)
                if r == 1:
                    v0[c, k] = value
                if out <= 2:
                    halo = (ytile[c, k] if r == 1 else beyond[c, 3 + k]) - flux[r, 1][c]
                    put(w0, c, at, 1, halo * (mask_y if edge_x is None else mask_y * edge_x))
                    value = pull(side_low, side_high, s)
                    put(w0, c, at, 2, value * (mask_z if edge_x is None else mask_z * edge_x))
                if out <= 1:
                    value = pull(corner_low, corner_high, s)
                    put(w0, c, at, 3, value * (masks[3] if edge_x is None else masks[3] * edge_x))
    peak = floor = None
    flat = got.shape[0] * got.shape[1] * got.shape[2]
    for k in range(flat):
        tile = got[k // (got.shape[1] * got.shape[2]), k // got.shape[2] % got.shape[1], k % got.shape[2]]
        peak = tile if peak is None else jnp.maximum(peak, tile)
        floor = tile if floor is None else jnp.minimum(floor, tile)
    peak = jnp.max(peak, axis=0, keepdims=True)[:, 126:127]
    floor = jnp.min(floor, axis=0, keepdims=True)[:, 127:128]
    middle = 0.5 * peak + 0.5 * floor
    spread_of = 6.0 + (0.5 * peak - 0.5 * floor)
    slots = lax.broadcasted_iota(jnp.int32, (1, 128), 1)
    shrink = 1.0 / spread_of
    scale[...] = jnp.where(slots == 0, (6.0 + middle) * shrink, shrink)
    shrink = jnp.broadcast_to(shrink, (8, 128))
    middle = jnp.broadcast_to(middle, (8, 128))
    for key in diag:
        diag[key] = diag[key] - middle
    shrunk = [shrink if mask is None else mask * shrink for mask in masks]

    first_lane, last_lane = lane == 0, lane == 127
    acc = [jnp.zeros((8, 128), jnp.float32) for _ in range(6)]
    levels = (w0, w1, w2, None)
    results = (v0, v1, v2, v3)
    for level in (1, 2, 3):
        src, dst = levels[level - 1], levels[level]
        reach = 3 - level
        for c in range(3):
            for at in range(max(base - reach, 0), base + slabs + reach):
                out = max(base - at, at - base - slabs + 1, 0)
                r = 0 if at < base else (1 if at < base + slabs else 2)
                depth = reach - out
                want = (0,) if depth == 0 else ((0, 1, 2) if depth == 1 else (0, 1, 2, 3))
                edge_x = edges[r]
                for t in want:
                    here, across = take(src, c, at, t), take(src, c, at, t ^ 2)
                    zm = jnp.where(first_lane, across, pltpu.roll(here, 1, 1))
                    zp = jnp.where(last_lane, across, pltpu.roll(here, 127, 1))
                    beside = take(src, c, at + 1, t) + (zp + zm) + (take(src, c, at, t, 1) + take(src, c, at, t, 2))
                    if at > 0:
                        beside = beside + take(src, c, at - 1, t)
                    value = (diag[r, t] * here - beside) * shrunk[t]
                    if edge_x is not None:
                        value = value * edge_x
                    if dst is not None:
                        put(dst, c, at, t, value)
                    if t == 0 and r == 1:
                        results[level][c, at - base] = value
                        acc[2 * level - 1] = acc[2 * level - 1] + here * value
                        if level < 3:
                            acc[2 * level] = acc[2 * level] + value * value
                        if level == 1:
                            acc[0] = acc[0] + here * here
    line = jnp.zeros((1, 128), jnp.float32)
    slot = lax.broadcasted_iota(jnp.int32, (1, 128), 1)
    for k in range(6):
        sums = jnp.sum(jnp.sum(acc[k], axis=0, keepdims=True), axis=1, keepdims=True)
        line = jnp.where(slot == k, sums, line)
    moments[...] = jnp.broadcast_to(line[None], moments.shape)


def combine_kernel(pair, parts, scale, v0, v1, v2, v3, step_out, residual_out):
    total = jnp.sum(parts[...], axis=0)
    nu = [total[:, k : k + 1] for k in range(6)]

    def gram(a, b):
        result = None
        for i, ai in enumerate(a):
            for j, bj in enumerate(b):
                term = ai * bj * nu[i + j]
                result = term if result is None else result + term
        return result

    def added(a, b):
        size = max(len(a), len(b))
        return [a[k] if k >= len(b) else (b[k] if k >= len(a) else a[k] + b[k]) for k in range(size)]

    centre, shrink = scale[:, 0:1], scale[:, 1:2]
    unit = jnp.ones((1, 1), jnp.float32)
    direction, residual, newton = [unit], [unit], []
    norm = nu[0]
    for iteration in range(ITERS):
        image = added([centre * d for d in direction], [0.0 * unit] + direction)
        alpha = norm / gram(direction, image)
        newton = added(newton, [alpha * d for d in direction])
        residual = added(residual, [-alpha * g for g in image])
        if iteration + 1 < ITERS:
            following = gram(residual, residual)
            ratio = following / norm
            direction = added(residual, [ratio * d for d in direction])
            norm = following
    wide = lambda a: jnp.broadcast_to(a, (8, 128))
    newton = [wide(a * shrink) for a in newton]
    residual = [wide(a) for a in residual]
    for c in range(v0.shape[0]):
        for x in range(v0.shape[1]):
            a, b, d = v0[c, x], v1[c, x], v2[c, x]
            to = jnp.where(lax.axis_index("gx") == 0, x, v0.shape[1] - 1 - x) if pair else x
            step_out[c, to] = newton[0] * a + newton[1] * b + newton[2] * d
            residual_out[c, to] = residual[0] * a + residual[1] * b + residual[2] * d + residual[3] * v3[c, x]


def call(body, outs, ins, scratch=(), last=False, raw=False):
    vmem = pl.BlockSpec(memory_space=pltpu.VMEM)
    shape = jax.ShapeDtypeStruct if last else pltpu.VMEM
    return pl.pallas_call(
        body,
        out_shape=tuple(shape(s, d) for s, d in outs),
        in_specs=[pl.BlockSpec(memory_space=pltpu.HBM) if raw else vmem] * len(ins),
        out_specs=tuple(vmem for _ in outs),
        scratch_shapes=list(scratch),
        compiler_params=pltpu.CompilerParams(vmem_limit_bytes=GRANT),
    )(*(pltpu.with_memory_space_constraint(x, pltpu.HBM if raw else pltpu.VMEM) for x in ins))


def ladder(axis):
    count = lax.axis_size(axis)
    forward = [(i, i + 1) for i in range(count - 1)]
    return forward, [(b, a) for a, b in forward]


def pairs_from(first, count):
    couples = [(i, i + 1) for i in range(first, count - 1, 2)]
    return couples + [(b, a) for a, b in couples]


def from_both(low_face, high_face, axis):
    forward, backward = ladder(axis)
    up = lax.ppermute(high_face, axis, forward)
    down = lax.ppermute(low_face, axis, backward)
    return up, down


def whole_step(source, contrast, point_field, point_class, cell_kind, inverse_blocks):
    f32, bf16 = jnp.float32, jnp.bfloat16
    rows = contrast.shape[0]
    counts = tuple(lax.axis_size(a) for a in AXES)
    nx, ny, nz = counts
    devices = nx * ny * nz
    slabs = source.shape[1]
    dense = devices <= DENSE
    pair = nx == 2
    library = inverse_blocks.transpose(0, 2, 3, 1, 4)
    field = (source.shape, f32)
    if pair:
        swap = [(0, 1), (1, 0)]
        other = lax.ppermute(library, "gx", swap)
    else:
        other = lax.all_gather(library, "gx", axis=0, tiled=True)
    count = TYPES * nx
    hartley, spectrum, columns, pick, weights, source, library, send_a, send_b = call(
        functools.partial(spectrum_kernel, pair, count),
        [((VOX, VOX), bf16), ((3 * rows, VOX), f32), ((rows, 8), f32), ((rows, 2 * count), bf16),
         (contrast.shape, f32), field, (library.shape, f32), ((3, slabs, 4, 128), f32), ((3, slabs, 4, 128), f32)],
        (contrast, point_field, point_class.reshape(1, rows), cell_kind.reshape(1, rows), source, library),
        [pltpu.VMEM((3 * rows, VOX), bf16), pltpu.VMEM((3, rows), bf16), pltpu.VMEM((1, rows), jnp.int32),
         pltpu.VMEM((1, rows), jnp.int32), pltpu.VMEM(*field), pltpu.VMEM(contrast.shape, bf16), pltpu.SemaphoreType.DMA((6,))],
        raw=True,
    )
    yb = lax.ppermute(send_b, "gy", pairs_from(1, ny))
    ya = lax.ppermute(send_a, "gy", pairs_from(0, ny))
    tiles, bundle = call(
        solve_kernel,
        [((4, 8, 128), f32), ((nx * ny if dense else 1, nz, 8, 128), f32)],
        (weights, columns, spectrum, hartley, pick, library if pair else other, other, source),
        [pltpu.VMEM((9, rows, VOX), f32), pltpu.VMEM((3 * rows, VOX), bf16), pltpu.VMEM((3 * rows, VOX), f32)],
    )
    if dense:
        got = lax.all_to_all(bundle.reshape(devices, 8, 128), AXES, 0, 0).reshape(nx, ny, nz, 8, 128)
    else:
        below, above = from_both(bundle[0], bundle[0], "gx")
        trio = jnp.stack([below, bundle[0], above], axis=1)
        trio = jnp.broadcast_to(trio[None], (ny,) + trio.shape).reshape(ny * nz, 3, 8, 128)
        got = lax.all_to_all(trio, ("gy", "gz"), 0, 0).reshape(ny, nz, 3, 8, 128).transpose(2, 0, 1, 3, 4)
    if not dense:
        got = got.at[..., 126].set(lax.pmax(jnp.max(tiles[3]), AXES))
        got = got.at[..., 127].set(lax.pmin(jnp.min(tiles[3]), AXES))
    even = lax.axis_index("gy") % 2 == 0
    ytile = jnp.concatenate([jnp.where(even, ya, yb), jnp.where(even, yb, ya)], axis=2)
    high = jnp.concatenate([source[:, : slabs - 4 : -1], ytile[:, : slabs - 3 : -1]], axis=1)
    if pair:
        xlow = xhigh = lax.ppermute(high, "gx", swap)
    else:
        xlow, xhigh = from_both(jnp.concatenate([source[:, :3], ytile[:, :2]], axis=1), high, "gx")
    v0, v1, v2, v3, moments, scale = call(
        functools.partial(moment_kernel, dense, counts),
        [field, field, field, field, ((devices if dense else 1, 1, 128), f32), ((1, 128), f32)],
        (tiles, got, source, ytile, xlow, xhigh),
        [pltpu.VMEM((3, slabs + (3 if pair else 6), 2, 24, 128), f32) for _ in range(3)],
    )
    if dense:
        parts = lax.all_to_all(moments, AXES, 0, 0)
    else:
        parts = lax.psum(moments, AXES)
    return call(functools.partial(combine_kernel, pair), [field, field], (parts, scale, v0, v1, v2, v3), last=True)


def solution(mesh):
    placed = (
        P(None, "gx", "gy", "gz"),
        P(("gx", "gy", "gz"), None),
        P(None, ("gx", "gy", "gz")),
        P(("gx", "gy", "gz"), None),
        P(("gx", "gy", "gz")),
        P("gx", None, None, None, None),
    )
    return jax.shard_map(
        whole_step,
        mesh=mesh,
        in_specs=placed,
        out_specs=(P(None, "gx", "gy", "gz"), P(None, "gx", "gy", "gz")),
        check_vma=False,
    )
```

```python
import functools
import math

import jax
import jax.numpy as jnp
from jax import lax
from jax.experimental import pallas as pl
from jax.experimental.pallas import tpu as pltpu
from jax.sharding import PartitionSpec as P


CELL = 8
VOX = 512
TYPES = 4
ZP = 8
ITERS = 3
AXES = ("gx", "gy", "gz")
DENSE = 64
GRANT = 16 * 1024 * 1024

kerr_scale = 0.1


def where_am_i():
    return tuple(lax.axis_index(a) for a in AXES)


def spectrum_kernel(pair, count, contrast_in, field_in, class_in, kind_in, source_in, library_in,
                    hartley, spectrum, columns, pick, weights, source, library, send_a, send_b,
                    polar, field, classes, kinds, plain_source, contrast, sems):
    rows = contrast.shape[0]
    slabs = source.shape[1]
    gx = lax.axis_index("gx")
    moves = [(field_in, field), (class_in, classes), (kind_in, kinds), (contrast_in, contrast),
             (source_in, plain_source)]
    if pair:
        moves.append((library_in, library))
    moves = [pltpu.make_async_copy(a, b, sems.at[k]) for k, (a, b) in enumerate(moves)]
    for move in moves:
        move.start()
    step = CELL * CELL
    inner = lax.broadcasted_iota(jnp.int32, (step, VOX), 0)
    voxel = lax.broadcasted_iota(jnp.int32, (step, VOX), 1)
    phase = (inner // CELL) * (voxel // CELL % CELL) + (inner % CELL) * (voxel % CELL)
    outer = voxel // step
    plain = 1.0 / math.sqrt(VOX)
    peak = math.sqrt(2.0) / math.sqrt(VOX)
    for block in range(VOX // step):
        turn = (phase + block * outer) & (CELL - 1)
        quarter = turn & 3
        size = jnp.where(quarter == 1, peak, jnp.where(quarter == 3, 0.0, plain))
        value = jnp.where(turn >= 4, -size, size)
        hartley[block * step : (block + 1) * step, :] = value.astype(jnp.bfloat16)
    for move in moves[:3]:
        move.wait()
    fields = field[...].astype(jnp.float32)
    fields = jnp.concatenate([fields, jnp.zeros((5, rows), jnp.float32)], axis=0)
    columns[...] = fields.T
    keys = jnp.where(classes[...] == gx, 0, 1) if pair else classes[...]
    keys = keys * TYPES + kinds[...]
    named = (lax.broadcasted_iota(jnp.int32, (count, rows), 0) == keys).astype(jnp.float32)
    named = jnp.concatenate([named, named], axis=0)
    pick[...] = named.T.astype(jnp.bfloat16)
    moves[3].wait()
    for j in range(3):
        e = columns[:, j : j + 1]
        m = contrast[:, j * VOX : (j + 1) * VOX].astype(jnp.float32)
        weights[:, j * VOX : (j + 1) * VOX] = m
        polar[j * rows : (j + 1) * rows, :] = (m * e).astype(jnp.bfloat16)
    spectrum[...] = jnp.dot(polar[...], hartley[...], preferred_element_type=jnp.float32)
    for move in moves[4:]:
        move.wait()
    even = lax.axis_index("gy") % 2 == 0
    for p in range(slabs):
        x = jnp.where(gx == 0, p, slabs - 1 - p) if pair else p
        for c in range(3):
            value = plain_source[c, x]
            source[c, p] = value
            send_a[c, p] = jnp.where(even, value[4:], value[:4])
            send_b[c, p] = jnp.where(even, value[:4], value[4:])


def solve_kernel(weights, columns, spectrum, hartley, pick, library, other, source, tiles, bundle,
                 mixing, stacked, product):
    rows = weights.shape[0]
    zb = rows // 8
    _, _, gz = where_am_i()
    for ij in range(9):
        i, j = ij // 3, ij % 3
        parts = [library[c, i, j] for c in range(library.shape[0])]
        if pick.shape[1] > 2 * TYPES * library.shape[0]:
            parts = parts + [other[c, i, j] for c in range(other.shape[0])]
        table = jnp.concatenate(parts, axis=0)
        high = table.astype(jnp.bfloat16).astype(jnp.float32)
        both = jnp.concatenate([high, table - high], axis=0).astype(jnp.bfloat16)
        mixing[ij] = jnp.dot(pick[...], both, preferred_element_type=jnp.float32)

    def mix(from_ref):
        for c in range(rows // 16):
            at = slice(c * 16, (c + 1) * 16)
            held = [from_ref[j * rows + c * 16 : j * rows + (c + 1) * 16, :] for j in range(3)]
            for i in range(3):
                total = mixing[3 * i, at, :] * held[0]
                total = total + mixing[3 * i + 1, at, :] * held[1]
                total = total + mixing[3 * i + 2, at, :] * held[2]
                stacked[i * rows + c * 16 : i * rows + (c + 1) * 16, :] = total.astype(jnp.bfloat16)

    mix(spectrum)
    product[...] = jnp.dot(stacked[...], hartley[...], preferred_element_type=jnp.float32)
    for c in range(rows // 16):
        for j in range(3):
            at = slice(j * rows + c * 16, j * rows + (c + 1) * 16)
            m = weights[c * 16 : (c + 1) * 16, j * VOX : (j + 1) * VOX]
            local = columns[c * 16 : (c + 1) * 16, j : j + 1] - product[at, :]
            stacked[at, :] = (m * local * (1.0 + kerr_scale * local * local)).astype(jnp.bfloat16)
    product[...] = jnp.dot(stacked[...], hartley[...], preferred_element_type=jnp.float32)
    mix(product)
    product[...] = jnp.dot(stacked[...], hartley[...], preferred_element_type=jnp.float32)

    depth = lax.broadcasted_iota(jnp.int32, (zb, 128), 0)
    lane = lax.broadcasted_iota(jnp.int32, (zb, 128), 1)
    spread = lane // ZP == depth
    packed = lane % zb == depth
    group = lane // zb
    for c in range(rows // 16):
        means = []
        stiff = jnp.zeros((16, VOX), jnp.float32)
        for j in range(3):
            at = slice(j * rows + c * 16, j * rows + (c + 1) * 16)
            m = weights[c * 16 : (c + 1) * 16, j * VOX : (j + 1) * VOX]
            final = columns[c * 16 : (c + 1) * 16, j : j + 1] - product[at, :]
            weighted = m * final
            means.append(jnp.sum(final + weighted, axis=1, keepdims=True) * (1.0 / VOX))
            stiff = stiff + weighted * final
        means.append(0.5 + jnp.sum(stiff, axis=1, keepdims=True) * (1.0 / (3 * VOX)))
        compact = jnp.zeros((zb, 128), jnp.float32)
        for t in range(4):
            wide = jnp.broadcast_to(means[t], (zb, 128))
            tiles[t, c : c + 1, :] = jnp.sum(jnp.where(spread, wide, 0.0), axis=0, keepdims=True)
            compact = compact + jnp.where(packed & (group == t), wide, 0.0)
        product[c : c + 1, 0:128] = jnp.sum(compact, axis=0, keepdims=True)
        product[c : c + 1, 128:256] = jnp.max(wide, axis=0, keepdims=True)
        product[c : c + 1, 256:384] = jnp.min(wide, axis=0, keepdims=True)
    compact = product[0:8, 0:128]
    tallest, lowest = product[0:8, 128:256], product[0:8, 256:384]

    place = lax.broadcasted_iota(jnp.int32, (8, 128), 1)
    low = jnp.zeros((8, 128), jnp.float32)
    high = jnp.zeros((8, 128), jnp.float32)
    slabs = source.shape[1]
    for s in range(3 * slabs + 1):
        if s < 3 * slabs:
            value = source[s // slabs, s % slabs] - tiles[s // slabs]
        else:
            value = tiles[3]
        here = (place >= 3 * s) & (place < 3 * s + 3)
        low = jnp.where(here, pltpu.roll(value, (3 * s) % 128, 1) if s else value, low)
        high = jnp.where(here, pltpu.roll(value, (3 * s + 3) % 128, 1), high)
    mirrored = jnp.minimum(place + 2 - 2 * (place % 3), 127)
    low = jnp.take_along_axis(low, mirrored, axis=1)
    high = jnp.take_along_axis(high, mirrored, axis=1)
    for d in range(bundle.shape[1]):
        zero = jnp.zeros((8, 128), jnp.float32)
        tile = jnp.where(gz == d, compact, jnp.where(gz + 1 == d, high, jnp.where(gz - 1 == d, low, zero)))
        tile = jnp.where(place == 126, tallest, jnp.where(place == 127, lowest, tile))
        for x in range(bundle.shape[0]):
            bundle[x, d] = tile


def moment_kernel(dense, counts, tiles, got, source, ytile, xlow, xhigh, v0, v1, v2, v3, moments, scale, w0, w1, w2):
    slabs = source.shape[1]
    gx, gy, gz = where_am_i()
    nx, ny, nz = counts
    pair = nx == 2
    base = 0 if pair else 3
    row = lax.broadcasted_iota(jnp.int32, (8, 128), 0)
    lane = lax.broadcasted_iota(jnp.int32, (8, 128), 1)
    has_xl, has_xh = gx > 0, gx < nx - 1
    has_yl, has_yh = gy > 0, gy < ny - 1
    has_zl, has_zh = gz > 0, gz < nz - 1
    one = lambda flag: jnp.where(flag, 1.0, 0.0)
    mask_y = jnp.where(row < 4, one(has_yh), one(has_yl))
    mask_z = jnp.where(lane < 64, one(has_zl), one(has_zh))
    masks = (None, mask_y, mask_z, mask_y * mask_z)
    yl, yh = jnp.maximum(gy - 1, 0), jnp.minimum(gy + 1, ny - 1)
    zl, zh = jnp.maximum(gz - 1, 0), jnp.minimum(gz + 1, nz - 1)
    if pair:
        regions = (None, gx, 1 - gx)
    elif dense:
        regions = (jnp.maximum(gx - 1, 0), gx, jnp.minimum(gx + 1, nx - 1))
    else:
        regions = (0, 1, 2)
    upper = row < 4
    spread = lane // ZP
    zb = 128 // ZP

    def unfold(tile, t):
        return jnp.take_along_axis(tile, spread + t * zb, axis=1)

    def pull(low_tile, high_tile, s):
        a = pltpu.roll(low_tile, (-3 * s) % 128, 1) if s else low_tile
        b = pltpu.roll(high_tile, (125 - 3 * s) % 128, 1)
        return jnp.where(lane < 64, a, b)

    def put(ref, c, at, t, value):
        if t & 1:
            ref[c, at, t >> 1, 0:8, :] = value
            ref[c, at, t >> 1, 16:24, :] = value
        else:
            ref[c, at, t >> 1, 8:16, :] = value

    def take(ref, c, at, t, shift=0):
        start = (8, 9, 7)[shift] if not t & 1 else (0, 1, 15)[shift]
        return ref[c, at, t >> 1, start : start + 8, :]

    diag = {}
    flux = {}
    edges = {1: None, 2: None} if pair else {0: one(has_xl), 1: None, 2: one(has_xh)}
    for r in edges:
        x = regions[r]
        rowtile = jnp.where(upper, got[x, yh, gz], got[x, yl, gz])
        flux[r, 1] = [unfold(rowtile, t) for t in range(3)]
        diag[r, 1] = unfold(rowtile, 3)
        if r == 1:
            flux[r, 0] = [tiles[t] for t in range(3)]
            diag[r, 0] = tiles[3]
        else:
            flux[r, 0] = [unfold(got[x, gy, gz], t) for t in range(3)]
            diag[r, 0] = unfold(got[x, gy, gz], 3)
        side_low, side_high = got[x, gy, zl], got[x, gy, zh]
        corner_low = jnp.where(upper, got[x, yh, zl], got[x, yl, zl])
        corner_high = jnp.where(upper, got[x, yh, zh], got[x, yl, zh])
        diag[r, 2] = pull(side_low, side_high, 3 * slabs)
        diag[r, 3] = pull(corner_low, corner_high, 3 * slabs)
        edge_x = edges[r]
        for c in range(3):
            for k in range(slabs if r == 1 else 3):
                at = base - 1 - k if r == 0 else (base + k if r == 1 else base + slabs + k)
                out = 0 if r == 1 else k + 1
                s = k if r == 1 or (r == 2 and not pair) else slabs - 1 - k
                s = c * slabs + s
                beyond = xlow if r == 0 else xhigh
                value = (source if r == 1 else beyond)[c, k] - flux[r, 0][c]
                put(w0, c, at, 0, value if edge_x is None else value * edge_x)
                if r == 1:
                    v0[c, k] = value
                if out <= 2:
                    halo = (ytile[c, k] if r == 1 else beyond[c, 3 + k]) - flux[r, 1][c]
                    put(w0, c, at, 1, halo * (mask_y if edge_x is None else mask_y * edge_x))
                    value = pull(side_low, side_high, s)
                    put(w0, c, at, 2, value * (mask_z if edge_x is None else mask_z * edge_x))
                if out <= 1:
                    value = pull(corner_low, corner_high, s)
                    put(w0, c, at, 3, value * (masks[3] if edge_x is None else masks[3] * edge_x))
    peak = floor = None
    flat = got.shape[0] * got.shape[1] * got.shape[2]
    for k in range(flat):
        tile = got[k // (got.shape[1] * got.shape[2]), k // got.shape[2] % got.shape[1], k % got.shape[2]]
        peak = tile if peak is None else jnp.maximum(peak, tile)
        floor = tile if floor is None else jnp.minimum(floor, tile)
    peak = jnp.max(peak, axis=0, keepdims=True)[:, 126:127]
    floor = jnp.min(floor, axis=0, keepdims=True)[:, 127:128]
    middle = 0.5 * peak + 0.5 * floor
    spread_of = 6.0 + (0.5 * peak - 0.5 * floor)
    slots = lax.broadcasted_iota(jnp.int32, (1, 128), 1)
    shrink = 1.0 / spread_of
    scale[...] = jnp.where(slots == 0, (6.0 + middle) * shrink, shrink)
    shrink = jnp.broadcast_to(shrink, (8, 128))
    middle = jnp.broadcast_to(middle, (8, 128))
    for key in diag:
        diag[key] = diag[key] - middle
    shrunk = [shrink if mask is None else mask * shrink for mask in masks]

    first_lane, last_lane = lane == 0, lane == 127
    acc = [jnp.zeros((8, 128), jnp.float32) for _ in range(6)]
    levels = (w0, w1, w2, None)
    results = (v0, v1, v2, v3)
    for level in (1, 2, 3):
        src, dst = levels[level - 1], levels[level]
        reach = 3 - level
        for c in range(3):
            for at in range(max(base - reach, 0), base + slabs + reach):
                out = max(base - at, at - base - slabs + 1, 0)
                r = 0 if at < base else (1 if at < base + slabs else 2)
                depth = reach - out
                want = (0,) if depth == 0 else ((0, 1, 2) if depth == 1 else (0, 1, 2, 3))
                edge_x = edges[r]
                for t in want:
                    here, across = take(src, c, at, t), take(src, c, at, t ^ 2)
                    zm = jnp.where(first_lane, across, pltpu.roll(here, 1, 1))
                    zp = jnp.where(last_lane, across, pltpu.roll(here, 127, 1))
                    beside = take(src, c, at + 1, t) + (zp + zm) + (take(src, c, at, t, 1) + take(src, c, at, t, 2))
                    if at > 0:
                        beside = beside + take(src, c, at - 1, t)
                    value = (diag[r, t] * here - beside) * shrunk[t]
                    if edge_x is not None:
                        value = value * edge_x
                    if dst is not None:
                        put(dst, c, at, t, value)
                    if t == 0 and r == 1:
                        results[level][c, at - base] = value
                        acc[2 * level - 1] = acc[2 * level - 1] + here * value
                        if level < 3:
                            acc[2 * level] = acc[2 * level] + value * value
                        if level == 1:
                            acc[0] = acc[0] + here * here
    line = jnp.zeros((1, 128), jnp.float32)
    slot = lax.broadcasted_iota(jnp.int32, (1, 128), 1)
    for k in range(6):
        sums = jnp.sum(jnp.sum(acc[k], axis=0, keepdims=True), axis=1, keepdims=True)
        line = jnp.where(slot == k, sums, line)
    moments[...] = jnp.broadcast_to(line[None], moments.shape)


def combine_kernel(pair, parts, scale, v0, v1, v2, v3, step_out, residual_out):
    total = jnp.sum(parts[...], axis=0)
    nu = [total[:, k : k + 1] for k in range(6)]

    def gram(a, b):
        result = None
        for i, ai in enumerate(a):
            for j, bj in enumerate(b):
                term = ai * bj * nu[i + j]
                result = term if result is None else result + term
        return result

    def added(a, b):
        size = max(len(a), len(b))
        return [a[k] if k >= len(b) else (b[k] if k >= len(a) else a[k] + b[k]) for k in range(size)]

    centre, shrink = scale[:, 0:1], scale[:, 1:2]
    unit = jnp.ones((1, 1), jnp.float32)
    direction, residual, newton = [unit], [unit], []
    norm = nu[0]
    for iteration in range(ITERS):
        image = added([centre * d for d in direction], [0.0 * unit] + direction)
        alpha = norm / gram(direction, image)
        newton = added(newton, [alpha * d for d in direction])
        residual = added(residual, [-alpha * g for g in image])
        if iteration + 1 < ITERS:
            following = gram(residual, residual)
            ratio = following / norm
            direction = added(residual, [ratio * d for d in direction])
            norm = following
    wide = lambda a: jnp.broadcast_to(a, (8, 128))
    newton = [wide(a * shrink) for a in newton]
    residual = [wide(a) for a in residual]
    for c in range(v0.shape[0]):
        for x in range(v0.shape[1]):
            a, b, d = v0[c, x], v1[c, x], v2[c, x]
            to = jnp.where(lax.axis_index("gx") == 0, x, v0.shape[1] - 1 - x) if pair else x
            step_out[c, to] = newton[0] * a + newton[1] * b + newton[2] * d
            residual_out[c, to] = residual[0] * a + residual[1] * b + residual[2] * d + residual[3] * v3[c, x]


def call(body, outs, ins, scratch=(), last=False, raw=False):
    vmem = pl.BlockSpec(memory_space=pltpu.VMEM)
    shape = jax.ShapeDtypeStruct if last else pltpu.VMEM
    return pl.pallas_call(
        body,
        out_shape=tuple(shape(s, d) for s, d in outs),
        in_specs=[pl.BlockSpec(memory_space=pltpu.HBM) if raw else vmem] * len(ins),
        out_specs=tuple(vmem for _ in outs),
        scratch_shapes=list(scratch),
        compiler_params=pltpu.CompilerParams(vmem_limit_bytes=GRANT),
    )(*(pltpu.with_memory_space_constraint(x, pltpu.HBM if raw else pltpu.VMEM) for x in ins))


def ladder(axis):
    count = lax.axis_size(axis)
    forward = [(i, i + 1) for i in range(count - 1)]
    return forward, [(b, a) for a, b in forward]


def pairs_from(first, count):
    couples = [(i, i + 1) for i in range(first, count - 1, 2)]
    return couples + [(b, a) for a, b in couples]


def from_both(low_face, high_face, axis):
    forward, backward = ladder(axis)
    up = lax.ppermute(high_face, axis, forward)
    down = lax.ppermute(low_face, axis, backward)
    return up, down


def whole_step(source, contrast, point_field, point_class, cell_kind, inverse_blocks):
    f32, bf16 = jnp.float32, jnp.bfloat16
    rows = contrast.shape[0]
    counts = tuple(lax.axis_size(a) for a in AXES)
    nx, ny, nz = counts
    devices = nx * ny * nz
    slabs = source.shape[1]
    dense = devices <= DENSE
    pair = nx == 2
    library = inverse_blocks.transpose(0, 2, 3, 1, 4)
    field = (source.shape, f32)
    if pair:
        swap = [(0, 1), (1, 0)]
        other = lax.ppermute(library, "gx", swap)
    else:
        other = lax.all_gather(library, "gx", axis=0, tiled=True)
    count = TYPES * nx
    hartley, spectrum, columns, pick, weights, source, library, send_a, send_b = call(
        functools.partial(spectrum_kernel, pair, count),
        [((VOX, VOX), bf16), ((3 * rows, VOX), f32), ((rows, 8), f32), ((rows, 2 * count), bf16),
         (contrast.shape, f32), field, (library.shape, f32), ((3, slabs, 4, 128), f32), ((3, slabs, 4, 128), f32)],
        (contrast, point_field, point_class.reshape(1, rows), cell_kind.reshape(1, rows), source, library),
        [pltpu.VMEM((3 * rows, VOX), bf16), pltpu.VMEM((3, rows), bf16), pltpu.VMEM((1, rows), jnp.int32),
         pltpu.VMEM((1, rows), jnp.int32), pltpu.VMEM(*field), pltpu.VMEM(contrast.shape, bf16), pltpu.SemaphoreType.DMA((6,))],
        raw=True,
    )
    couples = []
    for z in range(nz):
        mate = z ^ 1 if z ^ 1 < nz else z
        for i in range(ny):
            j = i + 1 if i % 2 else i - 1
            inside = 0 <= j < ny
            couples.append((i * nz + z, (j * nz + z) if inside else i * nz + mate))
    yb = lax.ppermute(send_b, ("gy", "gz"), couples)
    ya = lax.ppermute(send_a, "gy", pairs_from(0, ny))
    tiles, bundle = call(
        solve_kernel,
        [((4, 8, 128), f32), ((nx * ny if dense else 1, nz, 8, 128), f32)],
        (weights, columns, spectrum, hartley, pick, library if pair else other, other, source),
        [pltpu.VMEM((9, rows, VOX), f32), pltpu.VMEM((3 * rows, VOX), bf16), pltpu.VMEM((3 * rows, VOX), f32)],
    )
    if dense:
        got = lax.all_to_all(bundle.reshape(devices, 8, 128), AXES, 0, 0).reshape(nx, ny, nz, 8, 128)
    else:
        below, above = from_both(bundle[0], bundle[0], "gx")
        trio = jnp.stack([below, bundle[0], above], axis=1)
        trio = jnp.broadcast_to(trio[None], (ny,) + trio.shape).reshape(ny * nz, 3, 8, 128)
        got = lax.all_to_all(trio, ("gy", "gz"), 0, 0).reshape(ny, nz, 3, 8, 128).transpose(2, 0, 1, 3, 4)
    if not dense:
        got = got.at[..., 126].set(lax.pmax(jnp.max(tiles[3]), AXES))
        got = got.at[..., 127].set(lax.pmin(jnp.min(tiles[3]), AXES))
    even = lax.axis_index("gy") % 2 == 0
    ytile = jnp.concatenate([jnp.where(even, ya, yb), jnp.where(even, yb, ya)], axis=2)
    high = jnp.concatenate([source[:, : slabs - 4 : -1], ytile[:, : slabs - 3 : -1]], axis=1)
    if pair:
        xlow = xhigh = lax.ppermute(high, "gx", swap)
    else:
        xlow, xhigh = from_both(jnp.concatenate([source[:, :3], ytile[:, :2]], axis=1), high, "gx")
    v0, v1, v2, v3, moments, scale = call(
        functools.partial(moment_kernel, dense, counts),
        [field, field, field, field, ((devices if dense else 1, 1, 128), f32), ((1, 128), f32)],
        (tiles, got, source, ytile, xlow, xhigh),
        [pltpu.VMEM((3, slabs + (3 if pair else 6), 2, 24, 128), f32) for _ in range(3)],
    )
    if dense:
        parts = lax.all_to_all(moments, AXES, 0, 0)
    else:
        parts = lax.psum(moments, AXES)
    return call(functools.partial(combine_kernel, pair), [field, field], (parts, scale, v0, v1, v2, v3), last=True)


def solution(mesh):
    placed = (
        P(None, "gx", "gy", "gz"),
        P(("gx", "gy", "gz"), None),
        P(None, ("gx", "gy", "gz")),
        P(("gx", "gy", "gz"), None),
        P(("gx", "gy", "gz")),
        P("gx", None, None, None, None),
    )
    return jax.shard_map(
        whole_step,
        mesh=mesh,
        in_specs=placed,
        out_specs=(P(None, "gx", "gy", "gz"), P(None, "gx", "gy", "gz")),
        check_vma=False,
    )
```

```python
import functools
import math

import jax
import jax.numpy as jnp
from jax import lax
from jax.experimental import pallas as pl
from jax.experimental.pallas import tpu as pltpu
from jax.sharding import PartitionSpec as P


CELL = 8
VOX = 512
TYPES = 4
ZP = 8
ITERS = 3
AXES = ("gx", "gy", "gz")
DENSE = 64
GRANT = 16 * 1024 * 1024

kerr_scale = 0.1


def where_am_i():
    return tuple(lax.axis_index(a) for a in AXES)


def spectrum_kernel(pair, count, contrast_in, field_in, class_in, kind_in, source_in, library_in,
                    hartley, spectrum, columns, pick, weights, source, library, send_a, send_b, faces,
                    polar, field, classes, kinds, plain_source, contrast, sems):
    rows = contrast.shape[0]
    slabs = source.shape[1]
    gx = lax.axis_index("gx")
    moves = [(field_in, field), (class_in, classes), (kind_in, kinds), (contrast_in, contrast),
             (source_in, plain_source)]
    if pair:
        moves.append((library_in, library))
    moves = [pltpu.make_async_copy(a, b, sems.at[k]) for k, (a, b) in enumerate(moves)]
    for move in moves:
        move.start()
    step = CELL * CELL
    inner = lax.broadcasted_iota(jnp.int32, (step, VOX), 0)
    voxel = lax.broadcasted_iota(jnp.int32, (step, VOX), 1)
    phase = (inner // CELL) * (voxel // CELL % CELL) + (inner % CELL) * (voxel % CELL)
    outer = voxel // step
    plain = 1.0 / math.sqrt(VOX)
    peak = math.sqrt(2.0) / math.sqrt(VOX)
    for block in range(VOX // step):
        turn = (phase + block * outer) & (CELL - 1)
        quarter = turn & 3
        size = jnp.where(quarter == 1, peak, jnp.where(quarter == 3, 0.0, plain))
        value = jnp.where(turn >= 4, -size, size)
        hartley[block * step : (block + 1) * step, :] = value.astype(jnp.bfloat16)
    for move in moves[:3]:
        move.wait()
    fields = field[...].astype(jnp.float32)
    fields = jnp.concatenate([fields, jnp.zeros((5, rows), jnp.float32)], axis=0)
    columns[...] = fields.T
    keys = jnp.where(classes[...] == gx, 0, 1) if pair else classes[...]
    keys = keys * TYPES + kinds[...]
    named = (lax.broadcasted_iota(jnp.int32, (count, rows), 0) == keys).astype(jnp.float32)
    named = jnp.concatenate([named, named], axis=0)
    pick[...] = named.T.astype(jnp.bfloat16)
    moves[3].wait()
    for j in range(3):
        e = columns[:, j : j + 1]
        m = contrast[:, j * VOX : (j + 1) * VOX].astype(jnp.float32)
        weights[:, j * VOX : (j + 1) * VOX] = m
        polar[j * rows : (j + 1) * rows, :] = (m * e).astype(jnp.bfloat16)
    spectrum[...] = jnp.dot(polar[...], hartley[...], preferred_element_type=jnp.float32)
    for move in moves[4:]:
        move.wait()
    even = lax.axis_index("gy") % 2 == 0
    for p in range(slabs):
        x = jnp.where(gx == 0, p, slabs - 1 - p) if pair else p
        for c in range(3):
            value = plain_source[c, x]
            source[c, p] = value
            send_a[c, p] = jnp.where(even, value[4:], value[:4])
            send_b[c, p] = jnp.where(even, value[:4], value[4:])
    place = lax.broadcasted_iota(jnp.int32, (8, 128), 1)
    low = jnp.zeros((8, 128), jnp.float32)
    high = jnp.zeros((8, 128), jnp.float32)
    for s in range(3 * slabs):
        value = source[s // slabs, s % slabs]
        here = (place >= 3 * s) & (place < 3 * s + 3)
        low = jnp.where(here, pltpu.roll(value, (3 * s) % 128, 1) if s else value, low)
        high = jnp.where(here, pltpu.roll(value, (3 * s + 3) % 128, 1), high)
    mirrored = jnp.minimum(place + 2 - 2 * (place % 3), 127)
    faces[0] = jnp.take_along_axis(low, mirrored, axis=1)
    faces[1] = jnp.take_along_axis(high, mirrored, axis=1)


def solve_kernel(slabs, weights, columns, spectrum, hartley, pick, library, other, faces, tiles, bundle,
                 mixing, stacked, product):
    rows = weights.shape[0]
    zb = rows // 8
    _, _, gz = where_am_i()
    for ij in range(9):
        i, j = ij // 3, ij % 3
        parts = [library[c, i, j] for c in range(library.shape[0])]
        if pick.shape[1] > 2 * TYPES * library.shape[0]:
            parts = parts + [other[c, i, j] for c in range(other.shape[0])]
        table = jnp.concatenate(parts, axis=0)
        high = table.astype(jnp.bfloat16).astype(jnp.float32)
        both = jnp.concatenate([high, table - high], axis=0).astype(jnp.bfloat16)
        mixing[ij] = jnp.dot(pick[...], both, preferred_element_type=jnp.float32)

    def mix(from_ref):
        for c in range(rows // 16):
            at = slice(c * 16, (c + 1) * 16)
            held = [from_ref[j * rows + c * 16 : j * rows + (c + 1) * 16, :] for j in range(3)]
            for i in range(3):
                total = mixing[3 * i, at, :] * held[0]
                total = total + mixing[3 * i + 1, at, :] * held[1]
                total = total + mixing[3 * i + 2, at, :] * held[2]
                stacked[i * rows + c * 16 : i * rows + (c + 1) * 16, :] = total.astype(jnp.bfloat16)

    mix(spectrum)
    product[...] = jnp.dot(stacked[...], hartley[...], preferred_element_type=jnp.float32)
    for c in range(rows // 16):
        for j in range(3):
            at = slice(j * rows + c * 16, j * rows + (c + 1) * 16)
            m = weights[c * 16 : (c + 1) * 16, j * VOX : (j + 1) * VOX]
            local = columns[c * 16 : (c + 1) * 16, j : j + 1] - product[at, :]
            stacked[at, :] = (m * local * (1.0 + kerr_scale * local * local)).astype(jnp.bfloat16)
    product[...] = jnp.dot(stacked[...], hartley[...], preferred_element_type=jnp.float32)
    mix(product)
    product[...] = jnp.dot(stacked[...], hartley[...], preferred_element_type=jnp.float32)

    depth = lax.broadcasted_iota(jnp.int32, (zb, 128), 0)
    lane = lax.broadcasted_iota(jnp.int32, (zb, 128), 1)
    spread = lane // ZP == depth
    packed = lane % zb == depth
    group = lane // zb
    for c in range(rows // 16):
        means = []
        stiff = jnp.zeros((16, VOX), jnp.float32)
        for j in range(3):
            at = slice(j * rows + c * 16, j * rows + (c + 1) * 16)
            m = weights[c * 16 : (c + 1) * 16, j * VOX : (j + 1) * VOX]
            final = columns[c * 16 : (c + 1) * 16, j : j + 1] - product[at, :]
            weighted = m * final
            means.append(jnp.sum(final + weighted, axis=1, keepdims=True) * (1.0 / VOX))
            stiff = stiff + weighted * final
        means.append(0.5 + jnp.sum(stiff, axis=1, keepdims=True) * (1.0 / (3 * VOX)))
        compact = jnp.zeros((zb, 128), jnp.float32)
        for t in range(4):
            wide = jnp.broadcast_to(means[t], (zb, 128))
            tiles[t, c : c + 1, :] = jnp.sum(jnp.where(spread, wide, 0.0), axis=0, keepdims=True)
            compact = compact + jnp.where(packed & (group == t), wide, 0.0)
        product[c : c + 1, 0:128] = jnp.sum(compact, axis=0, keepdims=True)
        product[c : c + 1, 128:256] = jnp.max(wide, axis=0, keepdims=True)
        product[c : c + 1, 256:384] = jnp.min(wide, axis=0, keepdims=True)
    compact = product[0:8, 0:128]
    tallest, lowest = product[0:8, 128:256], product[0:8, 256:384]

    place = lax.broadcasted_iota(jnp.int32, (8, 128), 1)
    width = 3 * slabs
    sides = []
    for k, at in enumerate((0, 127)):
        edge = [jnp.broadcast_to(tiles[t][:, at : at + 1], (8, 128)) for t in range(4)]
        constant = jnp.where(place < width, edge[0], jnp.where(place < 2 * width, edge[1], edge[2]))
        sides.append(jnp.where(place < 3 * width, faces[k] - constant, edge[3]))
    low, high = sides
    for d in range(bundle.shape[1]):
        zero = jnp.zeros((8, 128), jnp.float32)
        tile = jnp.where(gz == d, compact, jnp.where(gz + 1 == d, high, jnp.where(gz - 1 == d, low, zero)))
        tile = jnp.where(place == 126, tallest, jnp.where(place == 127, lowest, tile))
        for x in range(bundle.shape[0]):
            bundle[x, d] = tile


def moment_kernel(dense, counts, tiles, got, source, ytile, xlow, xhigh, v0, v1, v2, v3, moments, scale, w0, w1, w2):
    slabs = source.shape[1]
    gx, gy, gz = where_am_i()
    nx, ny, nz = counts
    pair = nx == 2
    base = 0 if pair else 3
    row = lax.broadcasted_iota(jnp.int32, (8, 128), 0)
    lane = lax.broadcasted_iota(jnp.int32, (8, 128), 1)
    has_xl, has_xh = gx > 0, gx < nx - 1
    has_yl, has_yh = gy > 0, gy < ny - 1
    has_zl, has_zh = gz > 0, gz < nz - 1
    one = lambda flag: jnp.where(flag, 1.0, 0.0)
    mask_y = jnp.where(row < 4, one(has_yh), one(has_yl))
    mask_z = jnp.where(lane < 64, one(has_zl), one(has_zh))
    masks = (None, mask_y, mask_z, mask_y * mask_z)
    yl, yh = jnp.maximum(gy - 1, 0), jnp.minimum(gy + 1, ny - 1)
    zl, zh = jnp.maximum(gz - 1, 0), jnp.minimum(gz + 1, nz - 1)
    if pair:
        regions = (None, gx, 1 - gx)
    elif dense:
        regions = (jnp.maximum(gx - 1, 0), gx, jnp.minimum(gx + 1, nx - 1))
    else:
        regions = (0, 1, 2)
    upper = row < 4
    spread = lane // ZP
    zb = 128 // ZP

    def unfold(tile, t):
        return jnp.take_along_axis(tile, spread + t * zb, axis=1)

    def pull(low_tile, high_tile, s):
        a = pltpu.roll(low_tile, (-3 * s) % 128, 1) if s else low_tile
        b = pltpu.roll(high_tile, (125 - 3 * s) % 128, 1)
        return jnp.where(lane < 64, a, b)

    def put(ref, c, at, t, value):
        if t & 1:
            ref[c, at, t >> 1, 0:8, :] = value
            ref[c, at, t >> 1, 16:24, :] = value
        else:
            ref[c, at, t >> 1, 8:16, :] = value

    def take(ref, c, at, t, shift=0):
        start = (8, 9, 7)[shift] if not t & 1 else (0, 1, 15)[shift]
        return ref[c, at, t >> 1, start : start + 8, :]

    diag = {}
    flux = {}
    edges = {1: None, 2: None} if pair else {0: one(has_xl), 1: None, 2: one(has_xh)}
    for r in edges:
        x = regions[r]
        rowtile = jnp.where(upper, got[x, yh, gz], got[x, yl, gz])
        flux[r, 1] = [unfold(rowtile, t) for t in range(3)]
        diag[r, 1] = unfold(rowtile, 3)
        if r == 1:
            flux[r, 0] = [tiles[t] for t in range(3)]
            diag[r, 0] = tiles[3]
        else:
            flux[r, 0] = [unfold(got[x, gy, gz], t) for t in range(3)]
            diag[r, 0] = unfold(got[x, gy, gz], 3)
        side_low, side_high = got[x, gy, zl], got[x, gy, zh]
        corner_low = jnp.where(upper, got[x, yh, zl], got[x, yl, zl])
        corner_high = jnp.where(upper, got[x, yh, zh], got[x, yl, zh])
        diag[r, 2] = pull(side_low, side_high, 3 * slabs)
        diag[r, 3] = pull(corner_low, corner_high, 3 * slabs)
        edge_x = edges[r]
        for c in range(3):
            for k in range(slabs if r == 1 else 3):
                at = base - 1 - k if r == 0 else (base + k if r == 1 else base + slabs + k)
                out = 0 if r == 1 else k + 1
                s = k if r == 1 or (r == 2 and not pair) else slabs - 1 - k
                s = c * slabs + s
                beyond = xlow if r == 0 else xhigh
                value = (source if r == 1 else beyond)[c, k] - flux[r, 0][c]
                put(w0, c, at, 0, value if edge_x is None else value * edge_x)
                if r == 1:
                    v0[c, k] = value
                if out <= 2:
                    halo = (ytile[c, k] if r == 1 else beyond[c, 3 + k]) - flux[r, 1][c]
                    put(w0, c, at, 1, halo * (mask_y if edge_x is None else mask_y * edge_x))
                    value = pull(side_low, side_high, s)
                    put(w0, c, at, 2, value * (mask_z if edge_x is None else mask_z * edge_x))
                if out <= 1:
                    value = pull(corner_low, corner_high, s)
                    put(w0, c, at, 3, value * (masks[3] if edge_x is None else masks[3] * edge_x))
    peak = floor = None
    flat = got.shape[0] * got.shape[1] * got.shape[2]
    for k in range(flat):
        tile = got[k // (got.shape[1] * got.shape[2]), k // got.shape[2] % got.shape[1], k % got.shape[2]]
        peak = tile if peak is None else jnp.maximum(peak, tile)
        floor = tile if floor is None else jnp.minimum(floor, tile)
    peak = jnp.max(peak, axis=0, keepdims=True)[:, 126:127]
    floor = jnp.min(floor, axis=0, keepdims=True)[:, 127:128]
    middle = 0.5 * peak + 0.5 * floor
    spread_of = 6.0 + (0.5 * peak - 0.5 * floor)
    slots = lax.broadcasted_iota(jnp.int32, (1, 128), 1)
    shrink = 1.0 / spread_of
    scale[...] = jnp.where(slots == 0, (6.0 + middle) * shrink, shrink)
    shrink = jnp.broadcast_to(shrink, (8, 128))
    middle = jnp.broadcast_to(middle, (8, 128))
    for key in diag:
        diag[key] = diag[key] - middle
    shrunk = [shrink if mask is None else mask * shrink for mask in masks]

    first_lane, last_lane = lane == 0, lane == 127
    acc = [jnp.zeros((8, 128), jnp.float32) for _ in range(6)]
    levels = (w0, w1, w2, None)
    results = (v0, v1, v2, v3)
    for level in (1, 2, 3):
        src, dst = levels[level - 1], levels[level]
        reach = 3 - level
        for c in range(3):
            for at in range(max(base - reach, 0), base + slabs + reach):
                out = max(base - at, at - base - slabs + 1, 0)
                r = 0 if at < base else (1 if at < base + slabs else 2)
                depth = reach - out
                want = (0,) if depth == 0 else ((0, 1, 2) if depth == 1 else (0, 1, 2, 3))
                edge_x = edges[r]
                for t in want:
                    here, across = take(src, c, at, t), take(src, c, at, t ^ 2)
                    zm = jnp.where(first_lane, across, pltpu.roll(here, 1, 1))
                    zp = jnp.where(last_lane, across, pltpu.roll(here, 127, 1))
                    beside = take(src, c, at + 1, t) + (zp + zm) + (take(src, c, at, t, 1) + take(src, c, at, t, 2))
                    if at > 0:
                        beside = beside + take(src, c, at - 1, t)
                    value = (diag[r, t] * here - beside) * shrunk[t]
                    if edge_x is not None:
                        value = value * edge_x
                    if dst is not None:
                        put(dst, c, at, t, value)
                    if t == 0 and r == 1:
                        results[level][c, at - base] = value
                        acc[2 * level - 1] = acc[2 * level - 1] + here * value
                        if level < 3:
                            acc[2 * level] = acc[2 * level] + value * value
                        if level == 1:
                            acc[0] = acc[0] + here * here
    line = jnp.zeros((1, 128), jnp.float32)
    slot = lax.broadcasted_iota(jnp.int32, (1, 128), 1)
    for k in range(6):
        sums = jnp.sum(jnp.sum(acc[k], axis=0, keepdims=True), axis=1, keepdims=True)
        line = jnp.where(slot == k, sums, line)
    moments[...] = jnp.broadcast_to(line[None], moments.shape)


def combine_kernel(pair, parts, scale, v0, v1, v2, v3, step_out, residual_out):
    total = jnp.sum(parts[...], axis=0)
    nu = [total[:, k : k + 1] for k in range(6)]

    def gram(a, b):
        result = None
        for i, ai in enumerate(a):
            for j, bj in enumerate(b):
                term = ai * bj * nu[i + j]
                result = term if result is None else result + term
        return result

    def added(a, b):
        size = max(len(a), len(b))
        return [a[k] if k >= len(b) else (b[k] if k >= len(a) else a[k] + b[k]) for k in range(size)]

    centre, shrink = scale[:, 0:1], scale[:, 1:2]
    unit = jnp.ones((1, 1), jnp.float32)
    direction, residual, newton = [unit], [unit], []
    norm = nu[0]
    for iteration in range(ITERS):
        image = added([centre * d for d in direction], [0.0 * unit] + direction)
        alpha = norm / gram(direction, image)
        newton = added(newton, [alpha * d for d in direction])
        residual = added(residual, [-alpha * g for g in image])
        if iteration + 1 < ITERS:
            following = gram(residual, residual)
            ratio = following / norm
            direction = added(residual, [ratio * d for d in direction])
            norm = following
    wide = lambda a: jnp.broadcast_to(a, (8, 128))
    newton = [wide(a * shrink) for a in newton]
    residual = [wide(a) for a in residual]
    for c in range(v0.shape[0]):
        for x in range(v0.shape[1]):
            a, b, d = v0[c, x], v1[c, x], v2[c, x]
            to = jnp.where(lax.axis_index("gx") == 0, x, v0.shape[1] - 1 - x) if pair else x
            step_out[c, to] = newton[0] * a + newton[1] * b + newton[2] * d
            residual_out[c, to] = residual[0] * a + residual[1] * b + residual[2] * d + residual[3] * v3[c, x]


def call(body, outs, ins, scratch=(), last=False, raw=False):
    vmem = pl.BlockSpec(memory_space=pltpu.VMEM)
    shape = jax.ShapeDtypeStruct if last else pltpu.VMEM
    return pl.pallas_call(
        body,
        out_shape=tuple(shape(s, d) for s, d in outs),
        in_specs=[pl.BlockSpec(memory_space=pltpu.HBM) if raw else vmem] * len(ins),
        out_specs=tuple(vmem for _ in outs),
        scratch_shapes=list(scratch),
        compiler_params=pltpu.CompilerParams(vmem_limit_bytes=GRANT),
    )(*(pltpu.with_memory_space_constraint(x, pltpu.HBM if raw else pltpu.VMEM) for x in ins))


def ladder(axis):
    count = lax.axis_size(axis)
    forward = [(i, i + 1) for i in range(count - 1)]
    return forward, [(b, a) for a, b in forward]


def pairs_from(first, count):
    couples = [(i, i + 1) for i in range(first, count - 1, 2)]
    return couples + [(b, a) for a, b in couples]


def from_both(low_face, high_face, axis):
    forward, backward = ladder(axis)
    up = lax.ppermute(high_face, axis, forward)
    down = lax.ppermute(low_face, axis, backward)
    return up, down


def whole_step(source, contrast, point_field, point_class, cell_kind, inverse_blocks):
    f32, bf16 = jnp.float32, jnp.bfloat16
    rows = contrast.shape[0]
    counts = tuple(lax.axis_size(a) for a in AXES)
    nx, ny, nz = counts
    devices = nx * ny * nz
    slabs = source.shape[1]
    dense = devices <= DENSE
    pair = nx == 2
    library = inverse_blocks.transpose(0, 2, 3, 1, 4)
    field = (source.shape, f32)
    if pair:
        swap = [(0, 1), (1, 0)]
        other = lax.ppermute(library, "gx", swap)
    else:
        other = lax.all_gather(library, "gx", axis=0, tiled=True)
    count = TYPES * nx
    hartley, spectrum, columns, pick, weights, source, library, send_a, send_b, faces = call(
        functools.partial(spectrum_kernel, pair, count),
        [((VOX, VOX), bf16), ((3 * rows, VOX), f32), ((rows, 8), f32), ((rows, 2 * count), bf16),
         (contrast.shape, f32), field, (library.shape, f32), ((3, slabs, 4, 128), f32), ((3, slabs, 4, 128), f32),
         ((2, 8, 128), f32)],
        (contrast, point_field, point_class.reshape(1, rows), cell_kind.reshape(1, rows), source, library),
        [pltpu.VMEM((3 * rows, VOX), bf16), pltpu.VMEM((3, rows), bf16), pltpu.VMEM((1, rows), jnp.int32),
         pltpu.VMEM((1, rows), jnp.int32), pltpu.VMEM(*field), pltpu.VMEM(contrast.shape, bf16), pltpu.SemaphoreType.DMA((6,))],
        raw=True,
    )
    couples = []
    for z in range(nz):
        mate = z ^ 1 if z ^ 1 < nz else z
        for i in range(ny):
            j = i + 1 if i % 2 else i - 1
            inside = 0 <= j < ny
            couples.append((i * nz + z, (j * nz + z) if inside else i * nz + mate))
    yb = lax.ppermute(send_b, ("gy", "gz"), couples)
    ya = lax.ppermute(send_a, "gy", pairs_from(0, ny))
    tiles, bundle = call(
        functools.partial(solve_kernel, slabs),
        [((4, 8, 128), f32), ((nx * ny if dense else 1, nz, 8, 128), f32)],
        (weights, columns, spectrum, hartley, pick, library if pair else other, other, faces),
        [pltpu.VMEM((9, rows, VOX), f32), pltpu.VMEM((3 * rows, VOX), bf16), pltpu.VMEM((3 * rows, VOX), f32)],
    )
    if dense:
        got = lax.all_to_all(bundle.reshape(devices, 8, 128), AXES, 0, 0).reshape(nx, ny, nz, 8, 128)
    else:
        below, above = from_both(bundle[0], bundle[0], "gx")
        trio = jnp.stack([below, bundle[0], above], axis=1)
        trio = jnp.broadcast_to(trio[None], (ny,) + trio.shape).reshape(ny * nz, 3, 8, 128)
        got = lax.all_to_all(trio, ("gy", "gz"), 0, 0).reshape(ny, nz, 3, 8, 128).transpose(2, 0, 1, 3, 4)
    if not dense:
        got = got.at[..., 126].set(lax.pmax(jnp.max(tiles[3]), AXES))
        got = got.at[..., 127].set(lax.pmin(jnp.min(tiles[3]), AXES))
    even = lax.axis_index("gy") % 2 == 0
    ytile = jnp.concatenate([jnp.where(even, ya, yb), jnp.where(even, yb, ya)], axis=2)
    high = jnp.concatenate([source[:, : slabs - 4 : -1], ytile[:, : slabs - 3 : -1]], axis=1)
    if pair:
        xlow = xhigh = lax.ppermute(high, "gx", swap)
    else:
        xlow, xhigh = from_both(jnp.concatenate([source[:, :3], ytile[:, :2]], axis=1), high, "gx")
    v0, v1, v2, v3, moments, scale = call(
        functools.partial(moment_kernel, dense, counts),
        [field, field, field, field, ((devices if dense else 1, 1, 128), f32), ((1, 128), f32)],
        (tiles, got, source, ytile, xlow, xhigh),
        [pltpu.VMEM((3, slabs + (3 if pair else 6), 2, 24, 128), f32) for _ in range(3)],
    )
    if dense:
        parts = lax.all_to_all(moments, AXES, 0, 0)
    else:
        parts = lax.psum(moments, AXES)
    return call(functools.partial(combine_kernel, pair), [field, field], (parts, scale, v0, v1, v2, v3), last=True)


def solution(mesh):
    placed = (
        P(None, "gx", "gy", "gz"),
        P(("gx", "gy", "gz"), None),
        P(None, ("gx", "gy", "gz")),
        P(("gx", "gy", "gz"), None),
        P(("gx", "gy", "gz")),
        P("gx", None, None, None, None),
    )
    return jax.shard_map(
        whole_step,
        mesh=mesh,
        in_specs=placed,
        out_specs=(P(None, "gx", "gy", "gz"), P(None, "gx", "gy", "gz")),
        check_vma=False,
    )
```
